128 devices in a mesh: seq: 16 (over x, y), section: 8 (over z, core).
Axes of the slice: x: 4, y: 4, z: 4, core: 2. Of those that a mesh axis runs over, the one named last changes fastest.
Arguments:
- queries: bfloat16 [2048, 4096], P('seq', 'section'), may hold values from -10 to 10
- keys: bfloat16 [2048, 1024], P('seq', 'section'), may hold values from -10 to 10
- values: bfloat16 [2048, 1024], P('seq', 'section'), may hold values from -18 to 18
- residual: bfloat16 [2048, 8192], P(None, 'seq'), may hold values from -8 to 8
- out_weight: bfloat16 [4096, 8192], P('section', 'seq'), may hold values from -0.09375 to 0.09375
- norm_gain: float32 [8192], P('seq'), may hold values from 0.1 to 1.9
- in_weight: bfloat16 [8192, 2, 16, 512], P('seq', None, None, 'section'), may hold values from -0.09375 to 0.09375
- conv_weight: float32 [8192, 4], P(('seq', 'section')), may hold values from -3 to 3
- conv_bias: float32 [8192], P(('seq', 'section')), may hold values from -0.5 to 0.5
- proj_weight: bfloat16 [8192, 272], P(('seq', 'section')), may hold values from -0.0625 to 0.0625
- dt_weight: bfloat16 [256, 8192], P(None, ('seq', 'section')), may hold values from -0.375 to 0.375
- dt_bias: float32 [8192], P(('seq', 'section')), may hold values from -3 to 0
- a_log: float32 [8192, 8], P(('seq', 'section')), may hold values from -7 to 0
- skip_gain: float32 [8192], P(('seq', 'section')), may hold values from -2.5 to 2.5
Outputs:
- mixer_out: bfloat16 [8192, 2048], P(('seq', 'section'))
The draws below stay inside these ranges and needn't reach their ends.
All inputs are finite; a program needn't handle non-finite values.
Results may differ from the reference program's by a relative error of at most 0.03.
Values may be sent and summed in bfloat16 or wider, within the bound.
A program may use at most 128 MiB of HBM per device.

```python
import math
import jax
import jax.numpy as jnp
from jax import lax

D = 8192
HD = 128
GROUP = 4
KVH = 8
HQ = 32
NST = 8
DT_RANK = 256
CONV = 4
E = 8192
L = 2048
N_SEQ = 16


def drawn_pair(key):
    query_key = jax.random.fold_in(key, 101)
    key_key = jax.random.fold_in(key, 202)
    query_base = jnp.clip(jax.random.normal(query_key, (L, KVH, GROUP, HD), jnp.float32), -6.0, 6.0)
    key_base = jnp.clip(jax.random.normal(key_key, (L, KVH, HD), jnp.float32), -6.0, 6.0)
    return (query_base.reshape(L, KVH * GROUP * HD), key_base.reshape(L, KVH * HD))


def draw_queries(key, part):
    return drawn_pair(key)[0].astype(jnp.bfloat16)


def draw_keys(key, part):
    return drawn_pair(key)[1].astype(jnp.bfloat16)


def draw_residual(key, part):
    column_scale = 10.0 ** (jnp.arange(D, dtype=jnp.float32) / D)
    base = jnp.clip(jax.random.normal(jax.random.fold_in(key, 1), (L, D), jnp.float32), -4.0, 4.0)
    row_scale = 10.0 ** jax.random.uniform(jax.random.fold_in(key, 3), (L,), jnp.float32, 0.0, 1.0)
    return (0.01 * base * row_scale[:, None] * column_scale[None, :]).astype(jnp.bfloat16)


def with_spikes(values, rng, source, target, parts, factor):
    def block_of(dim):
        return (jnp.arange(values.shape[dim]) // (values.shape[dim] // parts)).reshape((-1,) + (1,) * (values.ndim - 1 - dim))

    first = jax.random.permutation(rng, parts)[block_of(target)]
    other_side = (block_of(target) + parts // 2) % parts
    return jnp.where((block_of(source) == first) | (block_of(source) == other_side), factor * values, values)


def level_of(key, shape, split, low, high):
    loudness = 1.0
    for axis_at, blocks in split:
        steps = jax.random.uniform(jax.random.fold_in(jax.random.fold_in(key, 6), axis_at), (blocks,), jnp.float32, low / len(split), high / len(split))
        loudness = loudness * jnp.repeat(jnp.exp(steps), shape[axis_at] // blocks).reshape((-1,) + (1,) * (len(shape) - 1 - axis_at))
    return loudness


def bell_draw(own_key, shape, deviation, limit, split=(), kind=jnp.bfloat16):
    factor_of = level_of(own_key, shape, split, -0.22, 0.18) if split else 1.0
    drawn = jax.random.normal(own_key, shape, jnp.float32) * deviation * factor_of
    return jnp.minimum(jnp.maximum(drawn, -limit), limit).astype(kind)


def bell_draw_with(stream_key, dims, scale, limit, cuts, heavy, kind=jnp.bfloat16):
    values = scale * jax.random.normal(stream_key, dims, jnp.float32)
    if cuts:
        values = values * level_of(stream_key, dims, cuts, -0.22, 0.18)
    return jnp.clip(with_spikes(values, jax.random.fold_in(stream_key, 3), *heavy), -limit, limit).astype(kind)


def setup_inputs(seed: int = 0) -> dict:
    key_of = jax.random.split(jax.random.key(seed), 15)
    queries = draw_queries(jax.random.fold_in(key_of[14], 71), 0)
    keys = draw_keys(jax.random.fold_in(key_of[14], 71), 0)
    values = bell_draw(key_of[2], (L, KVH * HD), 3.0, 18.0, ((0, 16), (1, 8)))
    residual = draw_residual(jax.random.fold_in(key_of[14], 71), 0)
    out_weight = bell_draw(key_of[4], (HQ * HD, D), (HQ * HD) ** -0.5, 0.09375, ((0, 8), (1, 16)))
    norm_gain = jnp.clip(1.0 + 0.18 * jax.random.normal(key_of[5], (D,), jnp.float32), 0.1, 1.9)
    in_weight = bell_draw_with(key_of[6], (D, 2, N_SEQ, E // N_SEQ), D ** -0.5, 0.09375, ((0, 16), (3, 8)), (0, 2, 16, 2.0))
    conv_weight = bell_draw(key_of[7], (E, CONV), 0.5, 3.0, ((0, 128),), jnp.float32)
    conv_bias = jnp.clip(jax.random.uniform(key_of[8], (E,), jnp.float32, -0.5, 0.5) * level_of(key_of[8], (E,), ((0, 128),), -0.4, 0.0), -0.5, 0.5)
    proj_weight = bell_draw(key_of[9], (E, DT_RANK + 2 * NST), E ** -0.5, 0.0625, ((0, 128),))
    dt_weight = bell_draw(key_of[10], (DT_RANK, E), DT_RANK ** -0.5, 0.375, ((1, 128),))
    dt_bias = jnp.clip(-3.0 + 3.0 * jax.random.uniform(key_of[11], (E,), jnp.float32) ** level_of(key_of[11], (E,), ((0, 128),), -0.2, 0.2), -3.0, 0.0)
    a_log = jnp.clip(-7.0 + 7.0 * jax.random.uniform(key_of[12], (E, NST), jnp.float32) ** level_of(key_of[12], (E, NST), ((0, 128),), -0.2, 0.2), -7.0, 0.0)
    skip_gain = jnp.clip(jax.random.uniform(key_of[13], (E,), jnp.float32, -2.5, 2.5) * level_of(key_of[13], (E,), ((0, 128),), -0.4, 0.0), -2.5, 2.5)
    return dict(queries=queries, keys=keys, values=values, residual=residual, out_weight=out_weight, norm_gain=norm_gain, in_weight=in_weight, conv_weight=conv_weight, conv_bias=conv_bias, proj_weight=proj_weight, dt_weight=dt_weight, dt_bias=dt_bias, a_log=a_log, skip_gain=skip_gain)


def attend_group(operands):
    query_group, key_rows, value_rows = operands
    scores = jnp.einsum('pgd,rd->gpr', query_group.astype(jnp.float32), key_rows.astype(jnp.float32)) / math.sqrt(HD)
    position = jnp.arange(L)
    allowed = (position[:, None] >= position[None, :])[None]
    scores = jnp.where(allowed, scores, -jnp.inf)
    row_max = lax.optimization_barrier(jnp.max(scores, axis=2, keepdims=True))
    exponent_terms = jnp.where(allowed, jnp.exp(scores - row_max), jnp.float32(0.0))
    weight_sum = lax.optimization_barrier(jnp.sum(exponent_terms, axis=2))
    weights_bf = exponent_terms.astype(jnp.bfloat16)
    summed = jnp.einsum('gpr,rd->pgd', weights_bf.astype(jnp.float32), value_rows.astype(jnp.float32))
    return (summed / jnp.transpose(weight_sum)[:, :, None]).astype(jnp.bfloat16)

def reference(queries, keys, values, residual, out_weight, norm_gain, in_weight, conv_weight, conv_bias, proj_weight, dt_weight, dt_bias, a_log, skip_gain):
    query_groups = jnp.transpose(queries.reshape(L, KVH, GROUP, HD), (1, 0, 2, 3))
    key_groups = jnp.transpose(keys.reshape(L, KVH, HD), (1, 0, 2))
    value_groups = jnp.transpose(values.reshape(L, KVH, HD), (1, 0, 2))
    attended = lax.map(attend_group, (query_groups, key_groups, value_groups))
    attended = jnp.transpose(attended, (1, 0, 2, 3)).reshape(L, HQ * HD)
    hidden = residual.astype(jnp.float32) + jnp.dot(attended, out_weight, preferred_element_type=jnp.float32)
    inv_rms = lax.rsqrt(lax.optimization_barrier(jnp.sum(hidden * hidden, axis=1)) / D + 1e-05)
    normed = (hidden * inv_rms[:, None] * norm_gain[None, :]).astype(jnp.bfloat16)
    weight_flat = in_weight.reshape(D, 2, E)
    width = D // N_SEQ

    def add_block(block_index, running):
        begin = (block_index * width).astype(jnp.int32)
        rows = lax.dynamic_slice_in_dim(normed, begin, width, 1)
        block_weight = lax.dynamic_slice_in_dim(weight_flat, begin, width, 0)
        partial_sum = jnp.einsum('ld,dke->kel', rows.astype(jnp.float32), block_weight.astype(jnp.float32))
        rounded = lax.optimization_barrier(partial_sum.astype(jnp.bfloat16))
        return running + rounded.astype(jnp.float32)
    mixed_in = lax.fori_loop(jnp.int32(0), jnp.int32(N_SEQ), add_block, jnp.zeros((2, E, L), jnp.float32))
    x_path = mixed_in[0]
    z_gate = mixed_in[1]
    padded = jnp.pad(x_path, ((0, 0), (CONV - 1, 0)))
    conv_out = conv_bias[:, None] + jnp.zeros((E, L), jnp.float32)
    for offset in range(CONV):
        conv_out = conv_out + conv_weight[:, offset:offset + 1] * padded[:, offset:offset + L]
    inputs = jax.nn.silu(conv_out).astype(jnp.bfloat16)
    projected = jnp.dot(jnp.transpose(proj_weight), inputs, preferred_element_type=jnp.float32)
    low_rank = projected[:DT_RANK].astype(jnp.bfloat16)
    in_map = projected[DT_RANK:DT_RANK + NST]
    out_map = projected[DT_RANK + NST:]
    step_size = jax.nn.softplus(jnp.dot(jnp.transpose(dt_weight), low_rank, preferred_element_type=jnp.float32) + dt_bias[:, None])
    decay = -jnp.exp(a_log)
    inputs_float = inputs.astype(jnp.float32)

    def advance(carried, column):
        step_col, input_col, in_col, out_col = column
        carried = jnp.exp(step_col[:, None] * decay) * carried + (step_col * input_col)[:, None] * in_col[None, :]
        return (carried, lax.optimization_barrier(jnp.sum(carried * out_col[None, :], axis=1)))
    columns = (jnp.transpose(step_size), jnp.transpose(inputs_float), jnp.transpose(in_map), jnp.transpose(out_map))
    final_state, outputs = lax.scan(advance, jnp.zeros((E, NST), jnp.float32), columns)
    readout = jnp.transpose(outputs)
    return ((readout + skip_gain[:, None] * inputs_float) * jax.nn.silu(z_gate)).astype(jnp.bfloat16)
```

```python
import math

import jax
import jax.numpy as jnp
from jax import lax
from jax.experimental import pallas as pl
from jax.experimental.pallas import tpu as pltpu
from jax.sharding import PartitionSpec as P

D = 8192
HD = 128
GROUP = 4
NST = 8
DT_RANK = 256
CONV = 4
NORM_EPS = 1e-05
MESH = pl.DeviceIdType.MESH
BF = jnp.bfloat16
F32 = jnp.float32
ROWS = 272
SPLIT = 144
LOG2E = math.log2(math.e)
NT = (((1,), (1,)), ((), ()))
TN = (((0,), (0,)), ((), ()))


def nt_dot(a, b, **kw):
    return lax.dot_general(a, b, NT, preferred_element_type=F32, **kw)


def mm(a, b):
    return jnp.dot(a, b, preferred_element_type=F32)


class Comm:
    def __init__(self, send_sem, recv_sem):
        self.send_sem = send_sem
        self.recv_sem = recv_sem
        self.copies = []

    def send(self, src, dst, dev):
        at = len(self.copies)
        copy = pltpu.make_async_remote_copy(
            src_ref=src,
            dst_ref=dst,
            send_sem=self.send_sem.at[at],
            recv_sem=self.recv_sem.at[at],
            device_id=dev,
            device_id_type=MESH,
        )
        copy.start()
        self.copies.append(copy)
        return copy

    def finish(self):
        for copy in self.copies:
            copy.wait_send()


def run(*streams):
    live = list(streams)
    while live:
        for stream in list(live):
            try:
                next(stream)
            except StopIteration:
                live.remove(stream)


def gather_plane(comm, place, size, first, second):
    half = size // 2
    one = comm.send(place(0, 0, 0, size), place(0, 0, 0, size), first[0])
    two = comm.send(place(0, 0, 0, size), place(0, 0, 0, size), first[1])

    def along(df):
        block = place(df, 0, 0, size)
        return comm.send(block, block, second[0]), comm.send(block, block, second[1])

    sent = [(0, along(0))]
    yield
    one.wait_recv()
    block = place(-1, 0, 0, half)
    three = comm.send(block, block, first[0])
    two.wait_recv()
    block = place(1, 0, half, size - half)
    four = comm.send(block, block, first[1])
    sent.append((-1, along(-1)))
    sent.append((1, along(1)))
    yield
    three.wait_recv()
    four.wait_recv()
    sent.append((2, along(2)))
    yield
    last = []
    for df, (up, down) in sent:
        up.wait_recv()
        block = place(df, -1, 0, half)
        last.append(comm.send(block, block, second[0]))
        down.wait_recv()
        block = place(df, 1, half, size - half)
        last.append(comm.send(block, block, second[1]))
    yield
    for copy in last:
        copy.wait_recv()


def ring_gather(comm, place, size, cut, ends, also=None):
    whole = place(0, 0, size)
    up = comm.send(whole, whole, ends[0])
    down = comm.send(whole, whole, ends[1])
    if also:
        also(0)
    yield
    up.wait_recv()
    block = place(-1, 0, cut)
    far_up = comm.send(block, block, ends[0])
    if also:
        also(-1)
    down.wait_recv()
    block = place(1, cut, size - cut)
    far_down = comm.send(block, block, ends[1])
    if also:
        also(1)
    yield
    far_up.wait_recv()
    far_down.wait_recv()
    if also:
        also(2)


def front_kernel(
    q_ref, k_ref, v_ref, res_ref, ow_ref, gain_ref, w_ref, cw_ref, cb_ref, pw_ref,
    uz_ref, g_ref,
    kv, att, cs, cr, zs, zn, zf, act, hid, ssq_out, ssq_in, res, wv,
    s1, r1, s2, r2, own, t1, u1, t2, u2, mixed,
    gs, gr, gz, gzn, gzf, gx, gfull,
    send_sem, recv_sem, local_sem,
):
    s = lax.axis_index("seq")
    c = lax.axis_index("section")
    x, y = s // 4, s % 4
    z, k = c // 2, c % 2
    o = 1 - k

    def seq_of(cx, cy):
        return {"seq": cx * 4 + cy}

    def section_of(cz, ck):
        return {"section": cz * 2 + ck}

    xe = (seq_of((x + 1) % 4, y), seq_of((x + 3) % 4, y))
    ye = (seq_of(x, (y + 1) % 4), seq_of(x, (y + 3) % 4))
    ze = (section_of((z + 1) % 4, k), section_of((z + 3) % 4, k))
    sib = section_of(z, o)

    res_copy = pltpu.make_async_copy(
        res_ref.at[pl.ds(1024 * k + 256 * z, 256)], res, local_sem.at[0]
    )
    res_copy.start()
    w_copy = pltpu.make_async_copy(w_ref, wv, local_sem.at[1])
    w_copy.start()

    barrier = pltpu.get_barrier_semaphore()
    for off in range(1, 16):
        pl.semaphore_signal(
            barrier, inc=1, device_id={"seq": (s + off) % 16}, device_id_type=MESH
        )
    for dev in (*ze, sib):
        pl.semaphore_signal(barrier, inc=1, device_id=dev, device_id_type=MESH)
    kv[x, y, :, 0:HD] = k_ref[...]
    kv[x, y, :, HD:] = v_ref[...]
    pl.semaphore_wait(barrier, 18)

    comm = Comm(send_sem, recv_sem)

    def plane_place(buf, x_first, base, by_rows=True):
        def place(df, ds, start, count):
            if x_first:
                cx, cy = (x + df) % 4, (y + ds) % 4
            else:
                cx, cy = (x + ds) % 4, (y + df) % 4
            return buf.at[cx, cy, pl.ds(base + start, count)]

        return place

    run(
        gather_plane(comm, plane_place(kv, True, 0), 64, xe, ye),
        gather_plane(comm, plane_place(kv, False, 64), 64, ye, xe),
    )

    query_pos = s * 128 + lax.broadcasted_iota(jnp.int32, (128, 2048), 0)
    key_pos = lax.broadcasted_iota(jnp.int32, (128, 2048), 1)
    allowed = query_pos >= key_pos
    key_rows = kv[:, :, :, 0:HD].reshape(2048, HD)
    value_rows = kv[:, :, :, HD:].reshape(2048, HD)
    for g in range(GROUP):
        scores = nt_dot(q_ref[:, g * HD : (g + 1) * HD], key_rows)
        scores = jnp.where(allowed, scores, -1e30)
        top = jnp.max(scores, axis=1, keepdims=True)
        terms = jnp.exp2((scores - top) * (LOG2E / math.sqrt(HD)))
        total = jnp.sum(terms, axis=1, keepdims=True)
        moved = mm(terms.astype(BF), value_rows)
        att[x, y, :, g * HD : (g + 1) * HD] = (moved / total).astype(BF)

    run(
        gather_plane(comm, plane_place(att, True, 0), 64, xe, ye),
        gather_plane(comm, plane_place(att, False, 64), 64, ye, xe),
    )

    def branch(kk, zt):
        rows = att[2 * kk + zt // 2, pl.ds((zt % 2) * 2, 2)].reshape(256, 512)
        return mm(rows, ow_ref[...])

    offsets = (2, 1, 3, 0)
    crossing = []
    for off in offsets:
        zt = (z + off) % 4
        cs[zt] = branch(o, zt).astype(BF)
        crossing.append(comm.send(cs.at[zt], cr.at[zt], sib))
    w_copy.wait()
    res_copy.wait()
    near = []
    for at, off in enumerate(offsets):
        zt = (z + off) % 4
        part = branch(k, zt)
        crossing[at].wait_recv()
        part = part + cr[zt].astype(F32)
        if off == 2:
            zs[0] = part.astype(BF)
            far = (
                comm.send(zs.at[0, 0:128], zf.at[0], ze[0]),
                comm.send(zs.at[0, 128:256], zf.at[1], ze[1]),
            )
        elif off == 1:
            far[0].wait_recv()
            zs[1, 0:128] = (part[0:128] + zf[0].astype(F32)).astype(BF)
            zs[1, 128:256] = part[128:256].astype(BF)
            near.append(comm.send(zs.at[1], zn.at[0], ze[0]))
        elif off == 3:
            far[1].wait_recv()
            zs[2, 0:128] = part[0:128].astype(BF)
            zs[2, 128:256] = (part[128:256] + zf[1].astype(F32)).astype(BF)
            near.append(comm.send(zs.at[2], zn.at[1], ze[1]))
        else:
            part = part + res[...].astype(F32)
            near[0].wait_recv()
            part = part + zn[0].astype(F32)
            near[1].wait_recv()
            hid[...] = part + zn[1].astype(F32)

    hidden = hid[...]
    ssq_out[...] = nt_dot(jnp.ones((8, 512), F32), hidden * hidden, precision=lax.Precision.HIGHEST)
    ssq_in[s] = ssq_out[...]
    squares = [
        comm.send(ssq_out, ssq_in.at[s], {"seq": (s + off) % 16}) for off in range(1, 16)
    ]
    for copy in squares:
        copy.wait_recv()
    total = ssq_in[0]
    for at in range(1, 16):
        total = total + ssq_in[at]
    inv = jnp.transpose(lax.rsqrt(total / D + NORM_EPS))[:, 0:1]
    act[k, z] = (hidden * inv * gain_ref[...]).astype(BF)

    across = []

    def act_place(d, start, count):
        return act.at[k, (z + d) % 4, pl.ds(start, count)]

    def act_also(d):
        block = act.at[k, (z + d) % 4]
        across.append(comm.send(block, block, sib))

    run(ring_gather(comm, act_place, 256, 128, ze, act_also))
    for copy in across:
        copy.wait_recv()

    def rs_half(h, main, main_ends, side, side_ends):
        def weights(p):
            rows = []
            for j in range(4):
                b = (j * 4 + p) if h == 0 else (p * 4 + j)
                rows += [wv[0, b], wv[1, b]]
            return jnp.concatenate(rows, axis=0)

        def product(p, put):
            wide = weights(p)
            for r in range(4):
                acc = nt_dot(act[h, r], wide)
                for j in range(4):
                    put(j, r * 256, acc[:, j * 128 : (j + 1) * 128])

        def into(buf, at):
            def put(j, row, value):
                buf[h, at, j, row : row + 256] = value.astype(BF)

            return put

        product((main + 2) % 4, into(s1, 0))
        far = []
        for j in range(4):
            far.append(comm.send(s1.at[h, 0, j], r1.at[h, j], main_ends[j // 2]))
        yield
        product((main + 1) % 4, into(s2, 0))
        near = {}
        for j in (2, 3):
            near[0, j] = comm.send(s2.at[h, 0, j], r2.at[h, 0, j], main_ends[0])
        product((main + 3) % 4, into(s2, 1))
        for j in (0, 1):
            near[1, j] = comm.send(s2.at[h, 1, j], r2.at[h, 1, j], main_ends[1])
        yield

        def put_own(j, row, value):
            own[h, j, row : row + 256] = value

        product(main, put_own)
        yield
        for a, b in ((0, 2), (1, 3)):
            far[a].wait_recv()
            s2[h, 0, a] = (s2[h, 0, a].astype(F32) + r1[h, a].astype(F32)).astype(BF)
            near[0, a] = comm.send(s2.at[h, 0, a], r2.at[h, 0, a], main_ends[0])
            far[b].wait_recv()
            s2[h, 1, b] = (s2[h, 1, b].astype(F32) + r1[h, b].astype(F32)).astype(BF)
            near[1, b] = comm.send(s2.at[h, 1, b], r2.at[h, 1, b], main_ends[1])
        yield
        for key in ((0, 2), (0, 3), (1, 0), (1, 1), (0, 0), (1, 2), (0, 1), (1, 3)):
            near[key].wait_recv()
        yield

        def summed(j):
            return own[h, j] + r2[h, 0, j].astype(F32) + r2[h, 1, j].astype(F32)

        t1[h] = summed((side + 2) % 4).astype(BF)
        last_far = (
            comm.send(t1.at[h, 0:512], u1.at[h, 0], side_ends[0]),
            comm.send(t1.at[h, 512:1024], u1.at[h, 1], side_ends[1]),
        )
        yield
        part_up = summed((side + 1) % 4)
        part_down = summed((side + 3) % 4)
        t2[h, 0, 512:1024] = part_up[512:1024].astype(BF)
        t2[h, 1, 0:512] = part_down[0:512].astype(BF)
        early = (
            comm.send(t2.at[h, 0, 512:1024], u2.at[h, 0, 512:1024], side_ends[0]),
            comm.send(t2.at[h, 1, 0:512], u2.at[h, 1, 0:512], side_ends[1]),
        )
        last_far[0].wait_recv()
        t2[h, 0, 0:512] = (part_up[0:512] + u1[h, 0].astype(F32)).astype(BF)
        last = [comm.send(t2.at[h, 0, 0:512], u2.at[h, 0, 0:512], side_ends[0])]
        last_far[1].wait_recv()
        t2[h, 1, 512:1024] = (part_down[512:1024] + u1[h, 1].astype(F32)).astype(BF)
        last.append(comm.send(t2.at[h, 1, 512:1024], u2.at[h, 1, 512:1024], side_ends[1]))
        yield
        part = summed(side)
        for copy in (*early, *last):
            copy.wait_recv()
        mixed[h * 1024 : (h + 1) * 1024] = (
            part + u2[h, 0].astype(F32) + u2[h, 1].astype(F32)
        )

    run(rs_half(0, y, ye, x, xe), rs_half(1, x, xe, y, ye))

    lane = lax.broadcasted_iota(jnp.int32, (16, 128), 1)
    row = lax.broadcasted_iota(jnp.int32, (16, 128), 0)
    is_path = lane < 64
    taps = [cw_ref[i : i + 1] for i in range(CONV)]
    bias = cb_ref[...]

    def strided(j):
        return mixed[pl.ds(j, 16, stride=128), :]

    def before(j):
        return jnp.where(row == 0, 0.0, pltpu.roll(strided(j), 1, 0))

    def conv_step(j, carried):
        older, old, recent = carried
        now = strided(j)
        total = bias + taps[0] * older + taps[1] * old + taps[2] * recent + taps[3] * now
        value = jnp.where(is_path, total, now)
        uz_ref[pl.ds(pl.multiple_of(j * 16, 16), 16), :] = value / (1.0 + jnp.exp(-value))
        return (old, recent, now)

    lax.fori_loop(0, 128, conv_step, (before(125), before(126), before(127)), unroll=4)

    zeros = jnp.zeros((64, 256), BF)
    rank_weight = jnp.concatenate([pw_ref[:, 0:256], zeros], axis=0)
    map_weight = jnp.transpose(pw_ref[:, 256:272].astype(F32))
    map_weight = jnp.concatenate([map_weight, jnp.zeros((16, 64), F32)], axis=1).astype(BF)

    def local_block(tb):
        u = uz_ref[pl.ds(pl.multiple_of(tb * 256, 256), 256), :].astype(BF)
        gs[tb, 0:256] = mm(u, rank_weight).astype(BF)
        gs[tb, 256:272] = nt_dot(map_weight, u).astype(BF)

    crossing = []
    for off in offsets:
        zt = (z + off) % 4
        local_block(4 * o + zt)
        crossing.append(comm.send(gs.at[4 * o + zt], gr.at[zt], sib))
    near = []
    for at, off in enumerate(offsets):
        zt = (z + off) % 4
        local_block(4 * k + zt)
        crossing[at].wait_recv()
        part = gs[4 * k + zt].astype(F32) + gr[zt].astype(F32)
        if off == 2:
            gz[0, 0] = part[:, 0:128].astype(BF)
            gz[0, 1] = part[:, 128:256].astype(BF)
            far = (
                comm.send(gz.at[0, 0], gzf.at[0], ze[0]),
                comm.send(gz.at[0, 1], gzf.at[1], ze[1]),
            )
        elif off == 1:
            far[0].wait_recv()
            gz[1, 0] = (part[:, 0:128] + gzf[0].astype(F32)).astype(BF)
            gz[1, 1] = part[:, 128:256].astype(BF)
            near.append(comm.send(gz.at[1], gzn.at[0], ze[0]))
        elif off == 3:
            far[1].wait_recv()
            gz[2, 0] = part[:, 0:128].astype(BF)
            gz[2, 1] = (part[:, 128:256] + gzf[1].astype(F32)).astype(BF)
            near.append(comm.send(gz.at[2], gzn.at[1], ze[1]))
        else:
            near[0].wait_recv()
            near[1].wait_recv()
            left, right = gzn[0].astype(F32), gzn[1].astype(F32)
            gx[0, 0, x] = (part[:, 0:128] + left[0] + right[0]).astype(BF)
            gx[1, 0, y] = (part[:, 128:256] + left[1] + right[1]).astype(BF)

    def sum_half(h, axes):
        for step, (mine, ends) in enumerate(axes):

            def place(d, start, count):
                return gx.at[h, step, (mine + d) % 4, pl.ds(start, count)]

            yield from ring_gather(comm, place, ROWS, SPLIT, ends)
            total = gx[h, step, 0].astype(F32)
            for at in range(1, 4):
                total = total + gx[h, step, at].astype(F32)
            if step == 0:
                gx[h, 1, axes[1][0]] = total.astype(BF)
            else:
                gfull[4 * k + z, :, h * 128 : (h + 1) * 128] = total.astype(BF)
            yield

    run(sum_half(0, ((x, xe), (y, ye))), sum_half(1, ((y, ye), (x, xe))))

    across = []

    def g_place(d, start, count):
        return gfull.at[4 * k + (z + d) % 4, pl.ds(start, count)]

    def g_also(d):
        block = gfull.at[4 * k + (z + d) % 4]
        across.append(comm.send(block, block, sib))

    run(ring_gather(comm, g_place, ROWS, SPLIT, ze, g_also))
    for copy in across:
        copy.wait_recv()
    g_ref[...] = gfull[...]
    comm.finish()


def front(queries, keys, values, residual, out_weight, gain, weights, cw, cb, pw):
    vmem = pl.BlockSpec(memory_space=pltpu.VMEM)
    anyspace = pl.BlockSpec(memory_space=pl.ANY)
    copies = 320
    return pl.pallas_call(
        front_kernel,
        out_shape=(
            jax.ShapeDtypeStruct((2048, 128), F32),
            jax.ShapeDtypeStruct((8, ROWS, 256), BF),
        ),
        in_specs=[vmem, vmem, vmem, anyspace, vmem, vmem, anyspace, vmem, vmem, vmem],
        out_specs=(vmem, vmem),
        scratch_shapes=[
            pltpu.VMEM((4, 4, 128, 256), BF),
            pltpu.VMEM((4, 4, 128, 512), BF),
            pltpu.VMEM((4, 256, 512), BF),
            pltpu.VMEM((4, 256, 512), BF),
            pltpu.VMEM((3, 256, 512), BF),
            pltpu.VMEM((2, 256, 512), BF),
            pltpu.VMEM((2, 128, 512), BF),
            pltpu.VMEM((2, 4, 256, 512), BF),
            pltpu.VMEM((256, 512), F32),
            pltpu.VMEM((8, 256), F32),
            pltpu.VMEM((16, 8, 256), F32),
            pltpu.VMEM((256, 512), BF),
            pltpu.VMEM((2, 16, 64, 512), BF),
            pltpu.VMEM((2, 1, 4, 1024, 128), BF),
            pltpu.VMEM((2, 4, 1024, 128), BF),
            pltpu.VMEM((2, 2, 4, 1024, 128), BF),
            pltpu.VMEM((2, 2, 4, 1024, 128), BF),
            pltpu.VMEM((2, 4, 1024, 128), F32),
            pltpu.VMEM((2, 1024, 128), BF),
            pltpu.VMEM((2, 2, 512, 128), BF),
            pltpu.VMEM((2, 2, 1024, 128), BF),
            pltpu.VMEM((2, 2, 1024, 128), BF),
            pltpu.VMEM((2048, 128), F32),
            pltpu.VMEM((8, ROWS, 256), BF),
            pltpu.VMEM((4, ROWS, 256), BF),
            pltpu.VMEM((3, 2, ROWS, 128), BF),
            pltpu.VMEM((2, 2, ROWS, 128), BF),
            pltpu.VMEM((2, ROWS, 128), BF),
            pltpu.VMEM((2, 2, 4, ROWS, 128), BF),
            pltpu.VMEM((8, ROWS, 256), BF),
            pltpu.SemaphoreType.DMA((copies,)),
            pltpu.SemaphoreType.DMA((copies,)),
            pltpu.SemaphoreType.DMA((2,)),
        ],
        compiler_params=pltpu.CompilerParams(
            collective_id=0, has_side_effects=True, vmem_limit_bytes=60 * 1024 * 1024
        ),
        name="front",
    )(queries, keys, values, residual, out_weight, gain, weights, cw, cb, pw)


def tail_kernel(uz_ref, g_ref, dtw_ref, dtb_ref, al_ref, skip_ref, out_ref, step, wide, drive, ys):
    lane8 = lax.broadcasted_iota(jnp.int32, (16, 1024), 1)
    row8 = lax.broadcasted_iota(jnp.int32, (16, 1024), 0)
    state = 2 * ((lane8 // 128) % 4) + (lane8 % 128) // 64 + 8 * (lane8 // 512)
    spread = jnp.where(row8 == state, 1.0, 0.0).astype(BF)
    dtw = jnp.concatenate([dtw_ref[...], dtw_ref[...]], axis=0)
    dtb = dtb_ref[...]
    lane = lax.broadcasted_iota(jnp.int32, (256, 128), 1)
    low = lane < 64
    for tb in range(8):
        rows = pl.ds(tb * 256, 256)
        pre = nt_dot(g_ref[tb, 0:256], dtw) + dtb
        st = jnp.maximum(pre, 0.0) + jnp.log1p(jnp.exp(-jnp.abs(pre)))
        step[rows] = st
        u = uz_ref[rows].astype(BF).astype(F32)
        u = jnp.where(low, u, pltpu.roll(u, 64, 1))
        drive[rows] = st * u
        wide[rows] = lax.dot_general(
            g_ref[tb, 256:272], spread, TN, preferred_element_type=F32
        )
    low_row = lax.broadcasted_iota(jnp.int32, (1, 128), 1) < 64
    decay = []
    for q in range(4):
        both = jnp.where(low_row, al_ref[2 * q : 2 * q + 1], al_ref[2 * q + 1 : 2 * q + 2])
        decay.append(-jnp.exp(both) * LOG2E)
    row = lax.broadcasted_iota(jnp.int32, (16, 128), 0)
    nothing = jnp.zeros((16, 128), F32)

    def advance(j, states):
        at = pl.ds(pl.multiple_of(j * 16, 16), 16)
        st = step[at]
        du = drive[at]
        return st, tuple(
            jnp.exp2(st * decay[q]) * states[q] + du * wide[at, q * 128 : (q + 1) * 128]
            for q in range(4)
        )

    def first_pass(j, carried):
        total, states = carried
        st, states = advance(j, states)
        return (total + st, states)

    total, ends = lax.fori_loop(0, 128, first_pass, (nothing, (nothing,) * 4), unroll=4)

    entry = []
    for q in range(4):
        factor = jnp.exp2(total * decay[q])
        value = ends[q]
        for d in (1, 2, 4, 8):
            moved_factor = jnp.where(row < d, 1.0, pltpu.roll(factor, d, 0))
            moved_value = jnp.where(row < d, 0.0, pltpu.roll(value, d, 0))
            value = factor * moved_value + value
            factor = factor * moved_factor
        entry.append(jnp.where(row < 1, 0.0, pltpu.roll(value, 1, 0)))

    skip = skip_ref[...]

    def second_pass(j, states):
        _, states = advance(j, states)
        at = pl.ds(pl.multiple_of(j * 16, 16), 16)
        uz = uz_ref[at]
        read = states[0] * wide[at, 512:640]
        for q in range(1, 4):
            read = read + states[q] * wide[at, 512 + q * 128 : 640 + q * 128]
        read = read + pltpu.roll(read, 64, 1)
        u = uz.astype(BF).astype(F32)
        ys[pl.ds(j, 16, stride=128), :] = (read + skip * u) * pltpu.roll(uz, 64, 1)
        return states

    lax.fori_loop(0, 128, second_pass, tuple(entry), unroll=4)
    for seg in range(16):
        block = jnp.transpose(ys[seg * 128 : (seg + 1) * 128, :])
        out_ref[:, seg * 128 : (seg + 1) * 128] = block[0:64].astype(BF)


def tail(uz, g, dtw, dtb, al, skip):
    vmem = pl.BlockSpec(memory_space=pltpu.VMEM)
    return pl.pallas_call(
        tail_kernel,
        out_shape=jax.ShapeDtypeStruct((64, 2048), BF),
        in_specs=[vmem] * 6,
        out_specs=vmem,
        scratch_shapes=[
            pltpu.VMEM((2048, 128), F32),
            pltpu.VMEM((2048, 1024), F32),
            pltpu.VMEM((2048, 128), F32),
            pltpu.VMEM((2048, 128), F32),
        ],
        compiler_params=pltpu.CompilerParams(vmem_limit_bytes=40 * 1024 * 1024),
        name="tail",
    )(uz, g, dtw, dtb, al, skip)


def twice(row):
    return jnp.concatenate([row, row], axis=-1)


def body(
    queries, keys, values, residual, out_weight, norm_gain, in_weight, conv_weight, conv_bias,
    proj_weight, dt_weight, dt_bias, a_log, skip_gain,
):
    uz, g = front(
        queries, keys, values, residual, out_weight, norm_gain[None, :],
        jnp.transpose(in_weight, (1, 2, 3, 0)),
        twice(conv_weight.T), twice(conv_bias[None, :]), proj_weight,
    )
    return tail(
        uz, g, dt_weight.T, twice(dt_bias[None, :]), twice(a_log.T), twice(skip_gain[None, :])
    )


def solution(mesh):
    return jax.shard_map(
        body,
        mesh=mesh,
        in_specs=(
            P("seq", "section"),
            P("seq", "section"),
            P("seq", "section"),
            P(None, "seq"),
            P("section", "seq"),
            P("seq"),
            P("seq", None, None, "section"),
            P(("seq", "section"), None),
            P(("seq", "section")),
            P(("seq", "section"), None),
            P(None, ("seq", "section")),
            P(("seq", "section")),
            P(("seq", "section"), None),
            P(("seq", "section")),
        ),
        out_specs=P(("seq", "section"), None),
        check_vma=False,
    )
```

```python
import math

import jax
import jax.numpy as jnp
from jax import lax
from jax.experimental import pallas as pl
from jax.experimental.pallas import tpu as pltpu
from jax.sharding import PartitionSpec as P

D = 8192
HD = 128
GROUP = 4
NST = 8
DT_RANK = 256
CONV = 4
NORM_EPS = 1e-05
MESH = pl.DeviceIdType.MESH
BF = jnp.bfloat16
F32 = jnp.float32
ROWS = 144
SPLIT = 80
ORDER = (0, -1, 1, 2)
LOG2E = math.log2(math.e)
NT = (((1,), (1,)), ((), ()))
TN = (((0,), (0,)), ((), ()))


def nt_dot(a, b, **kw):
    return lax.dot_general(a, b, NT, preferred_element_type=F32, **kw)


def mm(a, b):
    return jnp.dot(a, b, preferred_element_type=F32)


class Comm:
    def __init__(self, send_sem, recv_sem):
        self.send_sem = send_sem
        self.recv_sem = recv_sem
        self.copies = []

    def send(self, src, dst, dev):
        at = len(self.copies)
        copy = pltpu.make_async_remote_copy(
            src_ref=src,
            dst_ref=dst,
            send_sem=self.send_sem.at[at],
            recv_sem=self.recv_sem.at[at],
            device_id=dev,
            device_id_type=MESH,
        )
        copy.start()
        self.copies.append(copy)
        return copy

    def finish(self):
        for copy in self.copies:
            copy.wait_send()


def run(*streams):
    live = list(streams)
    while live:
        for stream in list(live):
            try:
                next(stream)
            except StopIteration:
                live.remove(stream)


def gather_plane(comm, place, size, first, second):
    half = size // 2
    one = comm.send(place(0, 0, 0, size), place(0, 0, 0, size), first[0])
    two = comm.send(place(0, 0, 0, size), place(0, 0, 0, size), first[1])

    def along(df):
        block = place(df, 0, 0, size)
        return comm.send(block, block, second[0]), comm.send(block, block, second[1])

    sent = [(0, along(0))]
    yield
    one.wait_recv()
    block = place(-1, 0, 0, half)
    three = comm.send(block, block, first[0])
    two.wait_recv()
    block = place(1, 0, half, size - half)
    four = comm.send(block, block, first[1])
    sent.append((-1, along(-1)))
    sent.append((1, along(1)))
    yield
    three.wait_recv()
    four.wait_recv()
    sent.append((2, along(2)))
    yield
    last = []
    for df, (up, down) in sent:
        up.wait_recv()
        block = place(df, -1, 0, half)
        last.append(comm.send(block, block, second[0]))
        down.wait_recv()
        block = place(df, 1, half, size - half)
        last.append(comm.send(block, block, second[1]))
    yield
    for copy in last:
        copy.wait_recv()


def ring_gather(comm, place, size, cut, ends, also=None):
    whole = place(0, 0, size)
    up = comm.send(whole, whole, ends[0])
    down = comm.send(whole, whole, ends[1])
    if also:
        also(0)
    yield
    up.wait_recv()
    block = place(-1, 0, cut)
    far_up = comm.send(block, block, ends[0])
    if also:
        also(-1)
    down.wait_recv()
    block = place(1, cut, size - cut)
    far_down = comm.send(block, block, ends[1])
    if also:
        also(1)
    yield
    far_up.wait_recv()
    far_down.wait_recv()
    if also:
        also(2)


def front_kernel(
    q_ref, k_ref, v_ref, res_ref, ow_ref, gain_ref, w_ref, cw_ref, cb_ref, pw_ref,
    dtw_ref, dtb_ref, al_ref, skip_ref,
    out_ref,
    kv, att, cs, cr, zs, zn, zf, act, hid, ssq_out, ssq_in, inv, res, wv,
    s1, r1, s2, r2, own, t1, u1, t2, u2, mixed, uz,
    gs, gr, gz, gzn, gzf, gx, gfull,
    step_size, wide, drive, ys,
    send_sem, recv_sem, local_sem,
):
    s = lax.axis_index("seq")
    c = lax.axis_index("section")
    x, y = s // 4, s % 4
    z, k = c // 2, c % 2
    o = 1 - k

    def seq_of(cx, cy):
        return {"seq": cx * 4 + cy}

    def section_of(cz, ck):
        return {"section": cz * 2 + ck}

    xe = (seq_of((x + 1) % 4, y), seq_of((x + 3) % 4, y))
    ye = (seq_of(x, (y + 1) % 4), seq_of(x, (y + 3) % 4))
    ze = (section_of((z + 1) % 4, k), section_of((z + 3) % 4, k))
    sib = section_of(z, o)

    res_copy = pltpu.make_async_copy(
        res_ref.at[pl.ds(1024 * k + 256 * z, 256)], res, local_sem.at[0]
    )
    res_copy.start()
    w_copy = pltpu.make_async_copy(w_ref, wv, local_sem.at[1])
    w_copy.start()

    barrier = pltpu.get_barrier_semaphore()
    for off in range(1, 16):
        pl.semaphore_signal(
            barrier, inc=1, device_id={"seq": (s + off) % 16}, device_id_type=MESH
        )
    for off in range(1, 8):
        pl.semaphore_signal(
            barrier, inc=1, device_id={"section": (c + off) % 8}, device_id_type=MESH
        )
    kv[x, y, :, 0:HD] = k_ref[...]
    kv[x, y, :, HD:] = v_ref[...]
    pl.semaphore_wait(barrier, 22)

    comm = Comm(send_sem, recv_sem)

    def plane_place(buf, x_first, base, by_rows=True):
        def place(df, ds, start, count):
            if x_first:
                cx, cy = (x + df) % 4, (y + ds) % 4
            else:
                cx, cy = (x + ds) % 4, (y + df) % 4
            return buf.at[cx, cy, pl.ds(base + start, count)]

        return place

    run(
        gather_plane(comm, plane_place(kv, True, 0), 64, xe, ye),
        gather_plane(comm, plane_place(kv, False, 64), 64, ye, xe),
    )

    query_pos = s * 128 + lax.broadcasted_iota(jnp.int32, (128, 2048), 0)
    key_pos = lax.broadcasted_iota(jnp.int32, (128, 2048), 1)
    allowed = query_pos >= key_pos
    key_rows = kv[:, :, :, 0:HD].reshape(2048, HD)
    value_rows = kv[:, :, :, HD:].reshape(2048, HD)
    for g in range(GROUP):
        scores = nt_dot(q_ref[:, g * HD : (g + 1) * HD], key_rows)
        scores = jnp.where(allowed, scores, -1e30)
        top = jnp.max(scores, axis=1, keepdims=True)
        terms = jnp.exp2((scores - top) * (LOG2E / math.sqrt(HD)))
        total = jnp.sum(terms, axis=1, keepdims=True)
        moved = mm(terms.astype(BF), value_rows)
        att[x, y, :, g * HD : (g + 1) * HD] = (moved / total).astype(BF)

    run(
        gather_plane(comm, plane_place(att, True, 0), 64, xe, ye),
        gather_plane(comm, plane_place(att, False, 64), 64, ye, xe),
    )

    def branch(kk, zt):
        rows = att[2 * kk + zt // 2, pl.ds((zt % 2) * 2, 2)].reshape(256, 512)
        return mm(rows, ow_ref[...])

    offsets = (2, 1, 3, 0)
    crossing = []
    for off in offsets:
        zt = (z + off) % 4
        cs[zt] = branch(o, zt).astype(BF)
        crossing.append(comm.send(cs.at[zt], cr.at[zt], sib))
    w_copy.wait()
    res_copy.wait()
    near = []
    for at, off in enumerate(offsets):
        zt = (z + off) % 4
        part = branch(k, zt)
        crossing[at].wait_recv()
        part = part + cr[zt].astype(F32)
        if off == 2:
            zs[0] = part.astype(BF)
            far = (
                comm.send(zs.at[0, 0:128], zf.at[0], ze[0]),
                comm.send(zs.at[0, 128:256], zf.at[1], ze[1]),
            )
        elif off == 1:
            far[0].wait_recv()
            zs[1, 0:128] = (part[0:128] + zf[0].astype(F32)).astype(BF)
            zs[1, 128:256] = part[128:256].astype(BF)
            near.append(comm.send(zs.at[1], zn.at[0], ze[0]))
        elif off == 3:
            far[1].wait_recv()
            zs[2, 0:128] = part[0:128].astype(BF)
            zs[2, 128:256] = (part[128:256] + zf[1].astype(F32)).astype(BF)
            near.append(comm.send(zs.at[2], zn.at[1], ze[1]))
        else:
            part = part + res[...].astype(F32)
            near[0].wait_recv()
            part = part + zn[0].astype(F32)
            near[1].wait_recv()
            hid[...] = part + zn[1].astype(F32)

    hidden = hid[...]
    act[k, z] = (hidden * gain_ref[...]).astype(BF)
    across = []

    def act_place(d, start, count):
        return act.at[k, (z + d) % 4, pl.ds(start, count)]

    def act_also(d):
        block = act.at[k, (z + d) % 4]
        across.append(comm.send(block, block, sib))

    def gather_act():
        yield from ring_gather(comm, act_place, 256, 128, ze, act_also)

    act_steps = gather_act()
    next(act_steps)
    ssq_out[...] = nt_dot(jnp.ones((8, 512), F32), hidden * hidden, precision=lax.Precision.HIGHEST)
    ssq_in[s] = ssq_out[...]
    squares = [
        comm.send(ssq_out, ssq_in.at[s], {"seq": (s + off) % 16}) for off in range(1, 16)
    ]
    inverses = []

    def share_inverse():
        for copy in squares:
            copy.wait_recv()
        total = ssq_in[0]
        for at in range(1, 16):
            total = total + ssq_in[at]
        inv[k, z] = lax.rsqrt(total / D + NORM_EPS)
        for dz in range(4):
            for flip in range(2):
                if dz or flip:
                    to = section_of((z + dz) % 4, (k + flip) % 2)
                    inverses.append(comm.send(inv.at[k, z], inv.at[k, z], to))

    def unit(u):
        ch = u // 4
        zt = (z + ORDER[u % 4]) % 4
        by_y = u % 2 == 0
        main, main_ends, side, side_ends = (y, ye, x, xe) if by_y else (x, xe, y, ye)

        def product(p):
            rows = []
            for j in range(4):
                b = (j * 4 + p) if by_y else (p * 4 + j)
                rows += [wv[0, b], wv[1, b]]
            return nt_dot(act[ch, zt], jnp.concatenate(rows, axis=0))

        acc = product((main + 2) % 4)
        for j in range(4):
            s1[u, j] = acc[:, j * 128 : (j + 1) * 128].astype(BF)
        far = [
            comm.send(s1.at[u, 2 * e : 2 * e + 2], r1.at[u, 2 * e : 2 * e + 2], main_ends[e])
            for e in range(2)
        ]
        yield
        early, late = [], []
        for e, step in ((0, 1), (1, 3)):
            acc = product((main + step) % 4)
            for j in range(4):
                s2[u, e, j] = acc[:, j * 128 : (j + 1) * 128].astype(BF)
            span = pl.ds(2 - 2 * e, 2)
            early.append(comm.send(s2.at[u, e, span], r2.at[u, e, span], main_ends[e]))
        yield
        acc = product(main)
        for j in range(4):
            own[u, j] = acc[:, j * 128 : (j + 1) * 128]
        yield
        for e in range(2):
            far[e].wait_recv()
            span = pl.ds(2 * e, 2)
            s2[u, e, span] = (s2[u, e, span].astype(F32) + r1[u, span].astype(F32)).astype(BF)
            late.append(comm.send(s2.at[u, e, span], r2.at[u, e, span], main_ends[e]))
        yield
        for copy in (*early, *late):
            copy.wait_recv()

        def summed(j):
            return own[u, j] + r2[u, 0, j].astype(F32) + r2[u, 1, j].astype(F32)

        def summed_rows(j, rest):
            return (
                own[u, j, rest] + r2[u, 0, j, rest].astype(F32) + r2[u, 1, j, rest].astype(F32)
            )

        t1[u] = summed((side + 2) % 4).astype(BF)
        last_far = [
            comm.send(t1.at[u, 128 * e : 128 * e + 128], u1.at[u, e], side_ends[e])
            for e in range(2)
        ]
        parts = summed((side + 1) % 4), summed((side + 3) % 4)
        last = []
        for e in range(2):
            rest = slice(128 - 128 * e, 256 - 128 * e)
            t2[u, e, rest] = parts[e][rest].astype(BF)
            last.append(comm.send(t2.at[u, e, rest], u2.at[u, e, rest], side_ends[e]))
        yield
        for e in range(2):
            last_far[e].wait_recv()
            rest = slice(128 * e, 128 * e + 128)
            j = (side + 1 + 2 * e) % 4
            part = summed_rows(j, rest) + u1[u, e].astype(F32)
            t2[u, e, rest] = part.astype(BF)
            last.append(comm.send(t2.at[u, e, rest], u2.at[u, e, rest], side_ends[e]))
        yield
        for copy in last:
            copy.wait_recv()
        part = summed(side) + u2[u, 0].astype(F32) + u2[u, 1].astype(F32)
        scale = jnp.transpose(inv[ch, zt])[:, 0:1]
        mixed[pl.ds(pl.multiple_of(ch * 1024 + zt * 256, 256), 256)] = part * scale
        yield

    lane = lax.broadcasted_iota(jnp.int32, (8, 128), 1)
    row = lax.broadcasted_iota(jnp.int32, (8, 128), 0)
    is_path = lane < 64
    low_row = lax.broadcasted_iota(jnp.int32, (1, 128), 1) < 64

    def twice(value):
        return jnp.concatenate([value, value], axis=1)

    taps = twice(cw_ref[...])
    bias = twice(cb_ref[...])

    def conv(ch):
        def strided(j):
            return mixed[pl.ds(ch * 1024 + j, 8, stride=128), :]

        def before(j):
            if ch:
                return mixed[pl.ds(ch * 1024 - 128 + j, 8, stride=128), :]
            return jnp.where(row == 0, 0.0, pltpu.roll(strided(j), 1, 0))

        def step(j, carried):
            older, old, recent = carried
            now = strided(j)
            total = (
                bias + taps[0:1] * older + taps[1:2] * old + taps[2:3] * recent + taps[3:4] * now
            )
            value = jnp.where(is_path, total, now)
            at = pl.ds(pl.multiple_of(ch * 1024 + j * 8, 8), 8)
            uz[at, :] = value / (1.0 + jnp.exp(-value))
            return (old, recent, now)

        lax.fori_loop(0, 128, step, (before(125), before(126), before(127)), unroll=8)

    def sum_maps(ch):
        rank_weight = jnp.concatenate([pw_ref[:, 0:256], jnp.zeros((64, 256), BF)], axis=0)
        map_weight = jnp.transpose(pw_ref[:, 256:272].astype(F32))
        map_weight = jnp.concatenate([map_weight, jnp.zeros((16, 64), F32)], axis=1).astype(BF)

        def local_block(i):
            at = pl.ds(pl.multiple_of(ch * 1024 + i * 128, 128), 128)
            u = uz[at, :].astype(BF)
            gs[ch, i, 0:128] = mm(u, rank_weight).astype(BF)
            maps = nt_dot(map_weight, u).astype(BF)
            gs[ch, i, 128:ROWS] = jnp.concatenate([maps, jnp.zeros((16, 128), BF)], axis=1)

        offs = (2, 1, 3, 0)
        crossing = []
        for off in offs:
            zt = (z + off) % 4
            local_block(4 * o + zt)
            crossing.append(comm.send(gs.at[ch, 4 * o + zt], gr.at[ch, zt], sib))
        yield
        for off in offs:
            local_block(4 * k + (z + off) % 4)
        near = []
        for at, off in enumerate(offs):
            zt = (z + off) % 4
            crossing[at].wait_recv()
            part = gs[ch, 4 * k + zt].astype(F32) + gr[ch, zt].astype(F32)
            left, right = part[:, 0:128], part[:, 128:256]
            if off == 2:
                gz[ch, 0, 0] = left.astype(BF)
                gz[ch, 0, 1] = right.astype(BF)
                far = [comm.send(gz.at[ch, 0, e], gzf.at[ch, e], ze[e]) for e in range(2)]
                yield
            elif off == 1:
                far[0].wait_recv()
                gz[ch, 1, 0] = (left + gzf[ch, 0].astype(F32)).astype(BF)
                gz[ch, 1, 1] = right.astype(BF)
                near.append(comm.send(gz.at[ch, 1], gzn.at[ch, 0], ze[0]))
            elif off == 3:
                far[1].wait_recv()
                gz[ch, 2, 0] = left.astype(BF)
                gz[ch, 2, 1] = (right + gzf[ch, 1].astype(F32)).astype(BF)
                near.append(comm.send(gz.at[ch, 2], gzn.at[ch, 1], ze[1]))
                yield
            else:
                near[0].wait_recv()
                near[1].wait_recv()
                down, up = gzn[ch, 0].astype(F32), gzn[ch, 1].astype(F32)
                gx[ch, 0, 0, x] = (left + down[0] + up[0]).astype(BF)
                gx[ch, 1, 0, y] = (right + down[1] + up[1]).astype(BF)

        def sum_half(h, axes):
            for step, (mine, ends) in enumerate(axes):

                def place(d, start, count):
                    return gx.at[ch, h, step, (mine + d) % 4, pl.ds(start, count)]

                yield from ring_gather(comm, place, ROWS, SPLIT, ends)
                total = gx[ch, h, step, 0].astype(F32)
                for at in range(1, 4):
                    total = total + gx[ch, h, step, at].astype(F32)
                if step == 0:
                    gx[ch, h, 1, axes[1][0]] = total.astype(BF)
                else:
                    gfull[ch, 4 * k + z, :, h * 128 : (h + 1) * 128] = total.astype(BF)

        halves = sum_half(0, ((x, xe), (y, ye))), sum_half(1, ((y, ye), (x, xe)))
        live = True
        while live:
            live = False
            for half in halves:
                try:
                    next(half)
                    live = True
                except StopIteration:
                    pass
            if live:
                yield

        across_maps = []

        def place(d, start, count):
            return gfull.at[ch, 4 * k + (z + d) % 4, pl.ds(start, count)]

        def also(d):
            block = gfull.at[ch, 4 * k + (z + d) % 4]
            across_maps.append(comm.send(block, block, sib))

        yield from ring_gather(comm, place, ROWS, SPLIT, ze, also)
        for copy in across_maps:
            copy.wait_recv()

    lane8 = lax.broadcasted_iota(jnp.int32, (16, 1024), 1)
    row8 = lax.broadcasted_iota(jnp.int32, (16, 1024), 0)
    which = 2 * ((lane8 // 128) % 4) + (lane8 % 128) // 64 + 8 * (lane8 // 512)
    spread = jnp.where(row8 == which, 1.0, 0.0).astype(BF)

    def decays():
        al = twice(al_ref[...])
        return [
            -jnp.exp(jnp.where(low_row, al[2 * q : 2 * q + 1], al[2 * q + 1 : 2 * q + 2])) * LOG2E
            for q in range(4)
        ]

    def prepare(ch):
        dtw = jnp.concatenate([dtw_ref[...], dtw_ref[...]], axis=0)
        dtb = twice(dtb_ref[...])
        low = lax.broadcasted_iota(jnp.int32, (128, 128), 1) < 64
        for i in range(8):
            rows = pl.ds(i * 128, 128)
            pre = nt_dot(gfull[ch, i, 0:128], dtw) + dtb
            st = jnp.maximum(pre, 0.0) + jnp.log1p(jnp.exp(-jnp.abs(pre)))
            step_size[rows] = st
            u = uz[pl.ds(ch * 1024 + i * 128, 128)].astype(BF).astype(F32)
            drive[rows] = st * jnp.where(low, u, pltpu.roll(u, 64, 1))
            wide[rows] = lax.dot_general(
                gfull[ch, i, 128:ROWS, 0:128], spread, TN, preferred_element_type=F32
            )

    nothing = jnp.zeros((8, 128), F32)

    def advance(j, states, decay):
        at = pl.ds(pl.multiple_of(j * 8, 8), 8)
        st = step_size[at]
        du = drive[at]
        return st, tuple(
            jnp.exp2(st * decay[q]) * states[q] + du * wide[at, q * 128 : (q + 1) * 128]
            for q in range(4)
        )

    def segment_ends():
        decay = decays()

        def first_pass(j, carried):
            total, states = carried
            st, states = advance(j, states, decay)
            return (total + st, states)

        return lax.fori_loop(0, 128, first_pass, (nothing, (nothing,) * 4), unroll=8)

    def entries(found, carry):
        total, ends = found
        decay = decays()
        starts, after = [], []
        for q in range(4):
            factor = jnp.exp2(total * decay[q])
            value = ends[q]
            for d in (1, 2, 4):
                moved_factor = jnp.where(row < d, 1.0, pltpu.roll(factor, d, 0))
                moved_value = jnp.where(row < d, 0.0, pltpu.roll(value, d, 0))
                value = factor * moved_value + value
                factor = factor * moved_factor
            if carry is not None:
                value = value + factor * carry[q]
            start = pltpu.roll(value, 1, 0)
            starts.append(jnp.where(row < 1, 0.0 if carry is None else carry[q], start))
            after.append(jnp.broadcast_to(value[7:8], (8, 128)))
        return starts, after

    def finish(ch, starts):
        decay = decays()
        skip = twice(skip_ref[...])

        def second_pass(j, states):
            _, states = advance(j, states, decay)
            at = pl.ds(pl.multiple_of(j * 8, 8), 8)
            gated = uz[pl.ds(pl.multiple_of(ch * 1024 + j * 8, 8), 8)]
            read = states[0] * wide[at, 512:640]
            for q in range(1, 4):
                read = read + states[q] * wide[at, 512 + q * 128 : 640 + q * 128]
            read = read + pltpu.roll(read, 64, 1)
            u = gated.astype(BF).astype(F32)
            ys[pl.ds(j, 8, stride=128), :] = (read + skip * u) * pltpu.roll(gated, 64, 1)
            return states

        lax.fori_loop(0, 128, second_pass, tuple(starts), unroll=8)
        for seg in range(8):
            block = jnp.transpose(ys[seg * 128 : (seg + 1) * 128, :])
            column = ch * 1024 + seg * 128
            out_ref[:, column : column + 128] = block[0:64].astype(BF)

    pairs = {}

    def go(pair, steps):
        if pair not in pairs:
            pairs[pair] = (unit(2 * pair), unit(2 * pair + 1))
        for _ in range(steps):
            for stream in pairs[pair]:
                next(stream)

    def advance_all(stream, steps=1):
        for _ in range(steps):
            next(stream, None)

    run(act_steps)
    for copy in across:
        copy.wait_recv()

    go(0, 3)
    share_inverse()
    go(0, 1)
    go(1, 3)
    go(0, 1)
    go(1, 1)
    go(0, 1)
    go(2, 3)
    for copy in inverses:
        copy.wait_recv()
    go(0, 1)
    go(1, 1)
    go(2, 1)
    go(1, 1)
    go(3, 3)
    go(1, 1)
    conv(0)
    maps0 = sum_maps(0)
    advance_all(maps0)
    go(2, 1)
    advance_all(maps0)
    go(3, 1)
    advance_all(maps0)
    go(2, 1)
    advance_all(maps0)
    go(3, 1)
    advance_all(maps0)
    go(2, 1)
    advance_all(maps0)
    go(3, 1)
    advance_all(maps0)
    go(3, 1)

    conv(1)
    maps1 = sum_maps(1)
    advance_all(maps1)
    advance_all(maps0)
    advance_all(maps1)
    for _ in maps0:
        pass
    prepare(0)
    advance_all(maps1)
    found = segment_ends()
    advance_all(maps1)
    starts, carry = entries(found, None)
    finish(0, starts)
    for _ in maps1:
        pass

    prepare(1)
    starts, carry = entries(segment_ends(), carry)
    finish(1, starts)
    comm.finish()


def body(
    queries, keys, values, residual, out_weight, norm_gain, in_weight, conv_weight, conv_bias,
    proj_weight, dt_weight, dt_bias, a_log, skip_gain,
):
    vmem = pl.BlockSpec(memory_space=pltpu.VMEM)
    anyspace = pl.BlockSpec(memory_space=pl.ANY)
    copies = 400
    return pl.pallas_call(
        front_kernel,
        out_shape=jax.ShapeDtypeStruct((64, 2048), BF),
        in_specs=[vmem, vmem, vmem, anyspace, vmem, vmem, anyspace] + [vmem] * 7,
        out_specs=vmem,
        scratch_shapes=[
            pltpu.VMEM((4, 4, 128, 256), BF),
            pltpu.VMEM((4, 4, 128, 512), BF),
            pltpu.VMEM((4, 256, 512), BF),
            pltpu.VMEM((4, 256, 512), BF),
            pltpu.VMEM((3, 256, 512), BF),
            pltpu.VMEM((2, 256, 512), BF),
            pltpu.VMEM((2, 128, 512), BF),
            pltpu.VMEM((2, 4, 256, 512), BF),
            pltpu.VMEM((256, 512), F32),
            pltpu.VMEM((8, 256), F32),
            pltpu.VMEM((16, 8, 256), F32),
            pltpu.VMEM((2, 4, 8, 256), F32),
            pltpu.VMEM((256, 512), BF),
            pltpu.VMEM((2, 16, 64, 512), BF),
            pltpu.VMEM((8, 4, 256, 128), BF),
            pltpu.VMEM((8, 4, 256, 128), BF),
            pltpu.VMEM((8, 2, 4, 256, 128), BF),
            pltpu.VMEM((8, 2, 4, 256, 128), BF),
            pltpu.VMEM((8, 4, 256, 128), F32),
            pltpu.VMEM((8, 256, 128), BF),
            pltpu.VMEM((8, 2, 128, 128), BF),
            pltpu.VMEM((8, 2, 256, 128), BF),
            pltpu.VMEM((8, 2, 256, 128), BF),
            pltpu.VMEM((2048, 128), F32),
            pltpu.VMEM((2048, 128), F32),
            pltpu.VMEM((2, 8, ROWS, 256), BF),
            pltpu.VMEM((2, 4, ROWS, 256), BF),
            pltpu.VMEM((2, 3, 2, ROWS, 128), BF),
            pltpu.VMEM((2, 2, 2, ROWS, 128), BF),
            pltpu.VMEM((2, 2, ROWS, 128), BF),
            pltpu.VMEM((2, 2, 2, 4, ROWS, 128), BF),
            pltpu.VMEM((2, 8, ROWS, 256), BF),
            pltpu.VMEM((1024, 128), F32),
            pltpu.VMEM((1024, 1024), F32),
            pltpu.VMEM((1024, 128), F32),
            pltpu.VMEM((1024, 128), F32),
            pltpu.SemaphoreType.DMA((copies,)),
            pltpu.SemaphoreType.DMA((copies,)),
            pltpu.SemaphoreType.DMA((2,)),
        ],
        compiler_params=pltpu.CompilerParams(
            collective_id=0, has_side_effects=True, vmem_limit_bytes=60 * 1024 * 1024
        ),
        name="front",
    )(
        queries, keys, values, residual, out_weight, norm_gain[None, :],
        jnp.transpose(in_weight, (1, 2, 3, 0)), conv_weight.T, conv_bias[None, :], proj_weight,
        dt_weight.T, dt_bias[None, :], a_log.T, skip_gain[None, :],
    )


def solution(mesh):
    return jax.shard_map(
        body,
        mesh=mesh,
        in_specs=(
            P("seq", "section"),
            P("seq", "section"),
            P("seq", "section"),
            P(None, "seq"),
            P("section", "seq"),
            P("seq"),
            P("seq", None, None, "section"),
            P(("seq", "section"), None),
            P(("seq", "section")),
            P(("seq", "section"), None),
            P(None, ("seq", "section")),
            P(("seq", "section")),
            P(("seq", "section"), None),
            P(("seq", "section")),
        ),
        out_specs=P(("seq", "section"), None),
        check_vma=False,
    )
```

```python
import math

import jax
import jax.numpy as jnp
from jax import lax
from jax.experimental import pallas as pl
from jax.experimental.pallas import tpu as pltpu
from jax.sharding import PartitionSpec as P

D = 8192
HD = 128
GROUP = 4
NST = 8
DT_RANK = 256
CONV = 4
NORM_EPS = 1e-05
MESH = pl.DeviceIdType.MESH
BF = jnp.bfloat16
F32 = jnp.float32
CHUNKS = ((0, 1024), (1024, 512), (1536, 512))
ORDER = (0, -1, 1, 2)
LOG2E = math.log2(math.e)
NT = (((1,), (1,)), ((), ()))
TN = (((0,), (0,)), ((), ()))


def nt_dot(a, b, **kw):
    return lax.dot_general(a, b, NT, preferred_element_type=F32, **kw)


def mm(a, b):
    return jnp.dot(a, b, preferred_element_type=F32)


class Comm:
    def __init__(self, send_sem, recv_sem):
        self.send_sem = send_sem
        self.recv_sem = recv_sem
        self.copies = []

    def send(self, src, dst, dev):
        at = len(self.copies)
        copy = pltpu.make_async_remote_copy(
            src_ref=src,
            dst_ref=dst,
            send_sem=self.send_sem.at[at],
            recv_sem=self.recv_sem.at[at],
            device_id=dev,
            device_id_type=MESH,
        )
        copy.start()
        self.copies.append(copy)
        return copy

    def finish(self):
        for copy in self.copies:
            copy.wait_send()


def run(*streams):
    live = list(streams)
    while live:
        for stream in list(live):
            try:
                next(stream)
            except StopIteration:
                live.remove(stream)


def gather_plane(comm, place, size, first, second):
    half = size // 2
    one = comm.send(place(0, 0, 0, size), place(0, 0, 0, size), first[0])
    two = comm.send(place(0, 0, 0, size), place(0, 0, 0, size), first[1])

    def along(df):
        block = place(df, 0, 0, size)
        return comm.send(block, block, second[0]), comm.send(block, block, second[1])

    sent = [(0, along(0))]
    yield
    one.wait_recv()
    block = place(-1, 0, 0, half)
    three = comm.send(block, block, first[0])
    two.wait_recv()
    block = place(1, 0, half, size - half)
    four = comm.send(block, block, first[1])
    sent.append((-1, along(-1)))
    sent.append((1, along(1)))
    yield
    three.wait_recv()
    four.wait_recv()
    sent.append((2, along(2)))
    yield
    last = []
    for df, (up, down) in sent:
        up.wait_recv()
        block = place(df, -1, 0, half)
        last.append(comm.send(block, block, second[0]))
        down.wait_recv()
        block = place(df, 1, half, size - half)
        last.append(comm.send(block, block, second[1]))
    yield
    for copy in last:
        copy.wait_recv()


def front_kernel(
    q_ref, k_ref, v_ref, res_ref, ow_ref, gain_ref, w_ref, cw_ref, cb_ref, pw_ref,
    dtw_ref, dtb_ref, al_ref, skip_ref,
    out_ref,
    kv, att, cs, cr, zs, zn, zf, act, hid, ssq_out, ssq_in, inv, res, wv,
    s1, r1, s2, r2, own, t1, u1, t2, u2, mixed, uz,
    gs, gd, gx, gfull,
    step_size, wide, drive, ys,
    send_sem, recv_sem, local_sem,
):
    s = lax.axis_index("seq")
    c = lax.axis_index("section")
    x, y = s // 4, s % 4
    z, k = c // 2, c % 2
    o = 1 - k

    def seq_of(cx, cy):
        return {"seq": cx * 4 + cy}

    def section_of(cz, ck):
        return {"section": cz * 2 + ck}

    xe = (seq_of((x + 1) % 4, y), seq_of((x + 3) % 4, y))
    ye = (seq_of(x, (y + 1) % 4), seq_of(x, (y + 3) % 4))
    ze = (section_of((z + 1) % 4, k), section_of((z + 3) % 4, k))
    sib = section_of(z, o)

    res_copy = pltpu.make_async_copy(
        res_ref.at[pl.ds(1024 * k + 256 * z, 256)], res, local_sem.at[0]
    )
    res_copy.start()
    w_copy = pltpu.make_async_copy(w_ref, wv, local_sem.at[1])
    w_copy.start()

    barrier = pltpu.get_barrier_semaphore()
    for off in range(1, 16):
        pl.semaphore_signal(
            barrier, inc=1, device_id={"seq": (s + off) % 16}, device_id_type=MESH
        )
    for off in range(1, 8):
        pl.semaphore_signal(
            barrier, inc=1, device_id={"section": (c + off) % 8}, device_id_type=MESH
        )
    kv[x, y, :, 0:HD] = k_ref[...]
    kv[x, y, :, HD:] = v_ref[...]
    pl.semaphore_wait(barrier, 22)

    comm = Comm(send_sem, recv_sem)

    def plane_place(buf, x_first, base, by_rows=True):
        def place(df, ds, start, count):
            if x_first:
                cx, cy = (x + df) % 4, (y + ds) % 4
            else:
                cx, cy = (x + ds) % 4, (y + df) % 4
            return buf.at[cx, cy, pl.ds(base + start, count)]

        return place

    run(
        gather_plane(comm, plane_place(kv, True, 0), 64, xe, ye),
        gather_plane(comm, plane_place(kv, False, 64), 64, ye, xe),
    )

    query_pos = s * 128 + lax.broadcasted_iota(jnp.int32, (128, 2048), 0)
    key_pos = lax.broadcasted_iota(jnp.int32, (128, 2048), 1)
    allowed = query_pos >= key_pos
    key_rows = kv[:, :, :, 0:HD].reshape(2048, HD)
    value_rows = kv[:, :, :, HD:].reshape(2048, HD)
    for g in range(GROUP):
        scores = nt_dot(q_ref[:, g * HD : (g + 1) * HD], key_rows)
        scores = jnp.where(allowed, scores, -1e30)
        top = jnp.max(scores, axis=1, keepdims=True)
        terms = jnp.exp2((scores - top) * (LOG2E / math.sqrt(HD)))
        total = jnp.sum(terms, axis=1, keepdims=True)
        moved = mm(terms.astype(BF), value_rows)
        att[x, y, :, g * HD : (g + 1) * HD] = (moved / total).astype(BF)

    run(
        gather_plane(comm, plane_place(att, True, 0), 64, xe, ye),
        gather_plane(comm, plane_place(att, False, 64), 64, ye, xe),
    )

    def branch(kk, zt):
        rows = att[2 * kk + zt // 2, pl.ds((zt % 2) * 2, 2)].reshape(256, 512)
        return mm(rows, ow_ref[...])

    offsets = (2, 1, 3, 0)
    crossing = []
    for off in offsets:
        zt = (z + off) % 4
        cs[zt] = branch(o, zt).astype(BF)
        crossing.append(comm.send(cs.at[zt], cr.at[zt], sib))
    w_copy.wait()
    res_copy.wait()
    near = []
    for at, off in enumerate(offsets):
        zt = (z + off) % 4
        part = branch(k, zt)
        crossing[at].wait_recv()
        part = part + cr[zt].astype(F32)
        if off == 2:
            zs[0] = part.astype(BF)
            far = (
                comm.send(zs.at[0, 0:128], zf.at[0], ze[0]),
                comm.send(zs.at[0, 128:256], zf.at[1], ze[1]),
            )
        elif off == 1:
            far[0].wait_recv()
            zs[1, 0:128] = (part[0:128] + zf[0].astype(F32)).astype(BF)
            zs[1, 128:256] = part[128:256].astype(BF)
            near.append(comm.send(zs.at[1], zn.at[0], ze[0]))
        elif off == 3:
            far[1].wait_recv()
            zs[2, 0:128] = part[0:128].astype(BF)
            zs[2, 128:256] = (part[128:256] + zf[1].astype(F32)).astype(BF)
            near.append(comm.send(zs.at[2], zn.at[1], ze[1]))
        else:
            part = part + res[...].astype(F32)
            near[0].wait_recv()
            part = part + zn[0].astype(F32)
            near[1].wait_recv()
            hid[...] = part + zn[1].astype(F32)

    hidden = hid[...]
    act[k, z] = (hidden * gain_ref[...]).astype(BF)
    def act_block(d, start=0, count=256):
        return act.at[k, (z + d) % 4, pl.ds(start, count)]

    def pass_on(d, dev, start=0, count=256):
        block = act_block(d, start, count)
        return comm.send(block, block, dev)

    act_up, act_down = pass_on(0, ze[0]), pass_on(0, ze[1])
    across = {0: pass_on(0, sib)}
    ssq_out[...] = nt_dot(jnp.ones((8, 512), F32), hidden * hidden, precision=lax.Precision.HIGHEST)
    ssq_in[s] = ssq_out[...]
    squares = [
        comm.send(ssq_out, ssq_in.at[s], {"seq": (s + off) % 16}) for off in range(1, 16)
    ]
    inverses = []

    def share_inverse():
        for copy in squares:
            copy.wait_recv()
        total = ssq_in[0]
        for at in range(1, 16):
            total = total + ssq_in[at]
        inv[k, z] = lax.rsqrt(total / D + NORM_EPS)
        for dz in range(4):
            for flip in range(2):
                if dz or flip:
                    to = section_of((z + dz) % 4, (k + flip) % 2)
                    inverses.append(comm.send(inv.at[k, z], inv.at[k, z], to))

    def unit(u):
        ch = u // 4
        zt = u % 4 if ch else (z + ORDER[u]) % 4
        by_y = u % 2 == 0
        main, main_ends, side, side_ends = (y, ye, x, xe) if by_y else (x, xe, y, ye)

        def product(p):
            rows = []
            for j in range(4):
                b = (j * 4 + p) if by_y else (p * 4 + j)
                rows += [wv[0, b], wv[1, b]]
            return nt_dot(act[ch, zt], jnp.concatenate(rows, axis=0))

        acc = product((main + 2) % 4)
        for j in range(4):
            s1[u, j] = acc[:, j * 128 : (j + 1) * 128].astype(BF)
        far = [
            comm.send(s1.at[u, 2 * e : 2 * e + 2], r1.at[u, 2 * e : 2 * e + 2], main_ends[e])
            for e in range(2)
        ]
        yield
        early, late = [], []
        for e, step in ((0, 1), (1, 3)):
            acc = product((main + step) % 4)
            for j in range(4):
                s2[u, e, j] = acc[:, j * 128 : (j + 1) * 128].astype(BF)
            span = pl.ds(2 - 2 * e, 2)
            early.append(comm.send(s2.at[u, e, span], r2.at[u, e, span], main_ends[e]))
        yield
        acc = product(main)
        for j in range(4):
            own[u, j] = acc[:, j * 128 : (j + 1) * 128]
        yield
        for e in range(2):
            far[e].wait_recv()
            span = pl.ds(2 * e, 2)
            s2[u, e, span] = (s2[u, e, span].astype(F32) + r1[u, span].astype(F32)).astype(BF)
            late.append(comm.send(s2.at[u, e, span], r2.at[u, e, span], main_ends[e]))
        yield
        for copy in (*early, *late):
            copy.wait_recv()

        def summed(j):
            return own[u, j] + r2[u, 0, j].astype(F32) + r2[u, 1, j].astype(F32)

        def summed_rows(j, rest):
            return (
                own[u, j, rest] + r2[u, 0, j, rest].astype(F32) + r2[u, 1, j, rest].astype(F32)
            )

        t1[u] = summed((side + 2) % 4).astype(BF)
        last_far = [
            comm.send(t1.at[u, 128 * e : 128 * e + 128], u1.at[u, e], side_ends[e])
            for e in range(2)
        ]
        parts = summed((side + 1) % 4), summed((side + 3) % 4)
        last = []
        for e in range(2):
            rest = slice(128 - 128 * e, 256 - 128 * e)
            t2[u, e, rest] = parts[e][rest].astype(BF)
            last.append(comm.send(t2.at[u, e, rest], u2.at[u, e, rest], side_ends[e]))
        yield
        for e in range(2):
            last_far[e].wait_recv()
            rest = slice(128 * e, 128 * e + 128)
            j = (side + 1 + 2 * e) % 4
            part = summed_rows(j, rest) + u1[u, e].astype(F32)
            t2[u, e, rest] = part.astype(BF)
            last.append(comm.send(t2.at[u, e, rest], u2.at[u, e, rest], side_ends[e]))
        yield
        for copy in last:
            copy.wait_recv()
        part = summed(side) + u2[u, 0].astype(F32) + u2[u, 1].astype(F32)
        scale = jnp.transpose(inv[ch, zt])[:, 0:1]
        mixed[pl.ds(pl.multiple_of(ch * 1024 + zt * 256, 256), 256)] = part * scale
        yield

    lane = lax.broadcasted_iota(jnp.int32, (8, 128), 1)
    row = lax.broadcasted_iota(jnp.int32, (8, 128), 0)
    is_path = lane < 64
    low_row = lax.broadcasted_iota(jnp.int32, (1, 128), 1) < 64

    def twice(value):
        return jnp.concatenate([value, value], axis=1)

    taps = twice(cw_ref[...])
    bias = twice(cb_ref[...])

    def conv(ch):
        first, count = CHUNKS[ch]
        length = count // 8

        def strided(j):
            return mixed[pl.ds(first + j, 8, stride=length), :]

        def before(j):
            if first:
                return mixed[pl.ds(first - length + j, 8, stride=length), :]
            return jnp.where(row == 0, 0.0, pltpu.roll(strided(j), 1, 0))

        def step(j, carried):
            older, old, recent = carried
            now = strided(j)
            total = (
                bias + taps[0:1] * older + taps[1:2] * old + taps[2:3] * recent + taps[3:4] * now
            )
            value = jnp.where(is_path, total, now)
            at = pl.ds(pl.multiple_of(first + j * 8, 8), 8)
            uz[at, :] = value / (1.0 + jnp.exp(-value))
            return (old, recent, now)

        begin = tuple(before(length - 3 + i) for i in range(3))
        lax.fori_loop(0, length, step, begin, unroll=8)

    def sum_maps(ch):
        first, count = CHUNKS[ch]
        n = count // 8
        whole = pl.ds(0, n + 16)
        rank_weight = jnp.concatenate([pw_ref[:, 0:256], jnp.zeros((64, 256), BF)], axis=0)
        map_weight = jnp.transpose(pw_ref[:, 256:272].astype(F32))
        map_weight = jnp.concatenate([map_weight, jnp.zeros((16, 64), F32)], axis=1).astype(BF)

        def local_block(i):
            u = uz[pl.ds(pl.multiple_of(first + i * n, n), n), :].astype(BF)
            gs[ch, i, 0:n] = mm(u, rank_weight).astype(BF)
            if n < 128:
                u = jnp.concatenate([u, jnp.zeros((128 - n, 128), BF)], axis=0)
            maps = nt_dot(map_weight, u).astype(BF)
            gs[ch, i, n : n + 16] = jnp.concatenate([maps, jnp.zeros((16, 128), BF)], axis=1)

        moved = []
        for off in (4, 3, 5, 2, 6, 1, 7):
            i = (c + off) % 8
            local_block(i)
            moved.append(comm.send(gs.at[ch, i, whole], gd.at[ch, c, whole], {"section": i}))
        local_block(c)
        gd[ch, c, whole] = gs[ch, c, whole]
        yield

        def total_of(parts):
            total = parts[0].astype(F32)
            for part in parts[1:]:
                total = total + part.astype(F32)
            return total.astype(BF)

        axes = ((x, lambda d: seq_of((x + d) % 4, y)), (y, lambda d: seq_of(x, (y + d) % 4)))

        def spread_out(h, step, value):
            mine, to = axes[h ^ step]
            gx[ch, h, step, mine, whole] = value
            block = gx.at[ch, h, step, mine, whole]
            return [comm.send(block, block, to(d)) for d in (2, 1, 3)]

        def gathered(h, step):
            return total_of([gx[ch, h, step, at, whole] for at in range(4)])

        for copy in moved:
            copy.wait_recv()
        value = total_of([gd[ch, at, whole] for at in range(8)])
        sent = [spread_out(h, 0, value[:, 128 * h : 128 * h + 128]) for h in range(2)]
        yield
        for h in range(2):
            for copy in sent[h]:
                copy.wait_recv()
            sent[h] = spread_out(h, 1, gathered(h, 0))
        yield
        for h in range(2):
            for copy in sent[h]:
                copy.wait_recv()
            gfull[ch, c, whole, 128 * h : 128 * h + 128] = gathered(h, 1)
        block = gfull.at[ch, c, whole]
        moved = [
            comm.send(block, block, {"section": (c + off) % 8}) for off in (4, 3, 5, 2, 6, 1, 7)
        ]
        yield
        for copy in moved:
            copy.wait_recv()
        yield

    lane8 = lax.broadcasted_iota(jnp.int32, (16, 1024), 1)
    row8 = lax.broadcasted_iota(jnp.int32, (16, 1024), 0)
    which = 2 * ((lane8 // 128) % 4) + (lane8 % 128) // 64 + 8 * (lane8 // 512)
    spread = jnp.where(row8 == which, 1.0, 0.0).astype(BF)

    def decays():
        al = twice(al_ref[...])
        return [
            -jnp.exp(jnp.where(low_row, al[2 * q : 2 * q + 1], al[2 * q + 1 : 2 * q + 2])) * LOG2E
            for q in range(4)
        ]

    def prepare(ch):
        first, count = CHUNKS[ch]
        n = count // 8
        dtw = jnp.concatenate([dtw_ref[...], dtw_ref[...]], axis=0)
        dtb = twice(dtb_ref[...])
        low = lax.broadcasted_iota(jnp.int32, (n, 128), 1) < 64
        for i in range(8):
            rows = pl.ds(i * n, n)
            pre = nt_dot(gfull[ch, i, 0:n], dtw) + dtb
            st = jnp.maximum(pre, 0.0) + jnp.log1p(jnp.exp(-jnp.abs(pre)))
            step_size[rows] = st
            u = uz[pl.ds(first + i * n, n)].astype(BF).astype(F32)
            drive[rows] = st * jnp.where(low, u, pltpu.roll(u, 64, 1))
            maps = gfull[ch, i, n : n + 16, 0:128]
            wide[rows] = lax.dot_general(maps, spread, TN, preferred_element_type=F32)[0:n]

    nothing = jnp.zeros((8, 128), F32)

    def advance(j, states, decay):
        at = pl.ds(pl.multiple_of(j * 8, 8), 8)
        st = step_size[at]
        du = drive[at]
        return st, tuple(
            jnp.exp2(st * decay[q]) * states[q] + du * wide[at, q * 128 : (q + 1) * 128]
            for q in range(4)
        )

    def segment_ends(ch):
        decay = decays()

        def first_pass(j, carried):
            total, states = carried
            st, states = advance(j, states, decay)
            return (total + st, states)

        return lax.fori_loop(
            0, CHUNKS[ch][1] // 8, first_pass, (nothing, (nothing,) * 4), unroll=8
        )

    def entries(found, carry):
        total, ends = found
        decay = decays()
        starts, after = [], []
        for q in range(4):
            factor = jnp.exp2(total * decay[q])
            value = ends[q]
            for d in (1, 2, 4):
                moved_factor = jnp.where(row < d, 1.0, pltpu.roll(factor, d, 0))
                moved_value = jnp.where(row < d, 0.0, pltpu.roll(value, d, 0))
                value = factor * moved_value + value
                factor = factor * moved_factor
            if carry is not None:
                value = value + factor * carry[q]
            start = pltpu.roll(value, 1, 0)
            starts.append(jnp.where(row < 1, 0.0 if carry is None else carry[q], start))
            after.append(jnp.broadcast_to(value[7:8], (8, 128)))
        return starts, after

    def finish(ch, starts):
        first, count = CHUNKS[ch]
        length = count // 8
        decay = decays()
        skip = twice(skip_ref[...])

        def second_pass(j, states):
            _, states = advance(j, states, decay)
            at = pl.ds(pl.multiple_of(j * 8, 8), 8)
            gated = uz[pl.ds(pl.multiple_of(first + j * 8, 8), 8)]
            read = states[0] * wide[at, 512:640]
            for q in range(1, 4):
                read = read + states[q] * wide[at, 512 + q * 128 : 640 + q * 128]
            read = read + pltpu.roll(read, 64, 1)
            u = gated.astype(BF).astype(F32)
            ys[pl.ds(j, 8, stride=length), :] = (read + skip * u) * pltpu.roll(gated, 64, 1)
            return states

        lax.fori_loop(0, length, second_pass, tuple(starts), unroll=8)
        for at in range(0, count, 128):
            block = jnp.transpose(ys[at : at + 128, :])
            out_ref[:, first + at : first + at + 128] = block[0:64].astype(BF)

    units = {}

    def go(*steps):
        for step in steps:
            u, count = step // 10, step % 10
            if u not in units:
                units[u] = unit(u)
            for _ in range(count):
                next(units[u])

    across[0].wait_recv()
    go(1)
    act_up.wait_recv()
    far_up = pass_on(-1, ze[0], 0, 128)
    across[-1] = pass_on(-1, sib)
    act_down.wait_recv()
    far_down = pass_on(1, ze[1], 128, 128)
    across[1] = pass_on(1, sib)
    go(1)
    across[-1].wait_recv()
    go(11, 1, 11)
    far_up.wait_recv()
    far_down.wait_recv()
    across[2] = pass_on(2, sib)
    go(11, 1)
    across[1].wait_recv()
    go(23)
    share_inverse()
    go(11)
    across[2].wait_recv()
    go(33, 1, 11, 21, 31)
    for copy in inverses:
        copy.wait_recv()
    go(43, 53, 1, 11, 1, 11, 21, 31, 41, 51, 21, 31, 63, 73, 21, 31)
    conv(0)
    maps0 = sum_maps(0)
    next(maps0)
    go(41, 51, 61, 71)
    next(maps0)
    go(41, 51, 41, 51)
    conv(1)
    maps1 = sum_maps(1)
    next(maps1)
    next(maps0)
    go(61, 71)
    next(maps1)
    next(maps0)
    go(61, 71)
    next(maps1)
    next(maps0)
    go(61, 71)
    conv(2)
    maps2 = sum_maps(2)
    next(maps2)
    next(maps1)
    prepare(0)
    found = segment_ends(0)
    next(maps2)
    next(maps1)
    starts, carry = entries(found, None)
    finish(0, starts)
    next(maps2)
    prepare(1)
    found = segment_ends(1)
    next(maps2)
    starts, carry = entries(found, carry)
    finish(1, starts)
    next(maps2)
    prepare(2)
    starts, carry = entries(segment_ends(2), carry)
    finish(2, starts)
    comm.finish()


def body(
    queries, keys, values, residual, out_weight, norm_gain, in_weight, conv_weight, conv_bias,
    proj_weight, dt_weight, dt_bias, a_log, skip_gain,
):
    vmem = pl.BlockSpec(memory_space=pltpu.VMEM)
    anyspace = pl.BlockSpec(memory_space=pl.ANY)
    copies = 400
    return pl.pallas_call(
        front_kernel,
        out_shape=jax.ShapeDtypeStruct((64, 2048), BF),
        in_specs=[vmem, vmem, vmem, anyspace, vmem, vmem, anyspace] + [vmem] * 7,
        out_specs=vmem,
        scratch_shapes=[
            pltpu.VMEM((4, 4, 128, 256), BF),
            pltpu.VMEM((4, 4, 128, 512), BF),
            pltpu.VMEM((4, 256, 512), BF),
            pltpu.VMEM((4, 256, 512), BF),
            pltpu.VMEM((3, 256, 512), BF),
            pltpu.VMEM((2, 256, 512), BF),
            pltpu.VMEM((2, 128, 512), BF),
            pltpu.VMEM((2, 4, 256, 512), BF),
            pltpu.VMEM((256, 512), F32),
            pltpu.VMEM((8, 256), F32),
            pltpu.VMEM((16, 8, 256), F32),
            pltpu.VMEM((2, 4, 8, 256), F32),
            pltpu.VMEM((256, 512), BF),
            pltpu.VMEM((2, 16, 64, 512), BF),
            pltpu.VMEM((8, 4, 256, 128), BF),
            pltpu.VMEM((8, 4, 256, 128), BF),
            pltpu.VMEM((8, 2, 4, 256, 128), BF),
            pltpu.VMEM((8, 2, 4, 256, 128), BF),
            pltpu.VMEM((8, 4, 256, 128), F32),
            pltpu.VMEM((8, 256, 128), BF),
            pltpu.VMEM((8, 2, 128, 128), BF),
            pltpu.VMEM((8, 2, 256, 128), BF),
            pltpu.VMEM((8, 2, 256, 128), BF),
            pltpu.VMEM((2048, 128), F32),
            pltpu.VMEM((2048, 128), F32),
            pltpu.VMEM((3, 8, 144, 256), BF),
            pltpu.VMEM((3, 8, 144, 256), BF),
            pltpu.VMEM((3, 2, 2, 4, 144, 128), BF),
            pltpu.VMEM((3, 8, 144, 256), BF),
            pltpu.VMEM((1024, 128), F32),
            pltpu.VMEM((1024, 1024), F32),
            pltpu.VMEM((1024, 128), F32),
            pltpu.VMEM((1024, 128), F32),
            pltpu.SemaphoreType.DMA((copies,)),
            pltpu.SemaphoreType.DMA((copies,)),
            pltpu.SemaphoreType.DMA((2,)),
        ],
        compiler_params=pltpu.CompilerParams(
            collective_id=0, has_side_effects=True, vmem_limit_bytes=60 * 1024 * 1024
        ),
        name="front",
    )(
        queries, keys, values, residual, out_weight, norm_gain[None, :],
        jnp.transpose(in_weight, (1, 2, 3, 0)), conv_weight.T, conv_bias[None, :], proj_weight,
        dt_weight.T, dt_bias[None, :], a_log.T, skip_gain[None, :],
    )


def solution(mesh):
    return jax.shard_map(
        body,
        mesh=mesh,
        in_specs=(
            P("seq", "section"),
            P("seq", "section"),
            P("seq", "section"),
            P(None, "seq"),
            P("section", "seq"),
            P("seq"),
            P("seq", None, None, "section"),
            P(("seq", "section"), None),
            P(("seq", "section")),
            P(("seq", "section"), None),
            P(None, ("seq", "section")),
            P(("seq", "section")),
            P(("seq", "section"), None),
            P(("seq", "section")),
        ),
        out_specs=P(("seq", "section"), None),
        check_vma=False,
    )
```

```python
import math

import jax
import jax.numpy as jnp
from jax import lax
from jax.experimental import pallas as pl
from jax.experimental.pallas import tpu as pltpu
from jax.sharding import PartitionSpec as P

D = 8192
HD = 128
GROUP = 4
NST = 8
DT_RANK = 256
CONV = 4
NORM_EPS = 1e-05
MESH = pl.DeviceIdType.MESH
BF = jnp.bfloat16
F32 = jnp.float32
CHUNKS = ((0, 1024), (1024, 512), (1536, 512))
ORDER = (0, -1, 1, 2)
SLOT = {0: 0, 1: 1, 3: 2}
LOG2E = math.log2(math.e)
NT = (((1,), (1,)), ((), ()))
TN = (((0,), (0,)), ((), ()))


def nt_dot(a, b, **kw):
    return lax.dot_general(a, b, NT, preferred_element_type=F32, **kw)


def mm(a, b):
    return jnp.dot(a, b, preferred_element_type=F32)


class Comm:
    def __init__(self, send_sem, recv_sem):
        self.send_sem = send_sem
        self.recv_sem = recv_sem
        self.copies = []

    def send(self, src, dst, dev):
        at = len(self.copies)
        copy = pltpu.make_async_remote_copy(
            src_ref=src,
            dst_ref=dst,
            send_sem=self.send_sem.at[at],
            recv_sem=self.recv_sem.at[at],
            device_id=dev,
            device_id_type=MESH,
        )
        copy.start()
        self.copies.append(copy)
        return copy

    def finish(self):
        assert len(self.copies) <= 480
        for copy in self.copies:
            copy.wait_send()


def run(*streams):
    live = list(streams)
    while live:
        for stream in list(live):
            try:
                next(stream)
            except StopIteration:
                live.remove(stream)


def gather_plane(comm, place, size, first, second):
    half = size // 2
    one = comm.send(place(0, 0, 0, size), place(0, 0, 0, size), first[0])
    two = comm.send(place(0, 0, 0, size), place(0, 0, 0, size), first[1])

    def along(df):
        block = place(df, 0, 0, size)
        return comm.send(block, block, second[0]), comm.send(block, block, second[1])

    sent = [(0, along(0))]
    yield
    one.wait_recv()
    block = place(-1, 0, 0, half)
    three = comm.send(block, block, first[0])
    two.wait_recv()
    block = place(1, 0, half, size - half)
    four = comm.send(block, block, first[1])
    sent.append((-1, along(-1)))
    sent.append((1, along(1)))
    yield
    three.wait_recv()
    four.wait_recv()
    sent.append((2, along(2)))
    yield
    last = []
    for df, (up, down) in sent:
        up.wait_recv()
        block = place(df, -1, 0, half)
        last.append(comm.send(block, block, second[0]))
        down.wait_recv()
        block = place(df, 1, half, size - half)
        last.append(comm.send(block, block, second[1]))
    yield
    for copy in last:
        copy.wait_recv()


def front_kernel(
    q_ref, k_ref, v_ref, res_ref, ow_ref, gain_ref, w_ref, cw_ref, cb_ref, pw_ref,
    dtw_ref, dtb_ref, al_ref, skip_ref,
    out_ref,
    kv, att, cs, cr, held, zs, zn, zf, act, ssq_out, ssq_in, inv, res, wv,
    s1, r1, s2, r2, own, t1, u1, t2, u2, mixed, uz,
    gs, gd, gx, gfull,
    step_size, wide, drive, ys,
    send_sem, recv_sem, local_sem,
):
    s = lax.axis_index("seq")
    c = lax.axis_index("section")
    x, y = s // 4, s % 4
    z, k = c // 2, c % 2
    o = 1 - k

    def seq_of(cx, cy):
        return {"seq": cx * 4 + cy}

    def section_of(cz, ck):
        return {"section": cz * 2 + ck}

    xe = (seq_of((x + 1) % 4, y), seq_of((x + 3) % 4, y))
    ye = (seq_of(x, (y + 1) % 4), seq_of(x, (y + 3) % 4))
    ze = (section_of((z + 1) % 4, k), section_of((z + 3) % 4, k))
    sib = section_of(z, o)

    res_copies = [
        pltpu.make_async_copy(
            res_ref.at[pl.ds(1024 * ch + 256 * z + 128 * k, 128)], res.at[ch], local_sem.at[ch]
        )
        for ch in range(2)
    ]
    for copy in res_copies:
        copy.start()
    w_copy = pltpu.make_async_copy(w_ref, wv, local_sem.at[2])
    w_copy.start()

    barrier = pltpu.get_barrier_semaphore()
    for off in range(1, 16):
        pl.semaphore_signal(
            barrier, inc=1, device_id={"seq": (s + off) % 16}, device_id_type=MESH
        )
    for off in range(1, 8):
        pl.semaphore_signal(
            barrier, inc=1, device_id={"section": (c + off) % 8}, device_id_type=MESH
        )
    kv[x, y, :, 0:HD] = k_ref[...]
    kv[x, y, :, HD:] = v_ref[...]
    pl.semaphore_wait(barrier, 22)

    comm = Comm(send_sem, recv_sem)

    def plane_place(buf, x_first, base, by_rows=True):
        def place(df, ds, start, count):
            if x_first:
                cx, cy = (x + df) % 4, (y + ds) % 4
            else:
                cx, cy = (x + ds) % 4, (y + df) % 4
            return buf.at[cx, cy, pl.ds(base + start, count)]

        return place

    run(
        gather_plane(comm, plane_place(kv, True, 0), 64, xe, ye),
        gather_plane(comm, plane_place(kv, False, 64), 64, ye, xe),
    )

    query_pos = s * 128 + lax.broadcasted_iota(jnp.int32, (128, 2048), 0)
    key_pos = lax.broadcasted_iota(jnp.int32, (128, 2048), 1)
    allowed = query_pos >= key_pos
    key_rows = kv[:, :, :, 0:HD].reshape(2048, HD)
    value_rows = kv[:, :, :, HD:].reshape(2048, HD)
    for g in range(GROUP):
        scores = nt_dot(q_ref[:, g * HD : (g + 1) * HD], key_rows)
        scores = jnp.where(allowed, scores, -1e30)
        top = jnp.max(scores, axis=1, keepdims=True)
        terms = jnp.exp2((scores - top) * (LOG2E / math.sqrt(HD)))
        total = jnp.sum(terms, axis=1, keepdims=True)
        moved = mm(terms.astype(BF), value_rows)
        att[x, y, :, g * HD : (g + 1) * HD] = (moved / total).astype(BF)

    run(
        gather_plane(comm, plane_place(att, True, 0), 64, xe, ye),
        gather_plane(comm, plane_place(att, False, 64), 64, ye, xe),
    )

    w_copy.wait()
    for copy in res_copies:
        copy.wait()
    across = ({}, {})
    offsets = (2, 1, 3, 0)

    def branch(ch, zt, kk):
        rows = att[2 * ch + zt // 2, 2 * (zt % 2) + kk]
        return mm(rows, ow_ref[...])

    def section_sum(ch):
        crossing = []
        for off in offsets:
            zt = (z + off) % 4
            cs[ch, zt] = branch(ch, zt, o).astype(BF)
            crossing.append(comm.send(cs.at[ch, zt], cr.at[ch, zt], sib))
        yield
        for at, off in enumerate(offsets):
            zt = (z + off) % 4
            part = branch(ch, zt, k)
            crossing[at].wait_recv()
            part = part + cr[ch, zt].astype(F32)
            if off == 2:
                zs[ch, 0] = part.astype(BF)
                far = [
                    comm.send(zs.at[ch, 0, 64 * e : 64 * e + 64], zf.at[ch, e], ze[e])
                    for e in range(2)
                ]
            else:
                held[ch, SLOT[off]] = part
        yield
        near = []
        for e in range(2):
            far[e].wait_recv()
            rest = slice(64 - 64 * e, 128 - 64 * e)
            same = slice(64 * e, 64 * e + 64)
            slot = 1 if e == 0 else 2
            source = 1 if e == 0 else 3
            zs[ch, slot, rest] = sums(ch, source, rest).astype(BF)
            zs[ch, slot, same] = (sums(ch, source, same) + zf[ch, e].astype(F32)).astype(BF)
            near.append(comm.send(zs.at[ch, slot], zn.at[ch, e], ze[e]))
        yield
        part = sums(ch, 0, slice(0, 128)) + res[ch].astype(F32)
        for e in range(2):
            near[e].wait_recv()
            part = part + zn[ch, e].astype(F32)
        act[ch, z, k] = (part * gain_ref[...]).astype(BF)

        def pass_on(d, dev, start=0, count=128):
            block = act.at[ch, (z + d) % 4, k, pl.ds(start, count)]
            return comm.send(block, block, dev)

        up, down = pass_on(0, ze[0]), pass_on(0, ze[1])
        across[ch][0] = pass_on(0, sib)
        ssq_out[:, 128 * ch : 128 * ch + 128] = nt_dot(
            jnp.ones((8, 512), F32), part * part, precision=lax.Precision.HIGHEST
        )
        yield
        up.wait_recv()
        far_up = pass_on(-1, ze[0], 0, 64)
        across[ch][-1] = pass_on(-1, sib)
        down.wait_recv()
        far_down = pass_on(1, ze[1], 64, 64)
        across[ch][1] = pass_on(1, sib)
        yield
        far_up.wait_recv()
        far_down.wait_recv()
        across[ch][2] = pass_on(2, sib)
        yield

    def sums(ch, off, rows):
        return held[ch, SLOT[off], rows]

    squares = []
    inverses = []

    def share_squares():
        ssq_in[s] = ssq_out[...]
        for off in range(1, 16):
            squares.append(comm.send(ssq_out, ssq_in.at[s], {"seq": (s + off) % 16}))

    def share_inverse():
        for copy in squares:
            copy.wait_recv()
        total = ssq_in[0]
        for at in range(1, 16):
            total = total + ssq_in[at]
        inv[z, k] = lax.rsqrt(total / D + NORM_EPS)
        for dz in range(4):
            for flip in range(2):
                if dz or flip:
                    to = section_of((z + dz) % 4, (k + flip) % 2)
                    inverses.append(comm.send(inv.at[z, k], inv.at[z, k], to))

    def unit(pair, kk):
        ch = pair // 4
        u = 2 * pair + kk
        zt = pair % 4 if ch else (z + ORDER[pair]) % 4
        main, main_ends, side, side_ends = (x, xe, y, ye) if kk else (y, ye, x, xe)

        def product(p):
            rows = []
            for j in range(4):
                b = (p * 4 + j) if kk else (j * 4 + p)
                rows += [wv[0, b], wv[1, b]]
            return nt_dot(act[ch, zt, kk], jnp.concatenate(rows, axis=0))

        acc = product((main + 2) % 4)
        for j in range(4):
            s1[u, j] = acc[:, j * 128 : (j + 1) * 128].astype(BF)
        far = [
            comm.send(s1.at[u, 2 * e : 2 * e + 2], r1.at[u, 2 * e : 2 * e + 2], main_ends[e])
            for e in range(2)
        ]
        yield
        early, late = [], []
        for e, step in ((0, 1), (1, 3)):
            acc = product((main + step) % 4)
            for j in range(4):
                s2[u, e, j] = acc[:, j * 128 : (j + 1) * 128].astype(BF)
            span = pl.ds(2 - 2 * e, 2)
            early.append(comm.send(s2.at[u, e, span], r2.at[u, e, span], main_ends[e]))
        yield
        acc = product(main)
        for j in range(4):
            own[u, j] = acc[:, j * 128 : (j + 1) * 128]
        yield
        for e in range(2):
            far[e].wait_recv()
            span = pl.ds(2 * e, 2)
            s2[u, e, span] = (s2[u, e, span].astype(F32) + r1[u, span].astype(F32)).astype(BF)
            late.append(comm.send(s2.at[u, e, span], r2.at[u, e, span], main_ends[e]))
        yield
        for copy in (*early, *late):
            copy.wait_recv()

        def summed(j, rows=slice(0, 128)):
            return (
                own[u, j, rows] + r2[u, 0, j, rows].astype(F32) + r2[u, 1, j, rows].astype(F32)
            )

        t1[u] = summed((side + 2) % 4).astype(BF)
        last_far = [
            comm.send(t1.at[u, 64 * e : 64 * e + 64], u1.at[u, e], side_ends[e])
            for e in range(2)
        ]
        last = []
        for e in range(2):
            rest = slice(64 - 64 * e, 128 - 64 * e)
            t2[u, e, rest] = summed((side + 1 + 2 * e) % 4, rest).astype(BF)
            last.append(comm.send(t2.at[u, e, rest], u2.at[u, e, rest], side_ends[e]))
        yield
        for e in range(2):
            last_far[e].wait_recv()
            rest = slice(64 * e, 64 * e + 64)
            part = summed((side + 1 + 2 * e) % 4, rest) + u1[u, e].astype(F32)
            t2[u, e, rest] = part.astype(BF)
            last.append(comm.send(t2.at[u, e, rest], u2.at[u, e, rest], side_ends[e]))
        yield
        for copy in last:
            copy.wait_recv()
        part = summed(side) + u2[u, 0].astype(F32) + u2[u, 1].astype(F32)
        scale = jnp.transpose(inv[zt, kk, :, 128 * ch : 128 * ch + 128])[:, 0:1]
        at = pl.multiple_of(ch * 1024 + zt * 256 + kk * 128, 128)
        mixed[pl.ds(at, 128)] = part * scale
        yield

    lane = lax.broadcasted_iota(jnp.int32, (8, 128), 1)
    row = lax.broadcasted_iota(jnp.int32, (8, 128), 0)
    is_path = lane < 64
    low_row = lax.broadcasted_iota(jnp.int32, (1, 128), 1) < 64

    def twice(value):
        return jnp.concatenate([value, value], axis=1)

    taps = twice(cw_ref[...])
    bias = twice(cb_ref[...])

    def conv(ch):
        first, count = CHUNKS[ch]
        length = count // 8

        def strided(j):
            return mixed[pl.ds(first + j, 8, stride=length), :]

        def before(j):
            if first:
                return mixed[pl.ds(first - length + j, 8, stride=length), :]
            return jnp.where(row == 0, 0.0, pltpu.roll(strided(j), 1, 0))

        def step(j, carried):
            older, old, recent = carried
            now = strided(j)
            total = (
                bias + taps[0:1] * older + taps[1:2] * old + taps[2:3] * recent + taps[3:4] * now
            )
            value = jnp.where(is_path, total, now)
            at = pl.ds(pl.multiple_of(first + j * 8, 8), 8)
            uz[at, :] = value / (1.0 + jnp.exp(-value))
            return (old, recent, now)

        begin = tuple(before(length - 3 + i) for i in range(3))
        lax.fori_loop(0, length, step, begin, unroll=8)

    def sum_maps(ch):
        first, count = CHUNKS[ch]
        n = count // 8
        whole = pl.ds(0, n + 16)
        rank_weight = jnp.concatenate([pw_ref[:, 0:256], jnp.zeros((64, 256), BF)], axis=0)
        map_weight = jnp.transpose(pw_ref[:, 256:272].astype(F32))
        map_weight = jnp.concatenate([map_weight, jnp.zeros((16, 64), F32)], axis=1).astype(BF)

        def local_block(i):
            u = uz[pl.ds(pl.multiple_of(first + i * n, n), n), :].astype(BF)
            gs[ch, i, 0:n] = mm(u, rank_weight).astype(BF)
            if n < 128:
                u = jnp.concatenate([u, jnp.zeros((128 - n, 128), BF)], axis=0)
            maps = nt_dot(map_weight, u).astype(BF)
            gs[ch, i, n : n + 16] = jnp.concatenate([maps, jnp.zeros((16, 128), BF)], axis=1)

        moved = []
        for off in (4, 3, 5, 2, 6, 1, 7):
            i = (c + off) % 8
            local_block(i)
            moved.append(comm.send(gs.at[ch, i, whole], gd.at[ch, c, whole], {"section": i}))
        local_block(c)
        gd[ch, c, whole] = gs[ch, c, whole]
        yield

        def total_of(parts):
            total = parts[0].astype(F32)
            for part in parts[1:]:
                total = total + part.astype(F32)
            return total.astype(BF)

        axes = ((x, lambda d: seq_of((x + d) % 4, y)), (y, lambda d: seq_of(x, (y + d) % 4)))

        def spread_out(h, step, value):
            mine, to = axes[h ^ step]
            gx[ch, h, step, mine, whole] = value
            block = gx.at[ch, h, step, mine, whole]
            return [comm.send(block, block, to(d)) for d in (2, 1, 3)]

        def gathered(h, step):
            return total_of([gx[ch, h, step, at, whole] for at in range(4)])

        for copy in moved:
            copy.wait_recv()
        value = total_of([gd[ch, at, whole] for at in range(8)])
        sent = [spread_out(h, 0, value[:, 128 * h : 128 * h + 128]) for h in range(2)]
        yield
        for h in range(2):
            for copy in sent[h]:
                copy.wait_recv()
            sent[h] = spread_out(h, 1, gathered(h, 0))
        yield
        for h in range(2):
            for copy in sent[h]:
                copy.wait_recv()
            gfull[ch, c, whole, 128 * h : 128 * h + 128] = gathered(h, 1)
        block = gfull.at[ch, c, whole]
        moved = [
            comm.send(block, block, {"section": (c + off) % 8}) for off in (4, 3, 5, 2, 6, 1, 7)
        ]
        yield
        for copy in moved:
            copy.wait_recv()
        yield

    lane8 = lax.broadcasted_iota(jnp.int32, (16, 1024), 1)
    row8 = lax.broadcasted_iota(jnp.int32, (16, 1024), 0)
    which = 2 * ((lane8 // 128) % 4) + (lane8 % 128) // 64 + 8 * (lane8 // 512)
    spread = jnp.where(row8 == which, 1.0, 0.0).astype(BF)

    def decays():
        al = twice(al_ref[...])
        return [
            -jnp.exp(jnp.where(low_row, al[2 * q : 2 * q + 1], al[2 * q + 1 : 2 * q + 2])) * LOG2E
            for q in range(4)
        ]

    def prepare(ch):
        first, count = CHUNKS[ch]
        n = count // 8
        dtw = jnp.concatenate([dtw_ref[...], dtw_ref[...]], axis=0)
        dtb = twice(dtb_ref[...])
        low = lax.broadcasted_iota(jnp.int32, (n, 128), 1) < 64
        for i in range(8):
            rows = pl.ds(i * n, n)
            pre = nt_dot(gfull[ch, i, 0:n], dtw) + dtb
            st = jnp.maximum(pre, 0.0) + jnp.log1p(jnp.exp(-jnp.abs(pre)))
            step_size[rows] = st
            u = uz[pl.ds(first + i * n, n)].astype(BF).astype(F32)
            drive[rows] = st * jnp.where(low, u, pltpu.roll(u, 64, 1))
            maps = gfull[ch, i, n : n + 16, 0:128]
            wide[rows] = lax.dot_general(maps, spread, TN, preferred_element_type=F32)[0:n]

    nothing = jnp.zeros((8, 128), F32)

    def advance(j, states, decay):
        at = pl.ds(pl.multiple_of(j * 8, 8), 8)
        st = step_size[at]
        du = drive[at]
        return st, tuple(
            jnp.exp2(st * decay[q]) * states[q] + du * wide[at, q * 128 : (q + 1) * 128]
            for q in range(4)
        )

    def segment_ends(ch):
        decay = decays()

        def first_pass(j, carried):
            total, states = carried
            st, states = advance(j, states, decay)
            return (total + st, states)

        return lax.fori_loop(
            0, CHUNKS[ch][1] // 8, first_pass, (nothing, (nothing,) * 4), unroll=8
        )

    def entries(found, carry):
        total, ends = found
        decay = decays()
        starts, after = [], []
        for q in range(4):
            factor = jnp.exp2(total * decay[q])
            value = ends[q]
            for d in (1, 2, 4):
                moved_factor = jnp.where(row < d, 1.0, pltpu.roll(factor, d, 0))
                moved_value = jnp.where(row < d, 0.0, pltpu.roll(value, d, 0))
                value = factor * moved_value + value
                factor = factor * moved_factor
            if carry is not None:
                value = value + factor * carry[q]
            start = pltpu.roll(value, 1, 0)
            starts.append(jnp.where(row < 1, 0.0 if carry is None else carry[q], start))
            after.append(jnp.broadcast_to(value[7:8], (8, 128)))
        return starts, after

    def finish(ch, starts):
        first, count = CHUNKS[ch]
        length = count // 8
        decay = decays()
        skip = twice(skip_ref[...])

        def second_pass(j, states):
            _, states = advance(j, states, decay)
            at = pl.ds(pl.multiple_of(j * 8, 8), 8)
            gated = uz[pl.ds(pl.multiple_of(first + j * 8, 8), 8)]
            read = states[0] * wide[at, 512:640]
            for q in range(1, 4):
                read = read + states[q] * wide[at, 512 + q * 128 : 640 + q * 128]
            read = read + pltpu.roll(read, 64, 1)
            u = gated.astype(BF).astype(F32)
            ys[pl.ds(j, 8, stride=length), :] = (read + skip * u) * pltpu.roll(gated, 64, 1)
            return states

        lax.fori_loop(0, length, second_pass, tuple(starts), unroll=8)
        for at in range(0, count, 128):
            block = jnp.transpose(ys[at : at + 128, :])
            out_ref[:, first + at : first + at + 128] = block[0:64].astype(BF)

    pairs = {}

    def go(*steps):
        for step in steps:
            pair, count = step // 10, step % 10
            if pair not in pairs:
                pairs[pair] = (unit(pair, 0), unit(pair, 1))
            for _ in range(count):
                for stream in pairs[pair]:
                    next(stream)

    sec0, sec1 = section_sum(0), section_sum(1)
    for stream in (sec0, sec0, sec1, sec0, sec1, sec0, sec1):
        next(stream)
    across[0][0].wait_recv()
    go(2)
    next(sec0)
    next(sec1)
    share_squares()
    across[0][-1].wait_recv()
    go(11, 1, 12, 1)
    next(sec0)
    next(sec1)
    across[0][1].wait_recv()
    go(23, 11, 1)
    across[0][2].wait_recv()
    go(33, 21)
    next(sec1)
    go(11, 1)
    share_inverse()
    for copy in across[1].values():
        copy.wait_recv()
    go(43, 31, 21, 11)
    for copy in inverses:
        copy.wait_recv()
    go(53, 41, 31, 21, 1, 11)
    go(63, 51, 41, 31, 21)
    go(73, 61, 51, 41, 31)
    conv(0)
    maps0 = sum_maps(0)
    next(maps0)
    go(71, 61, 51, 41)
    next(maps0)
    go(71, 61, 51)
    conv(1)
    maps1 = sum_maps(1)
    next(maps1)
    next(maps0)
    go(71, 61)
    next(maps1)
    go(71)
    conv(2)
    maps2 = sum_maps(2)
    next(maps2)
    next(maps1)
    next(maps0)
    next(maps2)
    next(maps1)
    next(maps0)
    prepare(0)
    next(maps2)
    found = segment_ends(0)
    next(maps1)
    starts, carry = entries(found, None)
    next(maps2)
    finish(0, starts)
    prepare(1)
    found = segment_ends(1)
    starts, carry = entries(found, carry)
    finish(1, starts)
    next(maps2)
    prepare(2)
    starts, carry = entries(segment_ends(2), carry)
    finish(2, starts)
    comm.finish()


def body(
    queries, keys, values, residual, out_weight, norm_gain, in_weight, conv_weight, conv_bias,
    proj_weight, dt_weight, dt_bias, a_log, skip_gain,
):
    vmem = pl.BlockSpec(memory_space=pltpu.VMEM)
    anyspace = pl.BlockSpec(memory_space=pl.ANY)
    copies = 480
    return pl.pallas_call(
        front_kernel,
        out_shape=jax.ShapeDtypeStruct((64, 2048), BF),
        in_specs=[vmem, vmem, vmem, anyspace, vmem, vmem, anyspace] + [vmem] * 7,
        out_specs=vmem,
        scratch_shapes=[
            pltpu.VMEM((4, 4, 128, 256), BF),
            pltpu.VMEM((4, 4, 128, 512), BF),
            pltpu.VMEM((2, 4, 128, 512), BF),
            pltpu.VMEM((2, 4, 128, 512), BF),
            pltpu.VMEM((2, 3, 128, 512), F32),
            pltpu.VMEM((2, 3, 128, 512), BF),
            pltpu.VMEM((2, 2, 128, 512), BF),
            pltpu.VMEM((2, 2, 64, 512), BF),
            pltpu.VMEM((2, 4, 2, 128, 512), BF),
            pltpu.VMEM((8, 256), F32),
            pltpu.VMEM((16, 8, 256), F32),
            pltpu.VMEM((4, 2, 8, 256), F32),
            pltpu.VMEM((2, 128, 512), BF),
            pltpu.VMEM((2, 16, 64, 512), BF),
            pltpu.VMEM((16, 4, 128, 128), BF),
            pltpu.VMEM((16, 4, 128, 128), BF),
            pltpu.VMEM((16, 2, 4, 128, 128), BF),
            pltpu.VMEM((16, 2, 4, 128, 128), BF),
            pltpu.VMEM((16, 4, 128, 128), F32),
            pltpu.VMEM((16, 128, 128), BF),
            pltpu.VMEM((16, 2, 64, 128), BF),
            pltpu.VMEM((16, 2, 128, 128), BF),
            pltpu.VMEM((16, 2, 128, 128), BF),
            pltpu.VMEM((2048, 128), F32),
            pltpu.VMEM((2048, 128), F32),
            pltpu.VMEM((3, 8, 144, 256), BF),
            pltpu.VMEM((3, 8, 144, 256), BF),
            pltpu.VMEM((3, 2, 2, 4, 144, 128), BF),
            pltpu.VMEM((3, 8, 144, 256), BF),
            pltpu.VMEM((1024, 128), F32),
            pltpu.VMEM((1024, 1024), F32),
            pltpu.VMEM((1024, 128), F32),
            pltpu.VMEM((1024, 128), F32),
            pltpu.SemaphoreType.DMA((copies,)),
            pltpu.SemaphoreType.DMA((copies,)),
            pltpu.SemaphoreType.DMA((3,)),
        ],
        compiler_params=pltpu.CompilerParams(
            collective_id=0, has_side_effects=True, vmem_limit_bytes=60 * 1024 * 1024
        ),
        name="front",
    )(
        queries, keys, values, residual, out_weight, norm_gain[None, :],
        jnp.transpose(in_weight, (1, 2, 3, 0)), conv_weight.T, conv_bias[None, :], proj_weight,
        dt_weight.T, dt_bias[None, :], a_log.T, skip_gain[None, :],
    )


def solution(mesh):
    return jax.shard_map(
        body,
        mesh=mesh,
        in_specs=(
            P("seq", "section"),
            P("seq", "section"),
            P("seq", "section"),
            P(None, "seq"),
            P("section", "seq"),
            P("seq"),
            P("seq", None, None, "section"),
            P(("seq", "section"), None),
            P(("seq", "section")),
            P(("seq", "section"), None),
            P(None, ("seq", "section")),
            P(("seq", "section")),
            P(("seq", "section"), None),
            P(("seq", "section")),
        ),
        out_specs=P(("seq", "section"), None),
        check_vma=False,
    )
```

```python
import math

import jax
import jax.numpy as jnp
from jax import lax
from jax.experimental import pallas as pl
from jax.experimental.pallas import tpu as pltpu
from jax.sharding import PartitionSpec as P

D = 8192
HD = 128
GROUP = 4
NST = 8
DT_RANK = 256
CONV = 4
NORM_EPS = 1e-05
MESH = pl.DeviceIdType.MESH
BF = jnp.bfloat16
F32 = jnp.float32
CHUNKS = ((0, 1024), (1024, 512), (1536, 512))
ORDER = (0, -1, 1, 2)
SLOT = {0: 0, 1: 1, 3: 2}
LOG2E = math.log2(math.e)
NT = (((1,), (1,)), ((), ()))
TN = (((0,), (0,)), ((), ()))


def nt_dot(a, b, **kw):
    return lax.dot_general(a, b, NT, preferred_element_type=F32, **kw)


def mm(a, b):
    return jnp.dot(a, b, preferred_element_type=F32)


class Comm:
    def __init__(self, send_sem, recv_sem):
        self.send_sem = send_sem
        self.recv_sem = recv_sem
        self.copies = []

    def send(self, src, dst, dev):
        at = len(self.copies)
        copy = pltpu.make_async_remote_copy(
            src_ref=src,
            dst_ref=dst,
            send_sem=self.send_sem.at[at],
            recv_sem=self.recv_sem.at[at],
            device_id=dev,
            device_id_type=MESH,
        )
        copy.start()
        self.copies.append(copy)
        return copy

    def finish(self):
        assert len(self.copies) <= 480
        for copy in self.copies:
            copy.wait_send()


def run(*streams):
    live = list(streams)
    while live:
        for stream in list(live):
            try:
                next(stream)
            except StopIteration:
                live.remove(stream)


def gather_plane(comm, place, size, first, second):
    half = size // 2
    one = comm.send(place(0, 0, 0, size), place(0, 0, 0, size), first[0])
    two = comm.send(place(0, 0, 0, size), place(0, 0, 0, size), first[1])

    def along(df):
        block = place(df, 0, 0, size)
        return comm.send(block, block, second[0]), comm.send(block, block, second[1])

    sent = [(0, along(0))]
    yield
    one.wait_recv()
    block = place(-1, 0, 0, half)
    three = comm.send(block, block, first[0])
    two.wait_recv()
    block = place(1, 0, half, size - half)
    four = comm.send(block, block, first[1])
    sent.append((-1, along(-1)))
    sent.append((1, along(1)))
    yield
    three.wait_recv()
    four.wait_recv()
    sent.append((2, along(2)))
    yield
    last = []
    for df, (up, down) in sent:
        up.wait_recv()
        block = place(df, -1, 0, half)
        last.append(comm.send(block, block, second[0]))
        down.wait_recv()
        block = place(df, 1, half, size - half)
        last.append(comm.send(block, block, second[1]))
    yield
    for copy in last:
        copy.wait_recv()


def front_kernel(
    q_hbm, k_ref, v_ref, res_ref, ow_hbm, gain_ref, w_ref, cw_ref, cb_ref, pw_ref,
    dtw_ref, dtb_ref, al_ref, skip_ref,
    out_ref,
    kv, att, cs, cr, held, zs, zn, zf, act, ssq_out, ssq_in, inv, res, wv,
    s1, r1, s2, r2, own, t1, u1, t2, u2, mixed, uz,
    gs, gr, gz, gd, gx, gfull,
    step_size, wide, drive, ys,
    q_ref, ow_ref,
    send_sem, recv_sem, local_sem,
):
    s = lax.axis_index("seq")
    c = lax.axis_index("section")
    x, y = s // 4, s % 4
    z, k = c // 2, c % 2
    o = 1 - k

    def seq_of(cx, cy):
        return {"seq": cx * 4 + cy}

    def section_of(cz, ck):
        return {"section": cz * 2 + ck}

    xe = (seq_of((x + 1) % 4, y), seq_of((x + 3) % 4, y))
    ye = (seq_of(x, (y + 1) % 4), seq_of(x, (y + 3) % 4))
    ze = (section_of((z + 1) % 4, k), section_of((z + 3) % 4, k))
    sib = section_of(z, o)

    barrier = pltpu.get_barrier_semaphore()
    for off in range(1, 16):
        pl.semaphore_signal(
            barrier, inc=1, device_id={"seq": (s + off) % 16}, device_id_type=MESH
        )
    for off in range(1, 8):
        pl.semaphore_signal(
            barrier, inc=1, device_id={"section": (c + off) % 8}, device_id_type=MESH
        )
    res_copies = [
        pltpu.make_async_copy(
            res_ref.at[pl.ds(1024 * ch + 256 * z + 128 * k, 128)], res.at[ch], local_sem.at[ch]
        )
        for ch in range(2)
    ]
    for copy in res_copies:
        copy.start()
    q_copy = pltpu.make_async_copy(q_hbm, q_ref, local_sem.at[3])
    q_copy.start()
    ow_copy = pltpu.make_async_copy(ow_hbm, ow_ref, local_sem.at[4])
    ow_copy.start()
    w_copy = pltpu.make_async_copy(w_ref, wv, local_sem.at[2])
    w_copy.start()

    kv[x, y, :, 0:HD] = k_ref[...]
    kv[x, y, :, HD:] = v_ref[...]
    pl.semaphore_wait(barrier, 22)

    comm = Comm(send_sem, recv_sem)

    def plane_place(buf, x_first, base, by_rows=True):
        def place(df, ds, start, count):
            if x_first:
                cx, cy = (x + df) % 4, (y + ds) % 4
            else:
                cx, cy = (x + ds) % 4, (y + df) % 4
            return buf.at[cx, cy, pl.ds(base + start, count)]

        return place

    run(
        gather_plane(comm, plane_place(kv, True, 0), 64, xe, ye),
        gather_plane(comm, plane_place(kv, False, 64), 64, ye, xe),
    )

    q_copy.wait()
    ow_copy.wait()
    query_pos = s * 128 + lax.broadcasted_iota(jnp.int32, (128, 2048), 0)
    key_pos = lax.broadcasted_iota(jnp.int32, (128, 2048), 1)
    allowed = query_pos >= key_pos
    key_rows = kv[:, :, :, 0:HD].reshape(2048, HD)
    value_rows = kv[:, :, :, HD:].reshape(2048, HD)
    for g in range(GROUP):
        scores = nt_dot(q_ref[:, g * HD : (g + 1) * HD], key_rows)
        scores = jnp.where(allowed, scores, -1e30)
        top = jnp.max(scores, axis=1, keepdims=True)
        terms = jnp.exp2((scores - top) * (LOG2E / math.sqrt(HD)))
        total = jnp.sum(terms, axis=1, keepdims=True)
        moved = mm(terms.astype(BF), value_rows)
        att[x, y, :, g * HD : (g + 1) * HD] = (moved / total).astype(BF)

    run(
        gather_plane(comm, plane_place(att, True, 0), 64, xe, ye),
        gather_plane(comm, plane_place(att, False, 64), 64, ye, xe),
    )

    w_copy.wait()
    for copy in res_copies:
        copy.wait()
    across = ({}, {})
    offsets = (2, 1, 3, 0)

    def branch(ch, zt, kk):
        rows = att[2 * ch + zt // 2, 2 * (zt % 2) + kk]
        return mm(rows, ow_ref[...])

    def section_sum(ch):
        crossing = []
        for off in offsets:
            zt = (z + off) % 4
            cs[ch, zt] = branch(ch, zt, o).astype(BF)
            crossing.append(comm.send(cs.at[ch, zt], cr.at[ch, zt], sib))
        yield
        for at, off in enumerate(offsets):
            zt = (z + off) % 4
            part = branch(ch, zt, k)
            crossing[at].wait_recv()
            part = part + cr[ch, zt].astype(F32)
            if off == 2:
                zs[ch, 0] = part.astype(BF)
                far = [
                    comm.send(zs.at[ch, 0, 64 * e : 64 * e + 64], zf.at[ch, e], ze[e])
                    for e in range(2)
                ]
            else:
                held[ch, SLOT[off]] = part
        yield
        near = []
        for e in range(2):
            far[e].wait_recv()
            rest = slice(64 - 64 * e, 128 - 64 * e)
            same = slice(64 * e, 64 * e + 64)
            slot = 1 if e == 0 else 2
            source = 1 if e == 0 else 3
            zs[ch, slot, rest] = sums(ch, source, rest).astype(BF)
            zs[ch, slot, same] = (sums(ch, source, same) + zf[ch, e].astype(F32)).astype(BF)
            near.append(comm.send(zs.at[ch, slot], zn.at[ch, e], ze[e]))
        yield
        part = sums(ch, 0, slice(0, 128)) + res[ch].astype(F32)
        for e in range(2):
            near[e].wait_recv()
            part = part + zn[ch, e].astype(F32)
        act[ch, z, k] = (part * gain_ref[...]).astype(BF)

        def pass_on(d, dev, start=0, count=128):
            block = act.at[ch, (z + d) % 4, k, pl.ds(start, count)]
            return comm.send(block, block, dev)

        up, down = pass_on(0, ze[0]), pass_on(0, ze[1])
        across[ch][0] = pass_on(0, sib)
        ssq_out[:, 128 * ch : 128 * ch + 128] = nt_dot(
            jnp.ones((8, 512), F32), part * part, precision=lax.Precision.HIGHEST
        )
        yield
        up.wait_recv()
        far_up = pass_on(-1, ze[0], 0, 64)
        across[ch][-1] = pass_on(-1, sib)
        down.wait_recv()
        far_down = pass_on(1, ze[1], 64, 64)
        across[ch][1] = pass_on(1, sib)
        yield
        far_up.wait_recv()
        far_down.wait_recv()
        across[ch][2] = pass_on(2, sib)
        yield

    def sums(ch, off, rows):
        return held[ch, SLOT[off], rows]

    squares = []
    inverses = []

    def share_squares():
        ssq_in[s] = ssq_out[...]
        for off in range(1, 16):
            squares.append(comm.send(ssq_out, ssq_in.at[s], {"seq": (s + off) % 16}))

    def share_inverse():
        for copy in squares:
            copy.wait_recv()
        total = ssq_in[0]
        for at in range(1, 16):
            total = total + ssq_in[at]
        inv[z, k] = lax.rsqrt(total / D + NORM_EPS)
        for dz in range(4):
            for flip in range(2):
                if dz or flip:
                    to = section_of((z + dz) % 4, (k + flip) % 2)
                    inverses.append(comm.send(inv.at[z, k], inv.at[z, k], to))

    def unit(pair, kk):
        ch = pair // 4
        u = 2 * pair + kk
        zt = pair % 4 if ch else (z + ORDER[pair]) % 4
        main, main_ends, side, side_ends = (x, xe, y, ye) if kk else (y, ye, x, xe)

        def product(p):
            rows = []
            for j in range(4):
                b = (p * 4 + j) if kk else (j * 4 + p)
                rows += [wv[0, b], wv[1, b]]
            return nt_dot(act[ch, zt, kk], jnp.concatenate(rows, axis=0))

        acc = product((main + 2) % 4)
        for j in range(4):
            s1[u, j] = acc[:, j * 128 : (j + 1) * 128].astype(BF)
        far = [
            comm.send(s1.at[u, 2 * e : 2 * e + 2], r1.at[u, 2 * e : 2 * e + 2], main_ends[e])
            for e in range(2)
        ]
        yield
        early, late = [], []
        for e, step in ((0, 1), (1, 3)):
            acc = product((main + step) % 4)
            for j in range(4):
                s2[u, e, j] = acc[:, j * 128 : (j + 1) * 128].astype(BF)
            span = pl.ds(2 - 2 * e, 2)
            early.append(comm.send(s2.at[u, e, span], r2.at[u, e, span], main_ends[e]))
        yield
        acc = product(main)
        for j in range(4):
            own[u, j] = acc[:, j * 128 : (j + 1) * 128]
        yield
        for e in range(2):
            far[e].wait_recv()
            span = pl.ds(2 * e, 2)
            s2[u, e, span] = (s2[u, e, span].astype(F32) + r1[u, span].astype(F32)).astype(BF)
            late.append(comm.send(s2.at[u, e, span], r2.at[u, e, span], main_ends[e]))
        yield
        for copy in (*early, *late):
            copy.wait_recv()

        def summed(j, rows=slice(0, 128)):
            return (
                own[u, j, rows] + r2[u, 0, j, rows].astype(F32) + r2[u, 1, j, rows].astype(F32)
            )

        t1[u] = summed((side + 2) % 4).astype(BF)
        last_far = [
            comm.send(t1.at[u, 64 * e : 64 * e + 64], u1.at[u, e], side_ends[e])
            for e in range(2)
        ]
        last = []
        for e in range(2):
            rest = slice(64 - 64 * e, 128 - 64 * e)
            t2[u, e, rest] = summed((side + 1 + 2 * e) % 4, rest).astype(BF)
            last.append(comm.send(t2.at[u, e, rest], u2.at[u, e, rest], side_ends[e]))
        yield
        for e in range(2):
            last_far[e].wait_recv()
            rest = slice(64 * e, 64 * e + 64)
            part = summed((side + 1 + 2 * e) % 4, rest) + u1[u, e].astype(F32)
            t2[u, e, rest] = part.astype(BF)
            last.append(comm.send(t2.at[u, e, rest], u2.at[u, e, rest], side_ends[e]))
        yield
        for copy in last:
            copy.wait_recv()
        part = summed(side) + u2[u, 0].astype(F32) + u2[u, 1].astype(F32)
        scale = jnp.transpose(inv[zt, kk, :, 128 * ch : 128 * ch + 128])[:, 0:1]
        at = pl.multiple_of(ch * 1024 + zt * 256 + kk * 128, 128)
        mixed[pl.ds(at, 128)] = part * scale
        yield

    lane = lax.broadcasted_iota(jnp.int32, (8, 128), 1)
    row = lax.broadcasted_iota(jnp.int32, (8, 128), 0)
    is_path = lane < 64
    low_row = lax.broadcasted_iota(jnp.int32, (1, 128), 1) < 64

    def twice(value):
        return jnp.concatenate([value, value], axis=1)

    taps = twice(cw_ref[...])
    bias = twice(cb_ref[...])

    def conv(ch):
        first, count = CHUNKS[ch]
        length = count // 8

        def strided(j):
            return mixed[pl.ds(first + j, 8, stride=length), :]

        def before(j):
            if first:
                return mixed[pl.ds(first - length + j, 8, stride=length), :]
            return jnp.where(row == 0, 0.0, pltpu.roll(strided(j), 1, 0))

        def step(j, carried):
            older, old, recent = carried
            now = strided(j)
            total = (
                bias + taps[0:1] * older + taps[1:2] * old + taps[2:3] * recent + taps[3:4] * now
            )
            value = jnp.where(is_path, total, now)
            at = pl.ds(pl.multiple_of(first + j * 8, 8), 8)
            uz[at, :] = value / (1.0 + jnp.exp(-value))
            return (old, recent, now)

        begin = tuple(before(length - 3 + i) for i in range(3))
        lax.fori_loop(0, length, step, begin, unroll=8)

    def sum_maps(ch):
        first, count = CHUNKS[ch]
        n = count // 8
        whole = pl.ds(0, n + 16)
        rank_weight = jnp.concatenate([pw_ref[:, 0:256], jnp.zeros((64, 256), BF)], axis=0)
        map_weight = jnp.transpose(pw_ref[:, 256:272].astype(F32))
        map_weight = jnp.concatenate([map_weight, jnp.zeros((16, 64), F32)], axis=1).astype(BF)

        def local_block(i):
            u = uz[pl.ds(pl.multiple_of(first + i * n, n), n), :].astype(BF)
            gs[ch, i, 0:n] = mm(u, rank_weight).astype(BF)
            if n < 128:
                u = jnp.concatenate([u, jnp.zeros((128 - n, 128), BF)], axis=0)
            maps = nt_dot(map_weight, u).astype(BF)
            gs[ch, i, n : n + 16] = jnp.concatenate([maps, jnp.zeros((16, 128), BF)], axis=1)

        crossing = {}
        for off in offsets:
            zt = (z + off) % 4
            local_block(2 * zt + o)
            crossing[off] = comm.send(gs.at[ch, 2 * zt + o, whole], gr.at[ch, zt, whole], sib)
        for off in offsets:
            local_block(2 * ((z + off) % 4) + k)
        yield
        moved = []
        for off in offsets:
            zt = (z + off) % 4
            crossing[off].wait_recv()
            part = gs[ch, 2 * zt + k, whole].astype(F32) + gr[ch, zt, whole].astype(F32)
            if off:
                gz[ch, zt, whole] = part.astype(BF)
                to = section_of(zt, k)
                moved.append(comm.send(gz.at[ch, zt, whole], gd.at[ch, z, whole], to))
            else:
                gd[ch, z, whole] = part.astype(BF)
        yield

        def total_of(parts):
            total = parts[0].astype(F32)
            for part in parts[1:]:
                total = total + part.astype(F32)
            return total.astype(BF)

        axes = ((x, lambda d: seq_of((x + d) % 4, y)), (y, lambda d: seq_of(x, (y + d) % 4)))

        def spread_out(h, step, value):
            mine, to = axes[h ^ step]
            gx[ch, h, step, mine, whole] = value
            block = gx.at[ch, h, step, mine, whole]
            return [comm.send(block, block, to(d)) for d in (2, 1, 3)]

        def gathered(h, step):
            return total_of([gx[ch, h, step, at, whole] for at in range(4)])

        for copy in moved:
            copy.wait_recv()
        value = total_of([gd[ch, at, whole] for at in range(4)])
        sent = [spread_out(h, 0, value[:, 128 * h : 128 * h + 128]) for h in range(2)]
        yield
        for h in range(2):
            for copy in sent[h]:
                copy.wait_recv()
            sent[h] = spread_out(h, 1, gathered(h, 0))
        yield
        for h in range(2):
            for copy in sent[h]:
                copy.wait_recv()
            gfull[ch, c, whole, 128 * h : 128 * h + 128] = gathered(h, 1)
        block = gfull.at[ch, c, whole]
        crossing = [comm.send(block, block, sib)]
        moved = [
            comm.send(block, block, section_of((z + off) % 4, k)) for off in (2, 1, 3)
        ]
        yield
        for at, off in ((1, 3), (2, 1), (0, 2)):
            moved[at].wait_recv()
            block = gfull.at[ch, 2 * ((z + off) % 4) + k, whole]
            crossing.append(comm.send(block, block, sib))
        yield
        for copy in crossing:
            copy.wait_recv()
        yield

    lane8 = lax.broadcasted_iota(jnp.int32, (16, 1024), 1)
    row8 = lax.broadcasted_iota(jnp.int32, (16, 1024), 0)
    which = 2 * ((lane8 // 128) % 4) + (lane8 % 128) // 64 + 8 * (lane8 // 512)
    spread = jnp.where(row8 == which, 1.0, 0.0).astype(BF)

    def decays():
        al = twice(al_ref[...])
        return [
            -jnp.exp(jnp.where(low_row, al[2 * q : 2 * q + 1], al[2 * q + 1 : 2 * q + 2])) * LOG2E
            for q in range(4)
        ]

    def prepare(ch):
        first, count = CHUNKS[ch]
        n = count // 8
        dtw = jnp.concatenate([dtw_ref[...], dtw_ref[...]], axis=0)
        dtb = twice(dtb_ref[...])
        low = lax.broadcasted_iota(jnp.int32, (n, 128), 1) < 64
        for i in range(8):
            rows = pl.ds(i * n, n)
            pre = nt_dot(gfull[ch, i, 0:n], dtw) + dtb
            st = jnp.maximum(pre, 0.0) + jnp.log1p(jnp.exp(-jnp.abs(pre)))
            step_size[rows] = st
            u = uz[pl.ds(first + i * n, n)].astype(BF).astype(F32)
            drive[rows] = st * jnp.where(low, u, pltpu.roll(u, 64, 1))
            maps = gfull[ch, i, n : n + 16, 0:128]
            wide[rows] = lax.dot_general(maps, spread, TN, preferred_element_type=F32)[0:n]

    nothing = jnp.zeros((8, 128), F32)

    def advance(j, states, decay):
        at = pl.ds(pl.multiple_of(j * 8, 8), 8)
        st = step_size[at]
        du = drive[at]
        return st, tuple(
            jnp.exp2(st * decay[q]) * states[q] + du * wide[at, q * 128 : (q + 1) * 128]
            for q in range(4)
        )

    def segment_ends(ch):
        decay = decays()

        def first_pass(j, carried):
            total, states = carried
            st, states = advance(j, states, decay)
            return (total + st, states)

        return lax.fori_loop(
            0, CHUNKS[ch][1] // 8, first_pass, (nothing, (nothing,) * 4), unroll=8
        )

    def entries(found, carry):
        total, ends = found
        decay = decays()
        starts, after = [], []
        for q in range(4):
            factor = jnp.exp2(total * decay[q])
            value = ends[q]
            for d in (1, 2, 4):
                moved_factor = jnp.where(row < d, 1.0, pltpu.roll(factor, d, 0))
                moved_value = jnp.where(row < d, 0.0, pltpu.roll(value, d, 0))
                value = factor * moved_value + value
                factor = factor * moved_factor
            if carry is not None:
                value = value + factor * carry[q]
            start = pltpu.roll(value, 1, 0)
            starts.append(jnp.where(row < 1, 0.0 if carry is None else carry[q], start))
            after.append(jnp.broadcast_to(value[7:8], (8, 128)))
        return starts, after

    def finish(ch, starts):
        first, count = CHUNKS[ch]
        length = count // 8
        decay = decays()
        skip = twice(skip_ref[...])

        def second_pass(j, states):
            _, states = advance(j, states, decay)
            at = pl.ds(pl.multiple_of(j * 8, 8), 8)
            gated = uz[pl.ds(pl.multiple_of(first + j * 8, 8), 8)]
            read = states[0] * wide[at, 512:640]
            for q in range(1, 4):
                read = read + states[q] * wide[at, 512 + q * 128 : 640 + q * 128]
            read = read + pltpu.roll(read, 64, 1)
            u = gated.astype(BF).astype(F32)
            ys[pl.ds(j, 8, stride=length), :] = (read + skip * u) * pltpu.roll(gated, 64, 1)
            return states

        lax.fori_loop(0, length, second_pass, tuple(starts), unroll=8)
        for at in range(0, count, 128):
            block = jnp.transpose(ys[at : at + 128, :])
            out_ref[:, first + at : first + at + 128] = block[0:64].astype(BF)

    pairs = {}

    def go(*steps):
        for step in steps:
            pair, count = step // 10, step % 10
            if pair not in pairs:
                pairs[pair] = (unit(pair, 0), unit(pair, 1))
            for _ in range(count):
                for stream in pairs[pair]:
                    next(stream)

    sec0, sec1 = section_sum(0), section_sum(1)
    for stream in (sec0, sec0, sec1, sec0, sec1, sec0, sec1):
        next(stream)
    across[0][0].wait_recv()
    go(2)
    next(sec0)
    next(sec1)
    share_squares()
    across[0][-1].wait_recv()
    go(11, 1, 12, 1)
    next(sec0)
    next(sec1)
    across[0][1].wait_recv()
    go(23, 11, 1)
    across[0][2].wait_recv()
    go(33, 21)
    next(sec1)
    go(11, 1)
    share_inverse()
    for copy in across[1].values():
        copy.wait_recv()
    go(43, 31, 21, 11)
    for copy in inverses:
        copy.wait_recv()
    go(53, 41, 31, 21, 1, 11)
    go(63, 51, 41, 31, 21)
    go(73, 61, 51, 41, 31)
    conv(0)
    maps0 = sum_maps(0)
    next(maps0)
    go(71, 61, 51, 41)
    next(maps0)
    go(71, 61, 51)
    conv(1)
    maps1 = sum_maps(1)
    next(maps1)
    next(maps0)
    go(71, 61)
    next(maps1)
    next(maps0)
    go(71)
    conv(2)
    maps2 = sum_maps(2)
    next(maps2)
    next(maps1)
    next(maps0)
    next(maps2)
    next(maps1)
    next(maps0)
    next(maps2)
    next(maps1)
    next(maps0)
    prepare(0)
    next(maps2)
    next(maps1)
    found = segment_ends(0)
    next(maps2)
    next(maps1)
    starts, carry = entries(found, None)
    finish(0, starts)
    next(maps2)
    prepare(1)
    found = segment_ends(1)
    starts, carry = entries(found, carry)
    finish(1, starts)
    next(maps2)
    prepare(2)
    starts, carry = entries(segment_ends(2), carry)
    finish(2, starts)
    comm.finish()


def body(
    queries, keys, values, residual, out_weight, norm_gain, in_weight, conv_weight, conv_bias,
    proj_weight, dt_weight, dt_bias, a_log, skip_gain,
):
    vmem = pl.BlockSpec(memory_space=pltpu.VMEM)
    anyspace = pl.BlockSpec(memory_space=pl.ANY)
    copies = 480
    return pl.pallas_call(
        front_kernel,
        out_shape=jax.ShapeDtypeStruct((64, 2048), BF),
        in_specs=[anyspace, vmem, vmem, anyspace, anyspace, vmem, anyspace] + [vmem] * 7,
        out_specs=vmem,
        scratch_shapes=[
            pltpu.VMEM((4, 4, 128, 256), BF),
            pltpu.VMEM((4, 4, 128, 512), BF),
            pltpu.VMEM((2, 4, 128, 512), BF),
            pltpu.VMEM((2, 4, 128, 512), BF),
            pltpu.VMEM((2, 3, 128, 512), F32),
            pltpu.VMEM((2, 3, 128, 512), BF),
            pltpu.VMEM((2, 2, 128, 512), BF),
            pltpu.VMEM((2, 2, 64, 512), BF),
            pltpu.VMEM((2, 4, 2, 128, 512), BF),
            pltpu.VMEM((8, 256), F32),
            pltpu.VMEM((16, 8, 256), F32),
            pltpu.VMEM((4, 2, 8, 256), F32),
            pltpu.VMEM((2, 128, 512), BF),
            pltpu.VMEM((2, 16, 64, 512), BF),
            pltpu.VMEM((16, 4, 128, 128), BF),
            pltpu.VMEM((16, 4, 128, 128), BF),
            pltpu.VMEM((16, 2, 4, 128, 128), BF),
            pltpu.VMEM((16, 2, 4, 128, 128), BF),
            pltpu.VMEM((16, 4, 128, 128), F32),
            pltpu.VMEM((16, 128, 128), BF),
            pltpu.VMEM((16, 2, 64, 128), BF),
            pltpu.VMEM((16, 2, 128, 128), BF),
            pltpu.VMEM((16, 2, 128, 128), BF),
            pltpu.VMEM((2048, 128), F32),
            pltpu.VMEM((2048, 128), F32),
            pltpu.VMEM((3, 8, 144, 256), BF),
            pltpu.VMEM((3, 4, 144, 256), BF),
            pltpu.VMEM((3, 4, 144, 256), BF),
            pltpu.VMEM((3, 4, 144, 256), BF),
            pltpu.VMEM((3, 2, 2, 4, 144, 128), BF),
            pltpu.VMEM((3, 8, 144, 256), BF),
            pltpu.VMEM((1024, 128), F32),
            pltpu.VMEM((1024, 1024), F32),
            pltpu.VMEM((1024, 128), F32),
            pltpu.VMEM((1024, 128), F32),
            pltpu.VMEM((128, 512), BF),
            pltpu.VMEM((512, 512), BF),
            pltpu.SemaphoreType.DMA((copies,)),
            pltpu.SemaphoreType.DMA((copies,)),
            pltpu.SemaphoreType.DMA((5,)),
        ],
        compiler_params=pltpu.CompilerParams(
            collective_id=0, has_side_effects=True, vmem_limit_bytes=60 * 1024 * 1024
        ),
        name="front",
    )(
        queries, keys, values, residual, out_weight, norm_gain[None, :],
        jnp.transpose(in_weight, (1, 2, 3, 0)), conv_weight.T, conv_bias[None, :], proj_weight,
        dt_weight.T, dt_bias[None, :], a_log.T, skip_gain[None, :],
    )


def solution(mesh):
    return jax.shard_map(
        body,
        mesh=mesh,
        in_specs=(
            P("seq", "section"),
            P("seq", "section"),
            P("seq", "section"),
            P(None, "seq"),
            P("section", "seq"),
            P("seq"),
            P("seq", None, None, "section"),
            P(("seq", "section"), None),
            P(("seq", "section")),
            P(("seq", "section"), None),
            P(None, ("seq", "section")),
            P(("seq", "section")),
            P(("seq", "section"), None),
            P(("seq", "section")),
        ),
        out_specs=P(("seq", "section"), None),
        check_vma=False,
    )
```

```python
import math

import jax
import jax.numpy as jnp
from jax import lax
from jax.experimental import pallas as pl
from jax.experimental.pallas import tpu as pltpu
from jax.sharding import PartitionSpec as P

D = 8192
HD = 128
GROUP = 4
NST = 8
DT_RANK = 256
CONV = 4
NORM_EPS = 1e-05
MESH = pl.DeviceIdType.MESH
BF = jnp.bfloat16
F32 = jnp.float32
CHUNKS = ((0, 1024), (1024, 512), (1536, 512))
ORDER = (0, -1, 1, 2)
SLOT = {0: 0, 1: 1, 3: 2}
LOG2E = math.log2(math.e)
NT = (((1,), (1,)), ((), ()))
TN = (((0,), (0,)), ((), ()))


def nt_dot(a, b, **kw):
    return lax.dot_general(a, b, NT, preferred_element_type=F32, **kw)


def mm(a, b):
    return jnp.dot(a, b, preferred_element_type=F32)


class Comm:
    def __init__(self, send_sem, recv_sem):
        self.send_sem = send_sem
        self.recv_sem = recv_sem
        self.copies = []

    def send(self, src, dst, dev):
        at = len(self.copies)
        copy = pltpu.make_async_remote_copy(
            src_ref=src,
            dst_ref=dst,
            send_sem=self.send_sem.at[at],
            recv_sem=self.recv_sem.at[at],
            device_id=dev,
            device_id_type=MESH,
        )
        copy.start()
        self.copies.append(copy)
        return copy

    def finish(self):
        assert len(self.copies) <= 480
        for copy in self.copies:
            copy.wait_send()


def run(*streams):
    live = list(streams)
    while live:
        for stream in list(live):
            try:
                next(stream)
            except StopIteration:
                live.remove(stream)


def gather_plane(comm, place, size, first, second):
    half = size // 2
    one = comm.send(place(0, 0, 0, size), place(0, 0, 0, size), first[0])
    two = comm.send(place(0, 0, 0, size), place(0, 0, 0, size), first[1])

    def along(df):
        block = place(df, 0, 0, size)
        return comm.send(block, block, second[0]), comm.send(block, block, second[1])

    sent = [(0, along(0))]
    yield
    one.wait_recv()
    block = place(-1, 0, 0, half)
    three = comm.send(block, block, first[0])
    two.wait_recv()
    block = place(1, 0, half, size - half)
    four = comm.send(block, block, first[1])
    sent.append((-1, along(-1)))
    sent.append((1, along(1)))
    yield
    three.wait_recv()
    four.wait_recv()
    sent.append((2, along(2)))
    yield
    last = []
    for df, (up, down) in sent:
        up.wait_recv()
        block = place(df, -1, 0, half)
        last.append(comm.send(block, block, second[0]))
        down.wait_recv()
        block = place(df, 1, half, size - half)
        last.append(comm.send(block, block, second[1]))
    yield
    for copy in last:
        copy.wait_recv()


def front_kernel(
    q_hbm, k_ref, v_ref, res_ref, ow_hbm, gain_ref, w_ref, cw_ref, cb_ref, pw_ref,
    dtw_ref, dtb_ref, al_ref, skip_ref,
    out_ref,
    kv, att, cs, cr, held, zs, zn, zf, act, ssq_out, ssq_in, inv, res, wv,
    s1, r1, s2, r2, own, t1, u1, t2, u2, t3, u3, mixed, uz,
    gs, gr, gz, gd, gx, gfull,
    step_size, wide, drive, ys,
    q_ref, ow_ref,
    send_sem, recv_sem, local_sem,
):
    s = lax.axis_index("seq")
    c = lax.axis_index("section")
    x, y = s // 4, s % 4
    z, k = c // 2, c % 2
    o = 1 - k

    def seq_of(cx, cy):
        return {"seq": cx * 4 + cy}

    def section_of(cz, ck):
        return {"section": cz * 2 + ck}

    xe = (seq_of((x + 1) % 4, y), seq_of((x + 3) % 4, y))
    ye = (seq_of(x, (y + 1) % 4), seq_of(x, (y + 3) % 4))
    ze = (section_of((z + 1) % 4, k), section_of((z + 3) % 4, k))
    sib = section_of(z, o)

    barrier = pltpu.get_barrier_semaphore()
    for off in range(1, 16):
        pl.semaphore_signal(
            barrier, inc=1, device_id={"seq": (s + off) % 16}, device_id_type=MESH
        )
    for off in range(1, 8):
        pl.semaphore_signal(
            barrier, inc=1, device_id={"section": (c + off) % 8}, device_id_type=MESH
        )
    res_copies = [
        pltpu.make_async_copy(
            res_ref.at[pl.ds(1024 * ch + 256 * z + 128 * k, 128)], res.at[ch], local_sem.at[ch]
        )
        for ch in range(2)
    ]
    for copy in res_copies:
        copy.start()
    q_copy = pltpu.make_async_copy(q_hbm, q_ref, local_sem.at[3])
    q_copy.start()
    ow_copy = pltpu.make_async_copy(ow_hbm, ow_ref, local_sem.at[4])
    ow_copy.start()
    w_copy = pltpu.make_async_copy(w_ref, wv, local_sem.at[2])
    w_copy.start()

    kv[x, y, :, 0:HD] = k_ref[...]
    kv[x, y, :, HD:] = v_ref[...]
    pl.semaphore_wait(barrier, 22)

    comm = Comm(send_sem, recv_sem)

    def plane_place(buf, x_first, base, by_rows=True):
        def place(df, ds, start, count):
            if x_first:
                cx, cy = (x + df) % 4, (y + ds) % 4
            else:
                cx, cy = (x + ds) % 4, (y + df) % 4
            return buf.at[cx, cy, pl.ds(base + start, count)]

        return place

    run(
        gather_plane(comm, plane_place(kv, True, 0), 64, xe, ye),
        gather_plane(comm, plane_place(kv, False, 64), 64, ye, xe),
    )

    q_copy.wait()
    ow_copy.wait()
    query_pos = s * 128 + lax.broadcasted_iota(jnp.int32, (128, 2048), 0)
    key_pos = lax.broadcasted_iota(jnp.int32, (128, 2048), 1)
    allowed = query_pos >= key_pos
    key_rows = kv[:, :, :, 0:HD].reshape(2048, HD)
    value_rows = kv[:, :, :, HD:].reshape(2048, HD)
    for g in range(GROUP):
        scores = nt_dot(q_ref[:, g * HD : (g + 1) * HD], key_rows)
        scores = jnp.where(allowed, scores, -1e30)
        top = jnp.max(scores, axis=1, keepdims=True)
        terms = jnp.exp2((scores - top) * (LOG2E / math.sqrt(HD)))
        total = jnp.sum(terms, axis=1, keepdims=True)
        moved = mm(terms.astype(BF), value_rows)
        att[x, y, :, g * HD : (g + 1) * HD] = (moved / total).astype(BF)

    run(
        gather_plane(comm, plane_place(att, True, 0), 64, xe, ye),
        gather_plane(comm, plane_place(att, False, 64), 64, ye, xe),
    )

    w_copy.wait()
    for copy in res_copies:
        copy.wait()
    across = ({}, {})
    offsets = (2, 1, 3, 0)

    def branch(ch, zt, kk):
        rows = att[2 * ch + zt // 2, 2 * (zt % 2) + kk]
        return mm(rows, ow_ref[...])

    def section_sum(ch):
        crossing = []
        for off in offsets:
            zt = (z + off) % 4
            cs[ch, zt] = branch(ch, zt, o).astype(BF)
            crossing.append(comm.send(cs.at[ch, zt], cr.at[ch, zt], sib))
        yield
        for at, off in enumerate(offsets):
            zt = (z + off) % 4
            part = branch(ch, zt, k)
            crossing[at].wait_recv()
            part = part + cr[ch, zt].astype(F32)
            if off == 2:
                zs[ch, 0] = part.astype(BF)
                far = [
                    comm.send(zs.at[ch, 0, 64 * e : 64 * e + 64], zf.at[ch, e], ze[e])
                    for e in range(2)
                ]
            else:
                held[ch, SLOT[off]] = part
        yield
        near = []
        for e in range(2):
            far[e].wait_recv()
            rest = slice(64 - 64 * e, 128 - 64 * e)
            same = slice(64 * e, 64 * e + 64)
            slot = 1 if e == 0 else 2
            source = 1 if e == 0 else 3
            zs[ch, slot, rest] = sums(ch, source, rest).astype(BF)
            zs[ch, slot, same] = (sums(ch, source, same) + zf[ch, e].astype(F32)).astype(BF)
            near.append(comm.send(zs.at[ch, slot], zn.at[ch, e], ze[e]))
        yield
        part = sums(ch, 0, slice(0, 128)) + res[ch].astype(F32)
        for e in range(2):
            near[e].wait_recv()
            part = part + zn[ch, e].astype(F32)
        act[ch, z, k] = (part * gain_ref[...]).astype(BF)

        def pass_on(d, dev, start=0, count=128):
            block = act.at[ch, (z + d) % 4, k, pl.ds(start, count)]
            return comm.send(block, block, dev)

        up, down = pass_on(0, ze[0]), pass_on(0, ze[1])
        across[ch][0] = pass_on(0, sib)
        ssq_out[:, 128 * ch : 128 * ch + 128] = nt_dot(
            jnp.ones((8, 512), F32), part * part, precision=lax.Precision.HIGHEST
        )
        yield
        up.wait_recv()
        far_up = pass_on(-1, ze[0], 0, 64)
        across[ch][-1] = pass_on(-1, sib)
        down.wait_recv()
        far_down = pass_on(1, ze[1], 64, 64)
        across[ch][1] = pass_on(1, sib)
        yield
        far_up.wait_recv()
        far_down.wait_recv()
        across[ch][2] = pass_on(2, sib)
        yield

    def sums(ch, off, rows):
        return held[ch, SLOT[off], rows]

    squares = []
    inverses = []

    def share_squares():
        ssq_in[s] = ssq_out[...]
        for off in range(1, 16):
            squares.append(comm.send(ssq_out, ssq_in.at[s], {"seq": (s + off) % 16}))

    def share_inverse():
        for copy in squares:
            copy.wait_recv()
        total = ssq_in[0]
        for at in range(1, 16):
            total = total + ssq_in[at]
        inv[z, k] = lax.rsqrt(total / D + NORM_EPS)
        for dz in range(4):
            for flip in range(2):
                if dz or flip:
                    to = section_of((z + dz) % 4, (k + flip) % 2)
                    inverses.append(comm.send(inv.at[z, k], inv.at[z, k], to))

    def unit(pair, kk):
        ch = pair // 4
        u = 2 * pair + kk
        zt = pair % 4 if ch else (z + ORDER[pair]) % 4
        main, main_ends, side, side_ends = (x, xe, y, ye) if kk else (y, ye, x, xe)

        def product(p):
            rows = []
            for j in range(4):
                b = (p * 4 + j) if kk else (j * 4 + p)
                rows += [wv[0, b], wv[1, b]]
            return nt_dot(act[ch, zt, kk], jnp.concatenate(rows, axis=0))

        def put_mixed(part):
            scale = jnp.transpose(inv[zt, kk, :, 128 * ch : 128 * ch + 128])[:, 0:1]
            at = pl.multiple_of(ch * 1024 + zt * 256 + kk * 128, 128)
            mixed[pl.ds(at, 128)] = part * scale

        acc = product((main + 2) % 4)
        for j in range(4):
            s1[u, j] = acc[:, j * 128 : (j + 1) * 128].astype(BF)
        far = [
            comm.send(s1.at[u, 2 * e : 2 * e + 2], r1.at[u, 2 * e : 2 * e + 2], main_ends[e])
            for e in range(2)
        ]
        yield
        early, late = [], []
        for e, step in ((0, 1), (1, 3)):
            acc = product((main + step) % 4)
            for j in range(4):
                s2[u, e, j] = acc[:, j * 128 : (j + 1) * 128].astype(BF)
            span = pl.ds(2 - 2 * e, 2)
            early.append(comm.send(s2.at[u, e, span], r2.at[u, e, span], main_ends[e]))
        yield
        acc = product(main)
        for j in range(4):
            own[u, j] = acc[:, j * 128 : (j + 1) * 128]
        yield
        for e in range(2):
            far[e].wait_recv()
            span = pl.ds(2 * e, 2)
            s2[u, e, span] = (s2[u, e, span].astype(F32) + r1[u, span].astype(F32)).astype(BF)
            late.append(comm.send(s2.at[u, e, span], r2.at[u, e, span], main_ends[e]))
        yield
        for copy in (*early, *late):
            copy.wait_recv()

        def summed(j, rows=slice(0, 128)):
            return (
                own[u, j, rows] + r2[u, 0, j, rows].astype(F32) + r2[u, 1, j, rows].astype(F32)
            )

        if pair >= 6:
            direct = []
            for d in (2, 1, 3):
                t3[u - 12, d - 1] = summed((side + d) % 4).astype(BF)
                to = seq_of(x, (y + d) % 4) if kk else seq_of((x + d) % 4, y)
                direct.append(comm.send(t3.at[u - 12, d - 1], u3.at[u - 12, d - 1], to))
            yield
            yield
            part = summed(side)
            for copy in direct:
                copy.wait_recv()
            for d in range(3):
                part = part + u3[u - 12, d].astype(F32)
            put_mixed(part)
            yield
            return
        t1[u] = summed((side + 2) % 4).astype(BF)
        last_far = [
            comm.send(t1.at[u, 64 * e : 64 * e + 64], u1.at[u, e], side_ends[e])
            for e in range(2)
        ]
        last = []
        for e in range(2):
            rest = slice(64 - 64 * e, 128 - 64 * e)
            t2[u, e, rest] = summed((side + 1 + 2 * e) % 4, rest).astype(BF)
            last.append(comm.send(t2.at[u, e, rest], u2.at[u, e, rest], side_ends[e]))
        yield
        for e in range(2):
            last_far[e].wait_recv()
            rest = slice(64 * e, 64 * e + 64)
            part = summed((side + 1 + 2 * e) % 4, rest) + u1[u, e].astype(F32)
            t2[u, e, rest] = part.astype(BF)
            last.append(comm.send(t2.at[u, e, rest], u2.at[u, e, rest], side_ends[e]))
        yield
        for copy in last:
            copy.wait_recv()
        part = summed(side) + u2[u, 0].astype(F32) + u2[u, 1].astype(F32)
        put_mixed(part)
        yield

    lane = lax.broadcasted_iota(jnp.int32, (8, 128), 1)
    row = lax.broadcasted_iota(jnp.int32, (8, 128), 0)
    is_path = lane < 64
    low_row = lax.broadcasted_iota(jnp.int32, (1, 128), 1) < 64

    def twice(value):
        return jnp.concatenate([value, value], axis=1)

    taps = twice(cw_ref[...])
    bias = twice(cb_ref[...])

    def conv(ch):
        first, count = CHUNKS[ch]
        length = count // 8

        def strided(j):
            return mixed[pl.ds(first + j, 8, stride=length), :]

        def before(j):
            if first:
                return mixed[pl.ds(first - length + j, 8, stride=length), :]
            return jnp.where(row == 0, 0.0, pltpu.roll(strided(j), 1, 0))

        def step(j, carried):
            older, old, recent = carried
            now = strided(j)
            total = (
                bias + taps[0:1] * older + taps[1:2] * old + taps[2:3] * recent + taps[3:4] * now
            )
            value = jnp.where(is_path, total, now)
            at = pl.ds(pl.multiple_of(first + j * 8, 8), 8)
            uz[at, :] = value / (1.0 + jnp.exp(-value))
            return (old, recent, now)

        begin = tuple(before(length - 3 + i) for i in range(3))
        lax.fori_loop(0, length, step, begin, unroll=8)

    def sum_maps(ch):
        first, count = CHUNKS[ch]
        n = count // 8
        whole = pl.ds(0, n + 16)
        rank_weight = jnp.concatenate([pw_ref[:, 0:256], jnp.zeros((64, 256), BF)], axis=0)
        map_weight = jnp.transpose(pw_ref[:, 256:272].astype(F32))
        map_weight = jnp.concatenate([map_weight, jnp.zeros((16, 64), F32)], axis=1).astype(BF)

        def local_block(i):
            u = uz[pl.ds(pl.multiple_of(first + i * n, n), n), :].astype(BF)
            gs[ch, i, 0:n] = mm(u, rank_weight).astype(BF)
            if n < 128:
                u = jnp.concatenate([u, jnp.zeros((128 - n, 128), BF)], axis=0)
            maps = nt_dot(map_weight, u).astype(BF)
            gs[ch, i, n : n + 16] = jnp.concatenate([maps, jnp.zeros((16, 128), BF)], axis=1)

        crossing = {}
        for off in offsets:
            zt = (z + off) % 4
            local_block(2 * zt + o)
            crossing[off] = comm.send(gs.at[ch, 2 * zt + o, whole], gr.at[ch, zt, whole], sib)
        for off in offsets:
            local_block(2 * ((z + off) % 4) + k)
        yield
        moved = []
        for off in offsets:
            zt = (z + off) % 4
            crossing[off].wait_recv()
            part = gs[ch, 2 * zt + k, whole].astype(F32) + gr[ch, zt, whole].astype(F32)
            if off:
                gz[ch, zt, whole] = part.astype(BF)
                to = section_of(zt, k)
                moved.append(comm.send(gz.at[ch, zt, whole], gd.at[ch, z, whole], to))
            else:
                gd[ch, z, whole] = part.astype(BF)
        yield

        def total_of(parts):
            total = parts[0].astype(F32)
            for part in parts[1:]:
                total = total + part.astype(F32)
            return total.astype(BF)

        axes = ((x, lambda d: seq_of((x + d) % 4, y)), (y, lambda d: seq_of(x, (y + d) % 4)))

        def spread_out(h, step, value):
            mine, to = axes[h ^ step]
            gx[ch, h, step, mine, whole] = value
            block = gx.at[ch, h, step, mine, whole]
            return [comm.send(block, block, to(d)) for d in (2, 1, 3)]

        def gathered(h, step):
            return total_of([gx[ch, h, step, at, whole] for at in range(4)])

        for copy in moved:
            copy.wait_recv()
        value = total_of([gd[ch, at, whole] for at in range(4)])
        sent = [spread_out(h, 0, value[:, 128 * h : 128 * h + 128]) for h in range(2)]
        yield
        for h in range(2):
            for copy in sent[h]:
                copy.wait_recv()
            sent[h] = spread_out(h, 1, gathered(h, 0))
        yield
        for h in range(2):
            for copy in sent[h]:
                copy.wait_recv()
            gfull[ch, c, whole, 128 * h : 128 * h + 128] = gathered(h, 1)
        block = gfull.at[ch, c, whole]
        crossing = [comm.send(block, block, sib)]
        moved = [
            comm.send(block, block, section_of((z + off) % 4, k)) for off in (2, 1, 3)
        ]
        yield
        for at, off in ((1, 3), (2, 1), (0, 2)):
            moved[at].wait_recv()
            block = gfull.at[ch, 2 * ((z + off) % 4) + k, whole]
            crossing.append(comm.send(block, block, sib))
        yield
        for copy in crossing:
            copy.wait_recv()
        yield

    lane8 = lax.broadcasted_iota(jnp.int32, (16, 1024), 1)
    row8 = lax.broadcasted_iota(jnp.int32, (16, 1024), 0)
    which = 2 * ((lane8 // 128) % 4) + (lane8 % 128) // 64 + 8 * (lane8 // 512)
    spread = jnp.where(row8 == which, 1.0, 0.0).astype(BF)

    def decays():
        al = twice(al_ref[...])
        return [
            -jnp.exp(jnp.where(low_row, al[2 * q : 2 * q + 1], al[2 * q + 1 : 2 * q + 2])) * LOG2E
            for q in range(4)
        ]

    def prepare(ch):
        first, count = CHUNKS[ch]
        n = count // 8
        dtw = jnp.concatenate([dtw_ref[...], dtw_ref[...]], axis=0)
        dtb = twice(dtb_ref[...])
        low = lax.broadcasted_iota(jnp.int32, (n, 128), 1) < 64
        for i in range(8):
            rows = pl.ds(i * n, n)
            pre = nt_dot(gfull[ch, i, 0:n], dtw) + dtb
            st = jnp.maximum(pre, 0.0) + jnp.log1p(jnp.exp(-jnp.abs(pre)))
            step_size[rows] = st
            u = uz[pl.ds(first + i * n, n)].astype(BF).astype(F32)
            drive[rows] = st * jnp.where(low, u, pltpu.roll(u, 64, 1))
            maps = gfull[ch, i, n : n + 16, 0:128]
            wide[rows] = lax.dot_general(maps, spread, TN, preferred_element_type=F32)[0:n]

    nothing = jnp.zeros((8, 128), F32)

    def advance(j, states, decay):
        at = pl.ds(pl.multiple_of(j * 8, 8), 8)
        st = step_size[at]
        du = drive[at]
        return st, tuple(
            jnp.exp2(st * decay[q]) * states[q] + du * wide[at, q * 128 : (q + 1) * 128]
            for q in range(4)
        )

    def segment_ends(ch):
        decay = decays()

        def first_pass(j, carried):
            total, states = carried
            st, states = advance(j, states, decay)
            return (total + st, states)

        return lax.fori_loop(
            0, CHUNKS[ch][1] // 8, first_pass, (nothing, (nothing,) * 4), unroll=8
        )

    def entries(found, carry):
        total, ends = found
        decay = decays()
        starts, after = [], []
        for q in range(4):
            factor = jnp.exp2(total * decay[q])
            value = ends[q]
            for d in (1, 2, 4):
                moved_factor = jnp.where(row < d, 1.0, pltpu.roll(factor, d, 0))
                moved_value = jnp.where(row < d, 0.0, pltpu.roll(value, d, 0))
                value = factor * moved_value + value
                factor = factor * moved_factor
            if carry is not None:
                value = value + factor * carry[q]
            start = pltpu.roll(value, 1, 0)
            starts.append(jnp.where(row < 1, 0.0 if carry is None else carry[q], start))
            after.append(jnp.broadcast_to(value[7:8], (8, 128)))
        return starts, after

    def finish(ch, starts):
        first, count = CHUNKS[ch]
        length = count // 8
        decay = decays()
        skip = twice(skip_ref[...])

        def second_pass(j, states):
            _, states = advance(j, states, decay)
            at = pl.ds(pl.multiple_of(j * 8, 8), 8)
            gated = uz[pl.ds(pl.multiple_of(first + j * 8, 8), 8)]
            read = states[0] * wide[at, 512:640]
            for q in range(1, 4):
                read = read + states[q] * wide[at, 512 + q * 128 : 640 + q * 128]
            read = read + pltpu.roll(read, 64, 1)
            u = gated.astype(BF).astype(F32)
            ys[pl.ds(j, 8, stride=length), :] = (read + skip * u) * pltpu.roll(gated, 64, 1)
            return states

        lax.fori_loop(0, length, second_pass, tuple(starts), unroll=8)
        for at in range(0, count, 128):
            block = jnp.transpose(ys[at : at + 128, :])
            out_ref[:, first + at : first + at + 128] = block[0:64].astype(BF)

    pairs = {}

    def go(*steps):
        for step in steps:
            pair, count = step // 10, step % 10
            if pair not in pairs:
                pairs[pair] = (unit(pair, 0), unit(pair, 1))
            for _ in range(count):
                for stream in pairs[pair]:
                    next(stream)

    sec0, sec1 = section_sum(0), section_sum(1)
    for stream in (sec0, sec1, sec0, sec1, sec0, sec1, sec0):
        next(stream)
    across[0][0].wait_recv()
    go(2)
    next(sec0)
    next(sec1)
    share_squares()
    across[0][-1].wait_recv()
    go(11, 1, 12, 1)
    next(sec0)
    next(sec1)
    across[0][1].wait_recv()
    go(23, 11, 1)
    across[0][2].wait_recv()
    go(33, 21)
    next(sec1)
    go(11, 1)
    share_inverse()
    for copy in across[1].values():
        copy.wait_recv()
    go(43, 31, 21, 11)
    for copy in inverses:
        copy.wait_recv()
    go(53, 41, 31, 21, 1, 11)
    go(63, 51, 41, 31, 21)
    go(73, 61, 51, 41, 31)
    conv(0)
    maps0 = sum_maps(0)
    next(maps0)
    go(71, 61, 51, 41)
    next(maps0)
    go(71, 61, 51)
    conv(1)
    maps1 = sum_maps(1)
    next(maps1)
    next(maps0)
    go(71, 61, 71)
    conv(2)
    maps2 = sum_maps(2)
    next(maps2)
    next(maps1)
    next(maps0)
    next(maps2)
    next(maps1)
    next(maps0)
    next(maps2)
    next(maps1)
    next(maps0)
    next(maps2)
    next(maps1)
    next(maps0)
    prepare(0)
    next(maps2)
    next(maps1)
    found = segment_ends(0)
    next(maps2)
    next(maps1)
    starts, carry = entries(found, None)
    finish(0, starts)
    prepare(1)
    found = segment_ends(1)
    starts, carry = entries(found, carry)
    finish(1, starts)
    next(maps2)
    prepare(2)
    starts, carry = entries(segment_ends(2), carry)
    finish(2, starts)
    comm.finish()


def body(
    queries, keys, values, residual, out_weight, norm_gain, in_weight, conv_weight, conv_bias,
    proj_weight, dt_weight, dt_bias, a_log, skip_gain,
):
    vmem = pl.BlockSpec(memory_space=pltpu.VMEM)
    anyspace = pl.BlockSpec(memory_space=pl.ANY)
    copies = 480
    return pl.pallas_call(
        front_kernel,
        out_shape=jax.ShapeDtypeStruct((64, 2048), BF),
        in_specs=[anyspace, vmem, vmem, anyspace, anyspace, vmem, anyspace] + [vmem] * 7,
        out_specs=vmem,
        scratch_shapes=[
            pltpu.VMEM((4, 4, 128, 256), BF),
            pltpu.VMEM((4, 4, 128, 512), BF),
            pltpu.VMEM((2, 4, 128, 512), BF),
            pltpu.VMEM((2, 4, 128, 512), BF),
            pltpu.VMEM((2, 3, 128, 512), F32),
            pltpu.VMEM((2, 3, 128, 512), BF),
            pltpu.VMEM((2, 2, 128, 512), BF),
            pltpu.VMEM((2, 2, 64, 512), BF),
            pltpu.VMEM((2, 4, 2, 128, 512), BF),
            pltpu.VMEM((8, 256), F32),
            pltpu.VMEM((16, 8, 256), F32),
            pltpu.VMEM((4, 2, 8, 256), F32),
            pltpu.VMEM((2, 128, 512), BF),
            pltpu.VMEM((2, 16, 64, 512), BF),
            pltpu.VMEM((16, 4, 128, 128), BF),
            pltpu.VMEM((16, 4, 128, 128), BF),
            pltpu.VMEM((16, 2, 4, 128, 128), BF),
            pltpu.VMEM((16, 2, 4, 128, 128), BF),
            pltpu.VMEM((16, 4, 128, 128), F32),
            pltpu.VMEM((16, 128, 128), BF),
            pltpu.VMEM((16, 2, 64, 128), BF),
            pltpu.VMEM((16, 2, 128, 128), BF),
            pltpu.VMEM((16, 2, 128, 128), BF),
            pltpu.VMEM((4, 3, 128, 128), BF),
            pltpu.VMEM((4, 3, 128, 128), BF),
            pltpu.VMEM((2048, 128), F32),
            pltpu.VMEM((2048, 128), F32),
            pltpu.VMEM((3, 8, 144, 256), BF),
            pltpu.VMEM((3, 4, 144, 256), BF),
            pltpu.VMEM((3, 4, 144, 256), BF),
            pltpu.VMEM((3, 4, 144, 256), BF),
            pltpu.VMEM((3, 2, 2, 4, 144, 128), BF),
            pltpu.VMEM((3, 8, 144, 256), BF),
            pltpu.VMEM((1024, 128), F32),
            pltpu.VMEM((1024, 1024), F32),
            pltpu.VMEM((1024, 128), F32),
            pltpu.VMEM((1024, 128), F32),
            pltpu.VMEM((128, 512), BF),
            pltpu.VMEM((512, 512), BF),
            pltpu.SemaphoreType.DMA((copies,)),
            pltpu.SemaphoreType.DMA((copies,)),
            pltpu.SemaphoreType.DMA((5,)),
        ],
        compiler_params=pltpu.CompilerParams(
            collective_id=0, has_side_effects=True, vmem_limit_bytes=60 * 1024 * 1024
        ),
        name="front",
    )(
        queries, keys, values, residual, out_weight, norm_gain[None, :],
        jnp.transpose(in_weight, (1, 2, 3, 0)), conv_weight.T, conv_bias[None, :], proj_weight,
        dt_weight.T, dt_bias[None, :], a_log.T, skip_gain[None, :],
    )


def solution(mesh):
    return jax.shard_map(
        body,
        mesh=mesh,
        in_specs=(
            P("seq", "section"),
            P("seq", "section"),
            P("seq", "section"),
            P(None, "seq"),
            P("section", "seq"),
            P("seq"),
            P("seq", None, None, "section"),
            P(("seq", "section"), None),
            P(("seq", "section")),
            P(("seq", "section"), None),
            P(None, ("seq", "section")),
            P(("seq", "section")),
            P(("seq", "section"), None),
            P(("seq", "section")),
        ),
        out_specs=P(("seq", "section"), None),
        check_vma=False,
    )
```

```python
import math

import jax
import jax.numpy as jnp
from jax import lax
from jax.experimental import pallas as pl
from jax.experimental.pallas import tpu as pltpu
from jax.sharding import PartitionSpec as P

D = 8192
HD = 128
GROUP = 4
NST = 8
DT_RANK = 256
CONV = 4
NORM_EPS = 1e-05
MESH = pl.DeviceIdType.MESH
BF = jnp.bfloat16
F32 = jnp.float32
CHUNKS = ((0, 1024), (1024, 512), (1536, 512))
ORDER = (0, -1, 1, 2)
SLOT = {0: 0, 1: 1, 3: 2}
LOG2E = math.log2(math.e)
NT = (((1,), (1,)), ((), ()))
TN = (((0,), (0,)), ((), ()))


def nt_dot(a, b, **kw):
    return lax.dot_general(a, b, NT, preferred_element_type=F32, **kw)


def mm(a, b):
    return jnp.dot(a, b, preferred_element_type=F32)


class Comm:
    def __init__(self, send_sem, recv_sem):
        self.send_sem = send_sem
        self.recv_sem = recv_sem
        self.copies = []

    def send(self, src, dst, dev):
        at = len(self.copies)
        copy = pltpu.make_async_remote_copy(
            src_ref=src,
            dst_ref=dst,
            send_sem=self.send_sem.at[at],
            recv_sem=self.recv_sem.at[at],
            device_id=dev,
            device_id_type=MESH,
        )
        copy.start()
        self.copies.append(copy)
        return copy

    def finish(self):
        assert len(self.copies) <= 480
        for copy in self.copies:
            copy.wait_send()


def run(*streams):
    live = list(streams)
    while live:
        for stream in list(live):
            try:
                next(stream)
            except StopIteration:
                live.remove(stream)


def gather_plane(comm, place, size, first, second):
    half = size // 2
    one = comm.send(place(0, 0, 0, size), place(0, 0, 0, size), first[0])
    two = comm.send(place(0, 0, 0, size), place(0, 0, 0, size), first[1])

    def along(df):
        block = place(df, 0, 0, size)
        return comm.send(block, block, second[0]), comm.send(block, block, second[1])

    yield
    sent = [(0, along(0))]
    yield
    one.wait_recv()
    block = place(-1, 0, 0, half)
    three = comm.send(block, block, first[0])
    two.wait_recv()
    block = place(1, 0, half, size - half)
    four = comm.send(block, block, first[1])
    yield
    sent.append((-1, along(-1)))
    sent.append((1, along(1)))
    yield
    three.wait_recv()
    four.wait_recv()
    sent.append((2, along(2)))
    yield
    last = []
    for df, (up, down) in sent:
        up.wait_recv()
        block = place(df, -1, 0, half)
        last.append(comm.send(block, block, second[0]))
        down.wait_recv()
        block = place(df, 1, half, size - half)
        last.append(comm.send(block, block, second[1]))
    yield
    for copy in last:
        copy.wait_recv()


def front_kernel(
    q_hbm, k_ref, v_ref, res_ref, ow_hbm, gain_ref, w_ref, cw_ref, cb_ref, pw_ref,
    dtw_ref, dtb_ref, al_ref, skip_ref,
    out_ref,
    kv, att, cs, cr, held, zs, zn, zf, act, ssq_out, ssq_in, inv, res, wv,
    s1, r1, s2, r2, own, t1, u1, t2, u2, t3, u3, mixed, uz,
    gs, gr, gz, gd, gx, gfull,
    step_size, wide, drive, ys,
    q_ref, ow_ref,
    send_sem, recv_sem, local_sem,
):
    s = lax.axis_index("seq")
    c = lax.axis_index("section")
    x, y = s // 4, s % 4
    z, k = c // 2, c % 2
    o = 1 - k

    def seq_of(cx, cy):
        return {"seq": cx * 4 + cy}

    def section_of(cz, ck):
        return {"section": cz * 2 + ck}

    xe = (seq_of((x + 1) % 4, y), seq_of((x + 3) % 4, y))
    ye = (seq_of(x, (y + 1) % 4), seq_of(x, (y + 3) % 4))
    ze = (section_of((z + 1) % 4, k), section_of((z + 3) % 4, k))
    sib = section_of(z, o)

    barrier = pltpu.get_barrier_semaphore()
    for off in range(1, 16):
        pl.semaphore_signal(
            barrier, inc=1, device_id={"seq": (s + off) % 16}, device_id_type=MESH
        )
    for off in range(1, 8):
        pl.semaphore_signal(
            barrier, inc=1, device_id={"section": (c + off) % 8}, device_id_type=MESH
        )
    res_copies = [
        pltpu.make_async_copy(
            res_ref.at[pl.ds(1024 * ch + 256 * z + 128 * k, 128)], res.at[ch], local_sem.at[ch]
        )
        for ch in range(2)
    ]
    for copy in res_copies:
        copy.start()
    q_copy = pltpu.make_async_copy(q_hbm, q_ref, local_sem.at[3])
    q_copy.start()
    ow_copy = pltpu.make_async_copy(ow_hbm, ow_ref, local_sem.at[4])
    ow_copy.start()
    w_copy = pltpu.make_async_copy(w_ref, wv, local_sem.at[2])
    w_copy.start()

    kv[x, y, :, 0:HD] = k_ref[...]
    kv[x, y, :, HD:] = v_ref[...]
    pl.semaphore_wait(barrier, 22)

    comm = Comm(send_sem, recv_sem)

    def plane_place(buf, x_first, base, by_rows=True):
        def place(df, ds, start, count):
            if x_first:
                cx, cy = (x + df) % 4, (y + ds) % 4
            else:
                cx, cy = (x + ds) % 4, (y + df) % 4
            return buf.at[cx, cy, pl.ds(base + start, count)]

        return place

    run(
        gather_plane(comm, plane_place(kv, True, 0), 64, xe, ye),
        gather_plane(comm, plane_place(kv, False, 64), 64, ye, xe),
    )

    q_copy.wait()
    ow_copy.wait()
    query_pos = s * 128 + lax.broadcasted_iota(jnp.int32, (128, 2048), 0)
    key_pos = lax.broadcasted_iota(jnp.int32, (128, 2048), 1)
    allowed = query_pos >= key_pos
    key_rows = kv[:, :, :, 0:HD].reshape(2048, HD)
    value_rows = kv[:, :, :, HD:].reshape(2048, HD)
    for g in range(GROUP):
        scores = nt_dot(q_ref[:, g * HD : (g + 1) * HD], key_rows)
        scores = jnp.where(allowed, scores, -1e30)
        top = jnp.max(scores, axis=1, keepdims=True)
        terms = jnp.exp2((scores - top) * (LOG2E / math.sqrt(HD)))
        total = jnp.sum(terms, axis=1, keepdims=True)
        moved = mm(terms.astype(BF), value_rows)
        att[x, y, :, g * HD : (g + 1) * HD] = (moved / total).astype(BF)

    run(
        gather_plane(comm, plane_place(att, True, 0), 64, xe, ye),
        gather_plane(comm, plane_place(att, False, 64), 64, ye, xe),
    )

    w_copy.wait()
    for copy in res_copies:
        copy.wait()
    across = ({}, {})
    offsets = (2, 1, 3, 0)

    def branch(ch, zt, kk):
        rows = att[2 * ch + zt // 2, 2 * (zt % 2) + kk]
        return mm(rows, ow_ref[...])

    def section_sum(ch):
        crossing = []
        for off in offsets:
            zt = (z + off) % 4
            cs[ch, zt] = branch(ch, zt, o).astype(BF)
            crossing.append(comm.send(cs.at[ch, zt], cr.at[ch, zt], sib))
        yield
        for at, off in enumerate(offsets):
            zt = (z + off) % 4
            part = branch(ch, zt, k)
            crossing[at].wait_recv()
            part = part + cr[ch, zt].astype(F32)
            if off == 2:
                zs[ch, 0] = part.astype(BF)
                far = [
                    comm.send(zs.at[ch, 0, 64 * e : 64 * e + 64], zf.at[ch, e], ze[e])
                    for e in range(2)
                ]
            else:
                held[ch, SLOT[off]] = part
        yield
        near = []
        for e in range(2):
            far[e].wait_recv()
            rest = slice(64 - 64 * e, 128 - 64 * e)
            same = slice(64 * e, 64 * e + 64)
            slot = 1 if e == 0 else 2
            source = 1 if e == 0 else 3
            zs[ch, slot, rest] = sums(ch, source, rest).astype(BF)
            zs[ch, slot, same] = (sums(ch, source, same) + zf[ch, e].astype(F32)).astype(BF)
            near.append(comm.send(zs.at[ch, slot], zn.at[ch, e], ze[e]))
        yield
        part = sums(ch, 0, slice(0, 128)) + res[ch].astype(F32)
        for e in range(2):
            near[e].wait_recv()
            part = part + zn[ch, e].astype(F32)
        act[ch, z, k] = (part * gain_ref[...]).astype(BF)

        def pass_on(d, dev, start=0, count=128):
            block = act.at[ch, (z + d) % 4, k, pl.ds(start, count)]
            return comm.send(block, block, dev)

        up, down = pass_on(0, ze[0]), pass_on(0, ze[1])
        across[ch][0] = pass_on(0, sib)
        ssq_out[:, 128 * ch : 128 * ch + 128] = nt_dot(
            jnp.ones((8, 512), F32), part * part, precision=lax.Precision.HIGHEST
        )
        yield
        up.wait_recv()
        far_up = pass_on(-1, ze[0], 0, 64)
        across[ch][-1] = pass_on(-1, sib)
        down.wait_recv()
        far_down = pass_on(1, ze[1], 64, 64)
        across[ch][1] = pass_on(1, sib)
        yield
        far_up.wait_recv()
        far_down.wait_recv()
        across[ch][2] = pass_on(2, sib)
        yield

    def sums(ch, off, rows):
        return held[ch, SLOT[off], rows]

    squares = []
    inverses = []

    def share_squares():
        ssq_in[s] = ssq_out[...]
        for off in range(1, 16):
            squares.append(comm.send(ssq_out, ssq_in.at[s], {"seq": (s + off) % 16}))

    def share_inverse():
        for copy in squares:
            copy.wait_recv()
        total = ssq_in[0]
        for at in range(1, 16):
            total = total + ssq_in[at]
        inv[z, k] = lax.rsqrt(total / D + NORM_EPS)
        for dz in range(4):
            for flip in range(2):
                if dz or flip:
                    to = section_of((z + dz) % 4, (k + flip) % 2)
                    inverses.append(comm.send(inv.at[z, k], inv.at[z, k], to))

    def unit(pair, kk):
        ch = pair // 4
        u = 2 * pair + kk
        zt = pair % 4 if ch else (z + ORDER[pair]) % 4
        main, main_ends, side, side_ends = (x, xe, y, ye) if kk else (y, ye, x, xe)

        def product(p):
            rows = []
            for j in range(4):
                b = (p * 4 + j) if kk else (j * 4 + p)
                rows += [wv[0, b], wv[1, b]]
            return nt_dot(act[ch, zt, kk], jnp.concatenate(rows, axis=0))

        def put_mixed(part):
            scale = jnp.transpose(inv[zt, kk, :, 128 * ch : 128 * ch + 128])[:, 0:1]
            at = pl.multiple_of(ch * 1024 + zt * 256 + kk * 128, 128)
            mixed[pl.ds(at, 128)] = part * scale

        acc = product((main + 2) % 4)
        for j in range(4):
            s1[u, j] = acc[:, j * 128 : (j + 1) * 128].astype(BF)
        far = [
            comm.send(s1.at[u, 2 * e : 2 * e + 2], r1.at[u, 2 * e : 2 * e + 2], main_ends[e])
            for e in range(2)
        ]
        yield
        early, late = [], []
        for e, step in ((0, 1), (1, 3)):
            acc = product((main + step) % 4)
            for j in range(4):
                s2[u, e, j] = acc[:, j * 128 : (j + 1) * 128].astype(BF)
            span = pl.ds(2 - 2 * e, 2)
            early.append(comm.send(s2.at[u, e, span], r2.at[u, e, span], main_ends[e]))
        yield
        acc = product(main)
        for j in range(4):
            own[u, j] = acc[:, j * 128 : (j + 1) * 128]
        yield
        for e in range(2):
            far[e].wait_recv()
            span = pl.ds(2 * e, 2)
            s2[u, e, span] = (s2[u, e, span].astype(F32) + r1[u, span].astype(F32)).astype(BF)
            late.append(comm.send(s2.at[u, e, span], r2.at[u, e, span], main_ends[e]))
        yield
        for copy in (*early, *late):
            copy.wait_recv()

        def summed(j, rows=slice(0, 128)):
            return (
                own[u, j, rows] + r2[u, 0, j, rows].astype(F32) + r2[u, 1, j, rows].astype(F32)
            )

        if pair >= 6:
            direct = []
            for d in (2, 1, 3):
                t3[u - 12, d - 1] = summed((side + d) % 4).astype(BF)
                to = seq_of(x, (y + d) % 4) if kk else seq_of((x + d) % 4, y)
                direct.append(comm.send(t3.at[u - 12, d - 1], u3.at[u - 12, d - 1], to))
            yield
            yield
            part = summed(side)
            for copy in direct:
                copy.wait_recv()
            for d in range(3):
                part = part + u3[u - 12, d].astype(F32)
            put_mixed(part)
            yield
            return
        t1[u] = summed((side + 2) % 4).astype(BF)
        last_far = [
            comm.send(t1.at[u, 64 * e : 64 * e + 64], u1.at[u, e], side_ends[e])
            for e in range(2)
        ]
        last = []
        for e in range(2):
            rest = slice(64 - 64 * e, 128 - 64 * e)
            t2[u, e, rest] = summed((side + 1 + 2 * e) % 4, rest).astype(BF)
            last.append(comm.send(t2.at[u, e, rest], u2.at[u, e, rest], side_ends[e]))
        yield
        for e in range(2):
            last_far[e].wait_recv()
            rest = slice(64 * e, 64 * e + 64)
            part = summed((side + 1 + 2 * e) % 4, rest) + u1[u, e].astype(F32)
            t2[u, e, rest] = part.astype(BF)
            last.append(comm.send(t2.at[u, e, rest], u2.at[u, e, rest], side_ends[e]))
        yield
        for copy in last:
            copy.wait_recv()
        part = summed(side) + u2[u, 0].astype(F32) + u2[u, 1].astype(F32)
        put_mixed(part)
        yield

    lane = lax.broadcasted_iota(jnp.int32, (8, 128), 1)
    row = lax.broadcasted_iota(jnp.int32, (8, 128), 0)
    is_path = lane < 64
    low_row = lax.broadcasted_iota(jnp.int32, (1, 128), 1) < 64

    def twice(value):
        return jnp.concatenate([value, value], axis=1)

    taps = twice(cw_ref[...])
    bias = twice(cb_ref[...])

    def conv(ch):
        first, count = CHUNKS[ch]
        length = count // 8

        def strided(j):
            return mixed[pl.ds(first + j, 8, stride=length), :]

        def before(j):
            if first:
                return mixed[pl.ds(first - length + j, 8, stride=length), :]
            return jnp.where(row == 0, 0.0, pltpu.roll(strided(j), 1, 0))

        def step(j, carried):
            older, old, recent = carried
            now = strided(j)
            total = (
                bias + taps[0:1] * older + taps[1:2] * old + taps[2:3] * recent + taps[3:4] * now
            )
            value = jnp.where(is_path, total, now)
            at = pl.ds(pl.multiple_of(first + j * 8, 8), 8)
            uz[at, :] = value / (1.0 + jnp.exp(-value))
            return (old, recent, now)

        begin = tuple(before(length - 3 + i) for i in range(3))
        lax.fori_loop(0, length, step, begin, unroll=8)

    def sum_maps(ch):
        first, count = CHUNKS[ch]
        n = count // 8
        whole = pl.ds(0, n + 16)
        rank_weight = jnp.concatenate([pw_ref[:, 0:256], jnp.zeros((64, 256), BF)], axis=0)
        map_weight = jnp.transpose(pw_ref[:, 256:272].astype(F32))
        map_weight = jnp.concatenate([map_weight, jnp.zeros((16, 64), F32)], axis=1).astype(BF)

        def local_block(i):
            u = uz[pl.ds(pl.multiple_of(first + i * n, n), n), :].astype(BF)
            gs[ch, i, 0:n] = mm(u, rank_weight).astype(BF)
            if n < 128:
                u = jnp.concatenate([u, jnp.zeros((128 - n, 128), BF)], axis=0)
            maps = nt_dot(map_weight, u).astype(BF)
            gs[ch, i, n : n + 16] = jnp.concatenate([maps, jnp.zeros((16, 128), BF)], axis=1)

        crossing = {}
        for off in offsets:
            zt = (z + off) % 4
            local_block(2 * zt + o)
            crossing[off] = comm.send(gs.at[ch, 2 * zt + o, whole], gr.at[ch, zt, whole], sib)
        for off in offsets:
            local_block(2 * ((z + off) % 4) + k)
        yield
        moved = []
        for off in offsets:
            zt = (z + off) % 4
            crossing[off].wait_recv()
            part = gs[ch, 2 * zt + k, whole].astype(F32) + gr[ch, zt, whole].astype(F32)
            if off:
                gz[ch, zt, whole] = part.astype(BF)
                to = section_of(zt, k)
                moved.append(comm.send(gz.at[ch, zt, whole], gd.at[ch, z, whole], to))
            else:
                gd[ch, z, whole] = part.astype(BF)
        yield

        def total_of(parts):
            total = parts[0].astype(F32)
            for part in parts[1:]:
                total = total + part.astype(F32)
            return total.astype(BF)

        axes = ((x, lambda d: seq_of((x + d) % 4, y)), (y, lambda d: seq_of(x, (y + d) % 4)))

        def spread_out(h, step, value):
            mine, to = axes[h ^ step]
            gx[ch, h, step, mine, whole] = value
            block = gx.at[ch, h, step, mine, whole]
            return [comm.send(block, block, to(d)) for d in (2, 1, 3)]

        def gathered(h, step):
            return total_of([gx[ch, h, step, at, whole] for at in range(4)])

        for copy in moved:
            copy.wait_recv()
        value = total_of([gd[ch, at, whole] for at in range(4)])
        sent = [spread_out(h, 0, value[:, 128 * h : 128 * h + 128]) for h in range(2)]
        yield
        for h in range(2):
            for copy in sent[h]:
                copy.wait_recv()
            sent[h] = spread_out(h, 1, gathered(h, 0))
        yield
        for h in range(2):
            for copy in sent[h]:
                copy.wait_recv()
            gfull[ch, c, whole, 128 * h : 128 * h + 128] = gathered(h, 1)
        block = gfull.at[ch, c, whole]
        crossing = [comm.send(block, block, sib)]
        moved = [
            comm.send(block, block, section_of((z + off) % 4, k)) for off in (2, 1, 3)
        ]
        yield
        for at, off in ((1, 3), (2, 1), (0, 2)):
            moved[at].wait_recv()
            block = gfull.at[ch, 2 * ((z + off) % 4) + k, whole]
            crossing.append(comm.send(block, block, sib))
        yield
        for copy in crossing:
            copy.wait_recv()
        yield

    lane8 = lax.broadcasted_iota(jnp.int32, (16, 1024), 1)
    row8 = lax.broadcasted_iota(jnp.int32, (16, 1024), 0)
    which = 2 * ((lane8 // 128) % 4) + (lane8 % 128) // 64 + 8 * (lane8 // 512)
    spread = jnp.where(row8 == which, 1.0, 0.0).astype(BF)

    def decays():
        al = twice(al_ref[...])
        return [
            -jnp.exp(jnp.where(low_row, al[2 * q : 2 * q + 1], al[2 * q + 1 : 2 * q + 2])) * LOG2E
            for q in range(4)
        ]

    def prepare(ch):
        first, count = CHUNKS[ch]
        n = count // 8
        dtw = jnp.concatenate([dtw_ref[...], dtw_ref[...]], axis=0)
        dtb = twice(dtb_ref[...])
        low = lax.broadcasted_iota(jnp.int32, (n, 128), 1) < 64
        for i in range(8):
            rows = pl.ds(i * n, n)
            pre = nt_dot(gfull[ch, i, 0:n], dtw) + dtb
            st = jnp.maximum(pre, 0.0) + jnp.log1p(jnp.exp(-jnp.abs(pre)))
            step_size[rows] = st
            u = uz[pl.ds(first + i * n, n)].astype(BF).astype(F32)
            drive[rows] = st * jnp.where(low, u, pltpu.roll(u, 64, 1))
            maps = gfull[ch, i, n : n + 16, 0:128]
            wide[rows] = lax.dot_general(maps, spread, TN, preferred_element_type=F32)[0:n]

    nothing = jnp.zeros((8, 128), F32)

    def advance(j, states, decay):
        at = pl.ds(pl.multiple_of(j * 8, 8), 8)
        st = step_size[at]
        du = drive[at]
        return st, tuple(
            jnp.exp2(st * decay[q]) * states[q] + du * wide[at, q * 128 : (q + 1) * 128]
            for q in range(4)
        )

    def segment_ends(ch):
        decay = decays()

        def first_pass(j, carried):
            total, states = carried
            st, states = advance(j, states, decay)
            return (total + st, states)

        return lax.fori_loop(
            0, CHUNKS[ch][1] // 8, first_pass, (nothing, (nothing,) * 4), unroll=8
        )

    def entries(found, carry):
        total, ends = found
        decay = decays()
        starts, after = [], []
        for q in range(4):
            factor = jnp.exp2(total * decay[q])
            value = ends[q]
            for d in (1, 2, 4):
                moved_factor = jnp.where(row < d, 1.0, pltpu.roll(factor, d, 0))
                moved_value = jnp.where(row < d, 0.0, pltpu.roll(value, d, 0))
                value = factor * moved_value + value
                factor = factor * moved_factor
            if carry is not None:
                value = value + factor * carry[q]
            start = pltpu.roll(value, 1, 0)
            starts.append(jnp.where(row < 1, 0.0 if carry is None else carry[q], start))
            after.append(jnp.broadcast_to(value[7:8], (8, 128)))
        return starts, after

    def finish(ch, starts):
        first, count = CHUNKS[ch]
        length = count // 8
        decay = decays()
        skip = twice(skip_ref[...])

        def second_pass(j, states):
            _, states = advance(j, states, decay)
            at = pl.ds(pl.multiple_of(j * 8, 8), 8)
            gated = uz[pl.ds(pl.multiple_of(first + j * 8, 8), 8)]
            read = states[0] * wide[at, 512:640]
            for q in range(1, 4):
                read = read + states[q] * wide[at, 512 + q * 128 : 640 + q * 128]
            read = read + pltpu.roll(read, 64, 1)
            u = gated.astype(BF).astype(F32)
            ys[pl.ds(j, 8, stride=length), :] = (read + skip * u) * pltpu.roll(gated, 64, 1)
            return states

        lax.fori_loop(0, length, second_pass, tuple(starts), unroll=8)
        for at in range(0, count, 128):
            block = jnp.transpose(ys[at : at + 128, :])
            out_ref[:, first + at : first + at + 128] = block[0:64].astype(BF)

    pairs = {}

    def go(*steps):
        for step in steps:
            pair, count = step // 10, step % 10
            if pair not in pairs:
                pairs[pair] = (unit(pair, 0), unit(pair, 1))
            for _ in range(count):
                for stream in pairs[pair]:
                    next(stream)

    sec0, sec1 = section_sum(0), section_sum(1)
    for stream in (sec0, sec1, sec0, sec1, sec0, sec1, sec0):
        next(stream)
    across[0][0].wait_recv()
    go(2)
    next(sec0)
    next(sec1)
    share_squares()
    across[0][-1].wait_recv()
    go(11, 1, 12, 1)
    next(sec0)
    next(sec1)
    across[0][1].wait_recv()
    go(23, 11, 1)
    across[0][2].wait_recv()
    go(33, 21)
    next(sec1)
    go(11, 1)
    share_inverse()
    for copy in across[1].values():
        copy.wait_recv()
    go(43, 31, 21, 11)
    for copy in inverses:
        copy.wait_recv()
    go(53, 41, 31, 21, 1, 11)
    go(63, 51, 41, 31, 21)
    go(73, 61, 51, 41, 31)
    conv(0)
    maps0 = sum_maps(0)
    next(maps0)
    go(71, 61, 51, 41)
    next(maps0)
    go(71, 61, 51)
    conv(1)
    maps1 = sum_maps(1)
    next(maps1)
    next(maps0)
    go(71, 61, 71)
    conv(2)
    maps2 = sum_maps(2)
    next(maps2)
    next(maps1)
    next(maps0)
    next(maps2)
    next(maps1)
    next(maps0)
    next(maps2)
    next(maps1)
    next(maps0)
    next(maps2)
    next(maps1)
    next(maps0)
    prepare(0)
    next(maps2)
    next(maps1)
    found = segment_ends(0)
    next(maps2)
    next(maps1)
    starts, carry = entries(found, None)
    finish(0, starts)
    prepare(1)
    found = segment_ends(1)
    starts, carry = entries(found, carry)
    finish(1, starts)
    next(maps2)
    prepare(2)
    starts, carry = entries(segment_ends(2), carry)
    finish(2, starts)
    comm.finish()


def body(
    queries, keys, values, residual, out_weight, norm_gain, in_weight, conv_weight, conv_bias,
    proj_weight, dt_weight, dt_bias, a_log, skip_gain,
):
    vmem = pl.BlockSpec(memory_space=pltpu.VMEM)
    anyspace = pl.BlockSpec(memory_space=pl.ANY)
    copies = 480
    return pl.pallas_call(
        front_kernel,
        out_shape=jax.ShapeDtypeStruct((64, 2048), BF),
        in_specs=[anyspace, vmem, vmem, anyspace, anyspace, vmem, anyspace] + [vmem] * 7,
        out_specs=vmem,
        scratch_shapes=[
            pltpu.VMEM((4, 4, 128, 256), BF),
            pltpu.VMEM((4, 4, 128, 512), BF),
            pltpu.VMEM((2, 4, 128, 512), BF),
            pltpu.VMEM((2, 4, 128, 512), BF),
            pltpu.VMEM((2, 3, 128, 512), F32),
            pltpu.VMEM((2, 3, 128, 512), BF),
            pltpu.VMEM((2, 2, 128, 512), BF),
            pltpu.VMEM((2, 2, 64, 512), BF),
            pltpu.VMEM((2, 4, 2, 128, 512), BF),
            pltpu.VMEM((8, 256), F32),
            pltpu.VMEM((16, 8, 256), F32),
            pltpu.VMEM((4, 2, 8, 256), F32),
            pltpu.VMEM((2, 128, 512), BF),
            pltpu.VMEM((2, 16, 64, 512), BF),
            pltpu.VMEM((16, 4, 128, 128), BF),
            pltpu.VMEM((16, 4, 128, 128), BF),
            pltpu.VMEM((16, 2, 4, 128, 128), BF),
            pltpu.VMEM((16, 2, 4, 128, 128), BF),
            pltpu.VMEM((16, 4, 128, 128), F32),
            pltpu.VMEM((16, 128, 128), BF),
            pltpu.VMEM((16, 2, 64, 128), BF),
            pltpu.VMEM((16, 2, 128, 128), BF),
            pltpu.VMEM((16, 2, 128, 128), BF),
            pltpu.VMEM((4, 3, 128, 128), BF),
            pltpu.VMEM((4, 3, 128, 128), BF),
            pltpu.VMEM((2048, 128), F32),
            pltpu.VMEM((2048, 128), F32),
            pltpu.VMEM((3, 8, 144, 256), BF),
            pltpu.VMEM((3, 4, 144, 256), BF),
            pltpu.VMEM((3, 4, 144, 256), BF),
            pltpu.VMEM((3, 4, 144, 256), BF),
            pltpu.VMEM((3, 2, 2, 4, 144, 128), BF),
            pltpu.VMEM((3, 8, 144, 256), BF),
            pltpu.VMEM((1024, 128), F32),
            pltpu.VMEM((1024, 1024), F32),
            pltpu.VMEM((1024, 128), F32),
            pltpu.VMEM((1024, 128), F32),
            pltpu.VMEM((128, 512), BF),
            pltpu.VMEM((512, 512), BF),
            pltpu.SemaphoreType.DMA((copies,)),
            pltpu.SemaphoreType.DMA((copies,)),
            pltpu.SemaphoreType.DMA((5,)),
        ],
        compiler_params=pltpu.CompilerParams(
            collective_id=0, has_side_effects=True, vmem_limit_bytes=60 * 1024 * 1024
        ),
        name="front",
    )(
        queries, keys, values, residual, out_weight, norm_gain[None, :],
        jnp.transpose(in_weight, (1, 2, 3, 0)), conv_weight.T, conv_bias[None, :], proj_weight,
        dt_weight.T, dt_bias[None, :], a_log.T, skip_gain[None, :],
    )


def solution(mesh):
    return jax.shard_map(
        body,
        mesh=mesh,
        in_specs=(
            P("seq", "section"),
            P("seq", "section"),
            P("seq", "section"),
            P(None, "seq"),
            P("section", "seq"),
            P("seq"),
            P("seq", None, None, "section"),
            P(("seq", "section"), None),
            P(("seq", "section")),
            P(("seq", "section"), None),
            P(None, ("seq", "section")),
            P(("seq", "section")),
            P(("seq", "section"), None),
            P(("seq", "section")),
        ),
        out_specs=P(("seq", "section"), None),
        check_vma=False,
    )
```
